32 devices in a mesh: dp: 4 (over x, core), gx: 2 (over y), gy: 4 (over z).
Axes of the slice: x: 2, y: 2, z: 4, core: 2. Of those that a mesh axis runs over, the one named last changes fastest.
Arguments:
- inputs: bfloat16 [4096, 960], P(('dp', 'gx', 'gy')), may hold values from -6 to 6
- segments: int32 [4096], P('dp'), may hold values from 0 to 15, never falling along the last dimension, each value on 1 to 512 neighbouring positions
- attn_gain: float32 [960], replicated, may hold values from 0.5 to 1.5
- query_weight: bfloat16 [960, 960], P('gx', 'gy'), may hold values from -1.6 to 1.6
- key_weight: bfloat16 [960, 320], P('gx', 'gy'), may hold values from -1.6 to 1.6
- value_weight: bfloat16 [960, 320], P('gx', 'gy'), may hold values from -0.1875 to 0.1875
- output_weight: bfloat16 [960, 960], P('gx', 'gy'), may hold values from -0.75 to 0.75
- mlp_gain: float32 [960], replicated, may hold values from 0.5 to 1.5
- gate_weight: bfloat16 [960, 2560], P('gx', 'gy'), may hold values from -0.1875 to 0.1875
- up_weight: bfloat16 [960, 2560], P('gx', 'gy'), may hold values from -0.1875 to 0.1875
- down_weight: bfloat16 [2560, 960], P('gx', 'gy'), may hold values from -0.125 to 0.125
- cotangent: bfloat16 [4096, 960], P(('dp', 'gx', 'gy')), may hold values from -6 to 6
Outputs:
- layer_out: bfloat16 [4096, 960], P(('dp', 'gx', 'gy'))
- input_grad: bfloat16 [4096, 960], P(('dp', 'gx', 'gy'))
- query_grad: float32 [960, 960], P('gx', 'gy')
- key_grad: float32 [960, 320], P('gx', 'gy')
- value_grad: float32 [960, 320], P('gx', 'gy')
- output_grad: float32 [960, 960], P('gx', 'gy')
- gate_grad: float32 [960, 2560], P('gx', 'gy')
- up_grad: float32 [960, 2560], P('gx', 'gy')
- down_grad: float32 [2560, 960], P('gx', 'gy')
- attgain_grad: float32 [960], replicated
- mlpgain_grad: float32 [960], replicated
The draws below stay inside these ranges and needn't reach their ends.
Inputs may be any that keep to these rules, and one draw needn't show every extreme that they name: `segments`: segment numbers never fall along the tokens; a document may run on past the end of a sequence.
All inputs are finite; a program needn't handle non-finite values.
Results may differ from the reference program's by a relative error of at most 0.04.
Values may be sent and summed in bfloat16 or wider, within the bound.
A program may use at most 128 MiB of HBM per device.

```python
import math
import jax
import jax.numpy as jnp
import numpy as np
from jax import lax

D = 960
QUERY_HEADS = 15
KEY_VALUE_HEADS = 5
HEAD_WIDTH = 64
FF = 2560
SEQUENCE_LENGTH = 1024
QW = 960
KVW = 320
TOKENS = 4096


def weight_draw(seed_key, fan_in, columns):
    normal_part = jax.random.truncated_normal(seed_key, -4.0, 4.0, (fan_in, columns), jnp.float32) * (1.0 / math.sqrt(fan_in))
    return normal_part.astype(jnp.bfloat16)


def draw_query_weight(key, part):
    return weight_draw(jax.random.fold_in(key, 3), D, QW)


def draw_key_weight(key, part):
    return weight_draw(jax.random.fold_in(key, 5), D, KVW)


def level_of(own_key, shape, split, low, largest):
    level = 1.0
    for dim, parts in split:
        draws = jax.random.uniform(jax.random.fold_in(jax.random.fold_in(own_key, 6), dim), (parts,), jnp.float32, low / len(split), largest / len(split))
        level = level * jnp.repeat(jnp.exp(draws), shape[dim] // parts).reshape((-1,) + (1,) * (len(shape) - 1 - dim))
    return level


def split_up(number_of, total, limit, slope):
    loads = [(1 << 20) // math.isqrt(grade ** slope) + 1 for grade in range(2, number_of + 1)]
    rest, given = total - limit - (number_of - 1), [1] * (number_of - 1)
    while rest > 0:
        candidates = [i for i in range(number_of - 1) if given[i] < limit]
        pool, remaining = sum([loads[i] for i in candidates]), rest
        for i in candidates:
            addition = min(limit - given[i], max(1, remaining * loads[i] // pool), rest)
            given[i] = given[i] + addition
            rest = rest - addition
    return np.array([limit] + given)


def uneven_parts(rng, count, total, bound, skew):
    if count == 2:
        one = jax.random.randint(rng, (), max(1, total - bound), min(bound, total - 1) + 1)
        return jnp.stack([one, total - one])
    sizes = jnp.asarray(split_up(count, total, bound, skew), jnp.int32)
    twos = (count - 1) // 2
    donor, receiver = sizes[1:1 + 2 * twos:2], sizes[2:2 + 2 * twos:2]
    room = jnp.minimum(donor - 1, bound - receiver)
    moved = jax.random.randint(jax.random.fold_in(rng, 1), (twos,), 0, 1 << 20) % (room + 1)
    sizes = sizes.at[1:1 + 2 * twos:2].set(donor - moved).at[2:2 + 2 * twos:2].set(receiver + moved)
    return sizes[jax.random.permutation(jax.random.fold_in(rng, 2), count)]


def normal_values(key, extent, spread, limit, split=(), kind=jnp.bfloat16):
    loudness = level_of(key, extent, split, -0.22, 0.18) if split else 1.0
    result = jax.random.normal(key, extent, jnp.float32) * spread * loudness
    return jnp.minimum(jnp.maximum(result, -limit), limit).astype(kind)


def setup_inputs(seed: int = 0) -> dict:
    seeds = jax.random.split(jax.random.key(seed), 13)
    return {
        "inputs": normal_values(seeds[0], (TOKENS, D), 1.0, 6.0, ((0, 32),)),
        "segments": jnp.searchsorted(jnp.cumsum(uneven_parts(seeds[1], TOKENS // (SEQUENCE_LENGTH // 4), TOKENS, SEQUENCE_LENGTH // 2, 0)), jnp.arange(TOKENS), side="right").astype(jnp.int32),
        "attn_gain": jnp.clip(1.0 + 0.1 * jax.random.normal(seeds[2], (D,), jnp.float32), 0.5, 1.5),
        "query_weight": draw_query_weight(jax.random.fold_in(seeds[12], 71), 0),
        "key_weight": draw_key_weight(jax.random.fold_in(seeds[12], 71), 0),
        "value_weight": normal_values(seeds[5], (D, KVW), D ** -0.5, 0.1875, ((0, 2), (1, 4))),
        "output_weight": normal_values(seeds[6], (QW, D), (QW // 16) ** -0.5, 0.75, ((0, 2), (1, 4))),
        "mlp_gain": jnp.clip(1.0 + 0.1 * jax.random.normal(seeds[7], (D,), jnp.float32), 0.5, 1.5),
        "gate_weight": normal_values(seeds[8], (D, FF), D ** -0.5, 0.1875, ((0, 2), (1, 4))),
        "up_weight": normal_values(seeds[9], (D, FF), D ** -0.5, 0.1875, ((0, 2), (1, 4))),
        "down_weight": normal_values(seeds[10], (FF, D), FF ** -0.5, 0.125, ((0, 2), (1, 4))),
        "cotangent": normal_values(seeds[11], (TOKENS, D), 1.0, 6.0, ((0, 32),)),
    }


THETA = 100000.0
EPSILON = 1e-05
MASKED = -1e+30

def rope_angles(positions):
    half_dim = HEAD_WIDTH // 2
    inverse = THETA ** (-(jnp.arange(half_dim, dtype=jnp.float32) * 2.0 / HEAD_WIDTH))
    angles = positions[:, None] * inverse[None, :]
    return (jnp.cos(angles)[:, None, :], jnp.sin(angles)[:, None, :])

def rotate(values, cos_table, sin_table):
    item_count = values.shape[0]
    shaped = values.reshape(item_count, -1, HEAD_WIDTH)
    half_dim = HEAD_WIDTH // 2
    front_part = shaped[:, :, :half_dim]
    back_part = shaped[:, :, half_dim:]
    turned = jnp.concatenate([front_part * cos_table - back_part * sin_table, back_part * cos_table + front_part * sin_table], axis=2)
    return turned.reshape(item_count, -1)

def unrotate(values, cos_table, sin_table):
    item_count = values.shape[0]
    shaped = values.reshape(item_count, -1, HEAD_WIDTH)
    half_dim = HEAD_WIDTH // 2
    front_part = shaped[:, :, :half_dim]
    back_part = shaped[:, :, half_dim:]
    turned = jnp.concatenate([front_part * cos_table + back_part * sin_table, back_part * cos_table - front_part * sin_table], axis=2)
    return turned.reshape(item_count, -1)

def normalize(values, gain):
    rms_rows = lax.rsqrt(lax.optimization_barrier(jnp.mean(values * values, axis=1, keepdims=True)) + EPSILON)
    unit_rows = values * rms_rows
    return (rms_rows, unit_rows, (unit_rows * gain).astype(jnp.bfloat16))

def normalize_back(dnormed, gain, rms_rows, unit_rows):
    scaled = dnormed * gain
    dvalues = rms_rows * (scaled - unit_rows * lax.optimization_barrier(jnp.mean(scaled * unit_rows, axis=1, keepdims=True)))
    return (dvalues, lax.optimization_barrier(jnp.sum(dnormed * unit_rows, axis=0)))

def matmul(left, right):
    return jnp.dot(left, right, preferred_element_type=jnp.float32)

def head_views(rotated_query, rotated_key, value_row_list):
    query_groups = QUERY_HEADS // KEY_VALUE_HEADS
    query_head_split = rotated_query.astype(jnp.float32).reshape(rotated_query.shape[0], KEY_VALUE_HEADS, query_groups, HEAD_WIDTH)
    key_head_split = rotated_key.astype(jnp.float32).reshape(rotated_key.shape[0], KEY_VALUE_HEADS, HEAD_WIDTH)
    value_head_split = value_row_list.astype(jnp.float32).reshape(value_row_list.shape[0], KEY_VALUE_HEADS, HEAD_WIDTH)
    return (query_head_split, key_head_split, value_head_split)

def masked_scores(query_head_split, key_head_split, allowed):
    scores = jnp.einsum('tkgd,ukd->kgtu', query_head_split, key_head_split) * HEAD_WIDTH ** (-0.5)
    return jnp.where(allowed, scores, MASKED)

def one_sequence(pieces, cos_table, sin_table, weights):
    inputs, seq_segments, cotangent = pieces
    attn_gain, query_weight, key_weight, value_weight, output_weight, mlp_gain, gate_weight, up_weight, down_weight = weights
    query_groups = QUERY_HEADS // KEY_VALUE_HEADS
    residual = inputs.astype(jnp.float32)
    rms_one, unit_one, normed_one = normalize(residual, attn_gain)
    query_rows = matmul(normed_one, query_weight).astype(jnp.bfloat16)
    key_rows = matmul(normed_one, key_weight).astype(jnp.bfloat16)
    value_row_list = matmul(normed_one, value_weight).astype(jnp.bfloat16)
    rotated_query = rotate(query_rows.astype(jnp.float32), cos_table, sin_table).astype(jnp.bfloat16)
    rotated_key = rotate(key_rows.astype(jnp.float32), cos_table, sin_table).astype(jnp.bfloat16)
    places = jnp.arange(SEQUENCE_LENGTH)
    allowed = (places[None, :] <= places[:, None]) & (seq_segments[:, None] == seq_segments[None, :])
    query_head_split, key_head_split, value_head_split = head_views(rotated_query, rotated_key, value_row_list)
    scores = masked_scores(query_head_split, key_head_split, allowed)
    highest = lax.optimization_barrier(jnp.max(scores, axis=3, keepdims=True))
    logsum = highest + jnp.log(lax.optimization_barrier(jnp.sum(jnp.exp(scores - highest), axis=3, keepdims=True)))
    probs = jnp.exp(scores - logsum).astype(jnp.bfloat16)
    attention_mixture = jnp.einsum('kgtu,ukd->tkgd', probs.astype(jnp.float32), value_head_split)
    attention_mixture = attention_mixture.reshape(SEQUENCE_LENGTH, -1).astype(jnp.bfloat16)
    attn_out = matmul(attention_mixture, output_weight).astype(jnp.bfloat16)
    hidden = residual + attn_out.astype(jnp.float32)
    rms_two, unit_two, normed_two = normalize(hidden, mlp_gain)
    gate_rows = matmul(normed_two, gate_weight).astype(jnp.bfloat16)
    up_rows = matmul(normed_two, up_weight).astype(jnp.bfloat16)
    gate_float = gate_rows.astype(jnp.float32)
    up_float = up_rows.astype(jnp.float32)
    sigmoid_gate = jax.nn.sigmoid(gate_float)
    activated = (gate_float * sigmoid_gate * up_float).astype(jnp.bfloat16)
    mlp_out = matmul(activated, down_weight).astype(jnp.bfloat16)
    layer_out = (hidden + mlp_out.astype(jnp.float32)).astype(jnp.bfloat16)
    down_grad = matmul(activated.T, cotangent)
    dactivated = matmul(cotangent, down_weight.T)
    gate_delta = (dactivated * up_float * sigmoid_gate * (1.0 + gate_float * (1.0 - sigmoid_gate))).astype(jnp.bfloat16)
    up_delta = (dactivated * gate_float * sigmoid_gate).astype(jnp.bfloat16)
    gate_grad = matmul(normed_two.T, gate_delta)
    up_grad = matmul(normed_two.T, up_delta)
    dnormed_two = matmul(gate_delta, gate_weight.T) + matmul(up_delta, up_weight.T)
    dhidden_norm, mlpgain_grad = normalize_back(dnormed_two, mlp_gain, rms_two, unit_two)
    dhidden = cotangent.astype(jnp.float32) + dhidden_norm
    dhidden_bf = dhidden.astype(jnp.bfloat16)
    output_grad = matmul(attention_mixture.T, dhidden_bf)
    mixture_gradient = matmul(dhidden_bf, output_weight.T).astype(jnp.bfloat16)
    soft_weights = jnp.exp(scores - logsum)
    mixture_head_gradient = mixture_gradient.astype(jnp.float32).reshape(SEQUENCE_LENGTH, KEY_VALUE_HEADS, query_groups, HEAD_WIDTH)
    mixture_heads = attention_mixture.astype(jnp.float32).reshape(SEQUENCE_LENGTH, KEY_VALUE_HEADS, query_groups, HEAD_WIDTH)
    row_delta = jnp.transpose(lax.optimization_barrier(jnp.sum(mixture_heads * mixture_head_gradient, axis=3)), (1, 2, 0))[:, :, :, None]
    dprobs = jnp.einsum('tkgd,ukd->kgtu', mixture_head_gradient, value_head_split)
    dscores = (soft_weights * (dprobs - row_delta)).astype(jnp.bfloat16).astype(jnp.float32)
    dquery_rot = jnp.einsum('kgtu,ukd->tkgd', dscores, key_head_split).reshape(SEQUENCE_LENGTH, -1) * HEAD_WIDTH ** (-0.5)
    dkey_rot = jnp.einsum('kgtu,tkgd->ukd', dscores, query_head_split).reshape(SEQUENCE_LENGTH, -1) * HEAD_WIDTH ** (-0.5)
    dvalue = jnp.einsum('kgtu,tkgd->ukd', probs.astype(jnp.float32), mixture_head_gradient).reshape(SEQUENCE_LENGTH, -1)
    dquery = unrotate(dquery_rot, cos_table, sin_table).astype(jnp.bfloat16)
    dkey = unrotate(dkey_rot, cos_table, sin_table).astype(jnp.bfloat16)
    dvalue_bf = dvalue.astype(jnp.bfloat16)
    query_grad = matmul(normed_one.T, dquery)
    key_grad = matmul(normed_one.T, dkey)
    value_grad = matmul(normed_one.T, dvalue_bf)
    dnormed_one = matmul(dquery, query_weight.T) + matmul(dkey, key_weight.T) + matmul(dvalue_bf, value_weight.T)
    dresidual, attgain_grad = normalize_back(dnormed_one, attn_gain, rms_one, unit_one)
    input_grad = (dhidden + dresidual).astype(jnp.bfloat16)
    grads = (query_grad, key_grad, value_grad, output_grad, gate_grad, up_grad, down_grad, attgain_grad, mlpgain_grad)
    return ((layer_out, input_grad), grads)

def reference(inputs, segments, attn_gain, query_weight, key_weight, value_weight, output_weight, mlp_gain, gate_weight, up_weight, down_weight, cotangent):
    seq_count = inputs.shape[0] // SEQUENCE_LENGTH
    cos_table, sin_table = rope_angles(jnp.arange(SEQUENCE_LENGTH).astype(jnp.float32))
    weights = (attn_gain, query_weight, key_weight, value_weight, output_weight, mlp_gain, gate_weight, up_weight, down_weight)
    shapes = (query_weight, key_weight, value_weight, output_weight, gate_weight, up_weight, down_weight, attn_gain, mlp_gain)
    totals = tuple((jnp.zeros(array.shape, jnp.float32) for array in shapes))

    def scan_step(running, pieces):
        outputs, grads = one_sequence(pieces, cos_table, sin_table, weights)
        return (jax.tree.map(jnp.add, running, grads), outputs)
    stacked = (inputs.reshape(seq_count, SEQUENCE_LENGTH, -1), segments.reshape(seq_count, SEQUENCE_LENGTH), cotangent.reshape(seq_count, SEQUENCE_LENGTH, -1))
    totals, outputs = lax.scan(scan_step, totals, stacked)
    layer_out = outputs[0].reshape(inputs.shape)
    input_grad = outputs[1].reshape(inputs.shape)
    return (layer_out, input_grad, totals[0], totals[1], totals[2], totals[3], totals[4], totals[5], totals[6], totals[7], totals[8])
```

```python
import functools

import jax
import jax.numpy as jnp
from jax import lax
from jax.experimental import pallas as pl
from jax.experimental.pallas import tpu as pltpu
from jax.sharding import PartitionSpec as P

QUERY_HEADS = 15
KEY_VALUE_HEADS = 5
HEAD_WIDTH = 64
SEQUENCE_LENGTH = 1024

THETA = 100000.0
EPSILON = 1e-05
MASKED = -1e30

F32 = jnp.float32
BF16 = jnp.bfloat16
MESH = pl.DeviceIdType.MESH
ANY = pl.BlockSpec(memory_space=pl.ANY)
VMEM = pl.BlockSpec(memory_space=pltpu.VMEM)


class Net:
    def __init__(self, sizes, send_sems, recv_sems):
        self.dp, self.gx, self.gy = sizes
        self.cores = 2 if self.dp % 2 == 0 else 1
        self.hops = self.dp // self.cores
        self.d = lax.axis_index("dp")
        self.x = lax.axis_index("gx")
        self.y = lax.axis_index("gy")
        self.core = lax.rem(self.d, self.cores)
        self.hop = self.d // self.cores
        self.send_sems, self.recv_sems = send_sems, recv_sems
        self.sent, self.slots, self.pending = 0, 0, []

    def at_gx(self, j):
        return lax.rem(self.x + j, self.gx)

    def at_gy(self, k):
        return lax.rem(self.y + k, self.gy)

    def at_hop(self, i):
        return lax.rem(self.hop + i, self.hops)

    def gx_peer(self, j):
        return {"gx": self.at_gx(j)}

    def gy_peer(self, k):
        return {"gy": self.at_gy(k)}

    def hop_peer(self, i):
        return {"dp": self.at_hop(i) * self.cores + self.core}

    def core_peer(self):
        return {"dp": self.hop * self.cores + 1 - self.core}

    def dp_peer(self, i):
        return {"dp": lax.rem(self.d + i, self.dp)}

    def plane_peers(self):
        return [self.gx_peer(j) for j in range(1, self.gx)] + [
            self.gy_peer(k) for k in range(1, self.gy)
        ]

    def share_peers(self):
        peers = [self.hop_peer(i) for i in range(1, self.hops)]
        return peers + ([self.core_peer()] if self.cores == 2 else [])

    def greet(self, peers):
        barrier = pltpu.get_barrier_semaphore()
        for peer in peers:
            pl.semaphore_signal(barrier, inc=1, device_id=peer, device_id_type=MESH)
        pl.semaphore_wait(barrier, len(peers))

    def block(self, count):
        first = self.slots
        self.slots += count
        return first

    def copy(self, src, dst, slot, peer):
        return pltpu.make_async_remote_copy(
            src_ref=src,
            dst_ref=dst,
            send_sem=self.send_sems.at[self.sent],
            recv_sem=self.recv_sems.at[slot],
            device_id=peer,
            device_id_type=MESH,
        )

    def send(self, src, dst, slot, peer):
        copy = self.copy(src, dst, slot, peer)
        copy.start()
        self.sent += 1
        self.pending.append(copy)

    def arrive(self, dst, slot):
        pltpu.make_async_remote_copy(
            src_ref=dst,
            dst_ref=dst,
            send_sem=self.send_sems.at[0],
            recv_sem=self.recv_sems.at[slot],
            device_id=self.gy_peer(1),
            device_id_type=MESH,
        ).wait_recv()

    def drain(self):
        for copy in self.pending:
            copy.wait_send()


def far_first(count):
    order = list(range(1, count))
    return sorted(order, key=lambda k: -min(k, count - k))


class PlaneGather:
    def __init__(self, net, src, out):
        self.net, self.src, self.out = net, src, out
        self.gy_slot = net.block(net.gy)
        self.gx_slot = net.block(net.gx * net.gy)

    def start(self):
        net = self.net
        own = self.out(net.x, net.y)
        for k in range(1, net.gy):
            net.send(self.src, own, self.gy_slot + net.y, net.gy_peer(k))
        for j in range(1, net.gx):
            net.send(self.src, own, self.gx_slot + net.x * net.gy + net.y, net.gx_peer(j))

    def relay(self, k):
        net = self.net
        row = net.at_gy(k)
        piece = self.out(net.x, row)
        net.arrive(piece, self.gy_slot + row)
        for j in range(1, net.gx):
            net.send(piece, piece, self.gx_slot + net.x * net.gy + row, net.gx_peer(j))

    def settle(self, j, k):
        net = self.net
        side, row = net.at_gx(j), net.at_gy(k)
        net.arrive(self.out(side, row), self.gx_slot + side * net.gy + row)


class Share:
    def __init__(self, net, out):
        self.net, self.out = net, out
        self.hop_slot = net.block(net.hops)
        self.core_slot = net.block(net.dp)

    def start(self, src):
        net = self.net
        own = self.out(net.d)
        for i in range(1, net.hops):
            net.send(src, own, self.hop_slot + net.hop, net.hop_peer(i))
        if net.cores == 2:
            net.send(src, own, self.core_slot + net.d, net.core_peer())

    def relay(self):
        net = self.net
        for i in range(1, net.hops):
            hop = net.at_hop(i)
            rank = hop * net.cores + net.core
            piece = self.out(rank)
            net.arrive(piece, self.hop_slot + hop)
            if net.cores == 2:
                net.send(piece, piece, self.core_slot + rank, net.core_peer())

    def settle(self):
        net = self.net
        if net.cores == 2:
            for hop in range(net.hops):
                rank = hop * net.cores + 1 - net.core
                net.arrive(self.out(rank), self.core_slot + rank)


class PlaneSum:
    def __init__(self, net, src, landing_x, stage, landing_y):
        self.net, self.src = net, src
        self.landing_x, self.stage, self.landing_y = landing_x, stage, landing_y
        self.gx_slot = net.block(net.gx * net.gy)
        self.gy_slot = net.block(net.gy)

    def start(self, k):
        net = self.net
        row = net.at_gy(k)
        for j in range(1, net.gx):
            net.send(
                self.src(net.at_gx(j), row),
                self.landing_x.at[net.x, row],
                self.gx_slot + net.x * net.gy + row,
                net.gx_peer(j),
            )

    def relay(self, k):
        net = self.net
        row = net.at_gy(k)
        total = self.src(net.x, row)[...].astype(F32)
        for j in range(1, net.gx):
            side = net.at_gx(j)
            net.arrive(self.landing_x.at[side, row], self.gx_slot + side * net.gy + row)
            total = total + self.landing_x[side, row].astype(F32)
        if k == 0:
            self.landing_y[net.y] = total.astype(self.landing_y.dtype)
        else:
            self.stage[row] = total.astype(self.stage.dtype)
            net.send(
                self.stage.at[row], self.landing_y.at[net.y], self.gy_slot + net.y, net.gy_peer(k)
            )

    def total(self):
        net = self.net
        for k in range(1, net.gy):
            row = net.at_gy(k)
            net.arrive(self.landing_y.at[row], self.gy_slot + row)
        total = self.landing_y[0].astype(F32)
        for row in range(1, net.gy):
            total = total + self.landing_y[row].astype(F32)
        return total


def call(kernel, sizes, number, name, out_shapes, out_specs, in_specs, scratch, sends, slots):
    def body(*refs):
        net = Net(sizes, refs[-2], refs[-1])
        kernel(net, *refs[:-2])
        net.drain()
        assert net.sent <= sends and net.slots <= slots, (net.sent, net.slots)

    return pl.pallas_call(
        body,
        name=name,
        out_shape=out_shapes,
        in_specs=in_specs,
        out_specs=out_specs,
        scratch_shapes=list(scratch)
        + [pltpu.SemaphoreType.DMA((sends,)), pltpu.SemaphoreType.DMA((slots,))],
        compiler_params=pltpu.CompilerParams(collective_id=number, has_side_effects=True),
    )


def local(copies):
    for copy in copies:
        copy.start()


def wait_local(copies):
    for copy in copies:
        copy.wait()


def gather_weights(sizes, att, gate_up, down, cot, normed):
    dp, gx, gy = sizes
    hops = dp // 2
    share_count = (gx * gy + 2) * (hops - 1 + hops) + gx * gy + 2
    sends = share_count + 3 * (gx * gy) + 4
    slots = (gx * gy + 2) * (hops + dp) + 3 * (gy + gx * gy)

    def kernel(net, att_ref, gu_ref, dn_ref, cot_ref, nm_ref, att_out, gu_out, dn_out, cot_out, nm_out, sems):
        net.greet(net.plane_peers() + net.share_peers())
        att_plane = PlaneGather(net, att_ref, lambda a, b: att_out.at[a, b, net.d])
        gu_plane = PlaneGather(net, gu_ref, lambda a, b: gu_out.at[a, :, b])
        dn_plane = PlaneGather(net, dn_ref, lambda a, b: dn_out.at[a, b])
        first_hop = net.block(gx * gy * net.hops)
        first_core = net.block(gx * gy * net.dp)

        def shared(a, b):
            item = Share.__new__(Share)
            item.net = net
            item.out = lambda rank: att_out.at[a, b, rank]
            place = a * gy + b
            item.hop_slot = first_hop + place * net.hops
            item.core_slot = first_core + place * net.dp
            return item

        tokens = [(cot_ref, Share(net, lambda r: cot_out.at[r])), (nm_ref, Share(net, lambda r: nm_out.at[r]))]
        own = [
            pltpu.make_async_copy(att_ref, att_out.at[net.x, net.y, net.d], sems.at[0]),
            pltpu.make_async_copy(gu_ref, gu_out.at[net.x, :, net.y], sems.at[1]),
            pltpu.make_async_copy(dn_ref, dn_out.at[net.x, net.y], sems.at[2]),
            pltpu.make_async_copy(cot_ref, cot_out.at[net.d], sems.at[3]),
            pltpu.make_async_copy(nm_ref, nm_out.at[net.d], sems.at[4]),
        ]
        att_plane.start()
        shared(net.x, net.y).start(att_ref)
        gu_plane.start()
        dn_plane.start()
        local(own)
        for k in range(1, gy):
            att_plane.relay(k)
            row = net.at_gy(k)
            shared(net.x, row).start(att_out.at[net.x, row, net.d])
        for j in range(1, gx):
            for k in range(gy):
                att_plane.settle(j, k)
                side, row = net.at_gx(j), net.at_gy(k)
                shared(side, row).start(att_out.at[side, row, net.d])
        for ref, item in tokens:
            item.start(ref)
        for k in range(1, gy):
            gu_plane.relay(k)
            dn_plane.relay(k)
        places = [(j, k) for j in range(gx) for k in range(gy)]
        for j, k in places:
            shared(net.at_gx(j), net.at_gy(k)).relay()
        for _, item in tokens:
            item.relay()
        for j in range(1, gx):
            for k in range(gy):
                gu_plane.settle(j, k)
                dn_plane.settle(j, k)
        for j, k in places:
            shared(net.at_gx(j), net.at_gy(k)).settle()
        for _, item in tokens:
            item.settle()
        wait_local(own)

    shapes = (
        jax.ShapeDtypeStruct((gx, gy, dp) + att.shape, BF16),
        jax.ShapeDtypeStruct((gx, 2, gy) + gate_up.shape[1:], BF16),
        jax.ShapeDtypeStruct((gx, gy) + down.shape, BF16),
        jax.ShapeDtypeStruct((dp,) + cot.shape, BF16),
        jax.ShapeDtypeStruct((dp,) + normed.shape, BF16),
    )
    return call(
        kernel, sizes, 1, "gather_weights", shapes, [ANY] * 5, [VMEM] * 5,
        [pltpu.SemaphoreType.DMA((5,))], sends, slots,
    )(att, gate_up, down, cot, normed)


def gather_plane(sizes, piece):
    dp, gx, gy = sizes

    def kernel(net, src, out, sems):
        net.greet(net.plane_peers())
        plane = PlaneGather(net, src, lambda a, b: out.at[a, b])
        own = [pltpu.make_async_copy(src, out.at[net.x, net.y], sems.at[0])]
        plane.start()
        local(own)
        for k in range(1, gy):
            plane.relay(k)
        for j in range(1, gx):
            for k in range(gy):
                plane.settle(j, k)
        wait_local(own)

    shape = jax.ShapeDtypeStruct((gx, gy) + piece.shape, piece.dtype)
    return call(
        kernel, sizes, 2, "gather_plane", shape, ANY, [VMEM],
        [pltpu.SemaphoreType.DMA((1,))], gx * gy + gy, gy + gx * gy,
    )(piece)


def share_tokens(sizes, *pieces):
    dp, gx, gy = sizes
    count = len(pieces)

    def kernel(net, *refs):
        srcs, outs, sems = refs[:count], refs[count : 2 * count], refs[2 * count]
        net.greet(net.share_peers())
        items = [Share(net, lambda r, out=out: out.at[r]) for out in outs]
        own = [
            pltpu.make_async_copy(src, out.at[net.d], sems.at[n])
            for n, (src, out) in enumerate(zip(srcs, outs))
        ]
        for item, src in zip(items, srcs):
            item.start(src)
        local(own)
        for item in items:
            item.relay()
        for item in items:
            item.settle()
        wait_local(own)

    shapes = tuple(jax.ShapeDtypeStruct((dp,) + p.shape, p.dtype) for p in pieces)
    return call(
        kernel, sizes, 3, "share_tokens", shapes, [ANY] * count, [VMEM] * count,
        [pltpu.SemaphoreType.DMA((count,))], count * dp, count * (dp // 2 + dp),
    )(*pieces)


def sum_tokens(sizes, *parts):
    dp, gx, gy = sizes
    count = len(parts)
    hops = dp // 2
    shape = parts[0].shape[1:]

    def kernel(net, *refs):
        srcs, outs, scratch = refs[:count], refs[count : 2 * count], refs[2 * count :]
        landing_core, stage, landing_hop = scratch[:count], scratch[count : 2 * count], scratch[2 * count :]
        net.greet(net.share_peers())
        core_slots = [net.block(net.hops) for _ in range(count)]
        hop_slots = [net.block(net.hops) for _ in range(count)]
        order = list(range(1, net.hops)) + [0]
        for n in range(count):
            for i in order:
                hop = net.at_hop(i)
                net.send(
                    srcs[n].at[hop * 2 + 1 - net.core], landing_core[n].at[hop],
                    core_slots[n] + hop, net.core_peer(),
                )
        for n in range(count):
            for i in order:
                hop = net.at_hop(i)
                net.arrive(landing_core[n].at[hop], core_slots[n] + hop)
                total = srcs[n][hop * 2 + net.core].astype(F32) + landing_core[n][hop].astype(F32)
                if i == 0:
                    outs[n][...] = total
                else:
                    stage[n][hop] = total.astype(BF16)
                    net.send(
                        stage[n].at[hop], landing_hop[n].at[net.hop],
                        hop_slots[n] + net.hop, net.hop_peer(i),
                    )
        for n in range(count):
            for i in range(1, net.hops):
                hop = net.at_hop(i)
                net.arrive(landing_hop[n].at[hop], hop_slots[n] + hop)
                outs[n][...] += landing_hop[n][hop].astype(F32)

    shapes = tuple(jax.ShapeDtypeStruct(shape, F32) for _ in parts)
    slab = pltpu.VMEM((hops,) + shape, BF16)
    return call(
        kernel, sizes, 4, "sum_tokens", shapes, [VMEM] * count, [VMEM] * count,
        [slab] * (3 * count), count * dp, count * dp,
    )(*parts)


def sum_plane(sizes, blocks):
    dp, gx, gy = sizes
    shape = blocks.shape[2:]

    def kernel(net, src, out, landing_x, stage, landing_y):
        net.greet(net.plane_peers())
        item = PlaneSum(net, lambda a, b: src.at[a, b], landing_x, stage, landing_y)
        order = far_first(gy) + [0]
        for k in order:
            item.start(k)
        for k in order:
            item.relay(k)
        out[...] = item.total()

    slab = pltpu.VMEM((gy,) + shape, BF16)
    return call(
        kernel, sizes, 5, "sum_plane", jax.ShapeDtypeStruct(shape, F32), VMEM, [VMEM],
        [pltpu.VMEM((gx, gy) + shape, BF16), slab, slab], gx * gy + gy, gx * gy + gy,
    )(blocks)


def trade_tokens(sizes, blocks):
    dp, gx, gy = sizes

    def kernel(net, src, out, sems):
        peers = [net.dp_peer(i) for i in range(1, dp)]
        net.greet(peers)
        slot = net.block(dp)
        for i in range(1, dp):
            rank = lax.rem(net.d + i, dp)
            net.send(src.at[rank], out.at[net.d], slot + net.d, net.dp_peer(i))
        own = pltpu.make_async_copy(src.at[net.d], out.at[net.d], sems.at[0])
        own.start()
        for i in range(1, dp):
            rank = lax.rem(net.d + i, dp)
            net.arrive(out.at[rank], slot + rank)
        own.wait()

    return call(
        kernel, sizes, 6, "trade_tokens", jax.ShapeDtypeStruct(blocks.shape, blocks.dtype), ANY, [VMEM],
        [pltpu.SemaphoreType.DMA((1,))], dp, dp,
    )(blocks)


def reduce_weights(sizes, gate_up, down, att, gains):
    dp, gx, gy = sizes
    halves = gate_up.shape[1]
    pieces = [gate_up.shape[3:]] * halves + [down.shape[2:], att.shape[2:]]
    count = len(pieces)

    def kernel(net, gu_ref, dn_ref, att_ref, gain_ref, *refs):
        gu_out, dn_out, att_out, gain_out = refs[:4]
        refs = refs[4:]
        landing_x, stage, landing_y, result = (refs[n * (count + 1) : (n + 1) * (count + 1)] for n in range(4))
        sems = refs[-1]
        net.greet(net.plane_peers() + net.share_peers())
        sources = [lambda a, b, n=n: gu_ref.at[a, n, b] for n in range(halves)]
        sources += [lambda a, b: dn_ref.at[a, b], lambda a, b: att_ref.at[a, b], lambda a, b: gain_ref]
        outs = [lambda r, n=n: gu_out.at[r, n] for n in range(halves)]
        outs += [lambda r: dn_out.at[r], lambda r: att_out.at[r], lambda r: gain_out.at[r]]
        sums = [
            PlaneSum(net, sources[n], landing_x[n], stage[n], landing_y[n]) for n in range(count + 1)
        ]
        shares = [Share(net, out) for out in outs]
        order = far_first(gy) + [0]
        for k in order:
            for item in sums:
                item.start(k)
        for k in order:
            for item in sums:
                item.relay(k)
        own = []
        for n, (item, share) in enumerate(zip(sums, shares)):
            result[n][...] = item.total().astype(result[n].dtype)
            share.start(result[n])
            own.append(pltpu.make_async_copy(result[n], share.out(net.d), sems.at[n]))
            own[-1].start()
        for share in shares:
            share.relay()
        for share in shares:
            share.settle()
        wait_local(own)

    shapes = (
        jax.ShapeDtypeStruct((dp, halves) + pieces[0], BF16),
        jax.ShapeDtypeStruct((dp,) + pieces[-2], BF16),
        jax.ShapeDtypeStruct((dp,) + pieces[-1], BF16),
        jax.ShapeDtypeStruct((dp,) + gains.shape, F32),
    )
    kinds = [(piece, BF16) for piece in pieces] + [(gains.shape, F32)]
    scratch = [pltpu.VMEM((gx, gy) + p, t) for p, t in kinds]
    scratch += [pltpu.VMEM((gy,) + p, t) for p, t in kinds] * 2
    scratch += [pltpu.VMEM(p, t) for p, t in kinds]
    scratch += [pltpu.SemaphoreType.DMA((count + 1,))]
    return call(
        kernel, sizes, 7, "reduce_weights", shapes, [ANY] * 4, [VMEM] * 4, scratch,
        (count + 1) * (gx * gy + gy + dp), (count + 1) * (gx * gy + gy + dp + dp // 2),
    )(gate_up, down, att, gains)


def rope_angles(positions):
    half_dim = HEAD_WIDTH // 2
    inverse = THETA ** (-(jnp.arange(half_dim, dtype=F32) * 2.0 / HEAD_WIDTH))
    angles = positions[:, None] * inverse[None, :]
    return (jnp.cos(angles)[:, None, :], jnp.sin(angles)[:, None, :])


def rotate(values, cos_table, sin_table):
    item_count = values.shape[0]
    shaped = values.reshape(item_count, -1, HEAD_WIDTH)
    half_dim = HEAD_WIDTH // 2
    front_part = shaped[:, :, :half_dim]
    back_part = shaped[:, :, half_dim:]
    turned = jnp.concatenate(
        [
            front_part * cos_table - back_part * sin_table,
            back_part * cos_table + front_part * sin_table,
        ],
        axis=2,
    )
    return turned.reshape(item_count, -1)


def unrotate(values, cos_table, sin_table):
    return rotate(values, cos_table, -sin_table)


def normalize(values, gain):
    rms_rows = lax.rsqrt(jnp.mean(values * values, axis=1, keepdims=True) + EPSILON)
    unit_rows = values * rms_rows
    return (rms_rows, unit_rows, (unit_rows * gain).astype(BF16))


def normalize_back(dnormed, gain, rms_rows, unit_rows):
    scaled = dnormed * gain
    dvalues = rms_rows * (scaled - unit_rows * jnp.mean(scaled * unit_rows, axis=1, keepdims=True))
    return (dvalues, jnp.sum(dnormed * unit_rows, axis=0))


def plain_product(left, right):
    return jnp.dot(left, right, preferred_element_type=F32)


def weight_product(left, right):
    return lax.dot_general(left, right, (((0,), (0,)), ((), ())), preferred_element_type=F32)


def back_product(left, right):
    return lax.dot_general(left, right, (((1,), (1,)), ((), ())), preferred_element_type=F32)


def head_views(rotated_query, key_sequence, value_sequence):
    query_groups = QUERY_HEADS // KEY_VALUE_HEADS
    query_head_split = rotated_query.reshape(
        rotated_query.shape[0], KEY_VALUE_HEADS, query_groups, HEAD_WIDTH
    )
    key_head_split = key_sequence.reshape(key_sequence.shape[0], KEY_VALUE_HEADS, HEAD_WIDTH)
    value_head_split = value_sequence.reshape(value_sequence.shape[0], KEY_VALUE_HEADS, HEAD_WIDTH)
    return (query_head_split, key_head_split, value_head_split)


def masked_scores(query_head_split, key_head_split, allowed):
    scores = jnp.einsum(
        "tkgd,ukd->kgtu", query_head_split, key_head_split, preferred_element_type=F32
    ) * HEAD_WIDTH ** (-0.5)
    return jnp.where(allowed, scores, MASKED)


def attend(rotated_query, key_sequence, value_sequence, allowed):
    query_head_split, key_head_split, value_head_split = head_views(
        rotated_query, key_sequence, value_sequence
    )
    scores = masked_scores(query_head_split, key_head_split, allowed)
    highest = jnp.max(scores, axis=3, keepdims=True)
    logsum = highest + jnp.log(jnp.sum(jnp.exp(scores - highest), axis=3, keepdims=True))
    probs = jnp.exp(scores - logsum).astype(BF16)
    attention_mixture = jnp.einsum(
        "kgtu,ukd->tkgd", probs, value_head_split, preferred_element_type=F32
    )
    return (attention_mixture.reshape(rotated_query.shape[0], -1).astype(BF16), logsum)


def attend_back(
    rotated_query,
    key_sequence,
    value_sequence,
    allowed,
    logsum,
    attention_mixture,
    mixture_gradient,
):
    query_head_split, key_head_split, value_head_split = head_views(
        rotated_query, key_sequence, value_sequence
    )
    count_of_rows = rotated_query.shape[0]
    query_groups = QUERY_HEADS // KEY_VALUE_HEADS
    soft_weights = jnp.exp(masked_scores(query_head_split, key_head_split, allowed) - logsum)
    probs = soft_weights.astype(BF16)
    mixture_head_gradient = mixture_gradient.reshape(
        count_of_rows, KEY_VALUE_HEADS, query_groups, HEAD_WIDTH
    )
    mixture_heads = attention_mixture.reshape(
        count_of_rows, KEY_VALUE_HEADS, query_groups, HEAD_WIDTH
    )
    row_delta = jnp.sum(mixture_heads.astype(F32) * mixture_head_gradient.astype(F32), axis=3)
    row_delta = jnp.transpose(row_delta, (1, 2, 0))[:, :, :, None]
    dprobs = jnp.einsum(
        "tkgd,ukd->kgtu", mixture_head_gradient, value_head_split, preferred_element_type=F32
    )
    dscores = (soft_weights * (dprobs - row_delta)).astype(BF16)
    dquery = jnp.einsum(
        "kgtu,ukd->tkgd", dscores, key_head_split, preferred_element_type=F32
    ).reshape(count_of_rows, -1) * HEAD_WIDTH ** (-0.5)
    dkeys = jnp.einsum(
        "kgtu,tkgd->ukd", dscores, query_head_split, preferred_element_type=F32
    ).reshape(key_sequence.shape[0], -1) * HEAD_WIDTH ** (-0.5)
    dvalues = jnp.einsum(
        "kgtu,tkgd->ukd", probs, mixture_head_gradient, preferred_element_type=F32
    ).reshape(key_sequence.shape[0], -1)
    return (dquery, dkeys, dvalues)


def on_device(
    sizes,
    inputs,
    segments,
    attn_gain,
    query_weight,
    key_weight,
    value_weight,
    output_weight,
    mlp_gain,
    gate_weight,
    up_weight,
    down_weight,
    cotangent,
):
    dp, gx, gy = sizes
    count_of_rows, width = inputs.shape
    rank = lax.axis_index("dp")
    begin_row = (lax.axis_index("gx") * gy + lax.axis_index("gy")) * count_of_rows
    seq_begin = begin_row // SEQUENCE_LENGTH * SEQUENCE_LENGTH
    local_places = begin_row - seq_begin + jnp.arange(count_of_rows)
    cos_table, sin_table = rope_angles(local_places.astype(F32))
    query_segs = lax.dynamic_slice_in_dim(segments, begin_row, count_of_rows, 0)
    allowed = (jnp.arange(SEQUENCE_LENGTH)[None, :] <= local_places[:, None]) & (
        query_segs[:, None] == segments[None, :]
    )
    residual = inputs.astype(F32)
    rms_one, unit_one, normed_one = normalize(residual, attn_gain)

    fan = query_weight.shape[0]
    q_cols, k_cols, v_cols = query_weight.shape[1], key_weight.shape[1], value_weight.shape[1]
    o_cols = output_weight.shape[1]
    qkv_cols = q_cols + k_cols + v_cols
    all_cols = qkv_cols + o_cols
    att_share = all_cols // dp
    packed = jnp.concatenate([query_weight, key_weight, value_weight, output_weight], axis=1).T
    att_part = lax.dynamic_slice_in_dim(packed, rank * att_share, att_share, 0)
    share = gate_weight.shape[1] // dp
    groups = gy // gx
    gate_up_part = jnp.stack(
        [
            lax.dynamic_slice_in_dim(gate_weight, rank * share, share, 1).T,
            lax.dynamic_slice_in_dim(up_weight, rank * share, share, 1).T,
        ]
    )
    down_cols = down_weight.shape[1]
    down_part = lax.dynamic_slice_in_dim(
        down_weight.reshape(groups, dp, share, down_cols), rank, 1, 1
    ).reshape(groups * share, down_cols).T

    att_all, gate_up_all, down_all, cot_all, normed_one_all = gather_weights(
        sizes, att_part, gate_up_part, down_part, cotangent, normed_one
    )
    att_all = att_all.reshape(gx, gy, all_cols, fan)
    qkv_rows = att_all[:, :, :qkv_cols].reshape(gx, gy * qkv_cols, fan)
    out_rows = att_all[:, :, qkv_cols:].reshape(gx, gy * o_cols, fan)
    hidden_width = gy * share
    gate_up_all = gate_up_all.reshape(gx, 2 * hidden_width, fan)
    half_hidden = groups * share
    down_all = down_all.reshape(gx, gy * down_cols, half_hidden)
    cot_all = cot_all.reshape(dp * count_of_rows, width)
    normed_one_all = normed_one_all.reshape(dp * count_of_rows, width)

    def parts(rows):
        return [rows[:, a * fan : (a + 1) * fan] for a in range(gx)]

    def onto(rows, weights):
        return sum(back_product(part, weights[a]) for a, part in enumerate(parts(rows)))

    def back_onto(rows, weights):
        return jnp.concatenate([plain_product(rows, weights[a]) for a in range(gx)], axis=1)

    qkv = onto(normed_one, qkv_rows).astype(BF16).reshape(count_of_rows, gy, qkv_cols)
    query_rows = qkv[:, :, :q_cols].reshape(count_of_rows, -1)
    key_rows = qkv[:, :, q_cols : q_cols + k_cols].reshape(count_of_rows, -1)
    value_rows = qkv[:, :, q_cols + k_cols :].reshape(count_of_rows, -1)
    rotated_query = rotate(query_rows.astype(F32), cos_table, sin_table).astype(BF16)
    rotated_key = rotate(key_rows.astype(F32), cos_table, sin_table).astype(BF16)
    kv_width = rotated_key.shape[1]
    kv_all = gather_plane(sizes, jnp.concatenate([rotated_key, value_rows], axis=1))
    kv_all = kv_all.reshape(gx * gy * count_of_rows, 2 * kv_width)
    key_all, value_all = kv_all[:, :kv_width], kv_all[:, kv_width:]
    attention_mixture, logsum = attend(rotated_query, key_all, value_all, allowed)
    attn_out = onto(attention_mixture, out_rows).astype(BF16)
    hidden = residual + attn_out.astype(F32)
    rms_two, unit_two, normed_two = normalize(hidden, mlp_gain)

    normed_all, mixed_all = share_tokens(sizes, normed_two, attention_mixture)
    normed_all = normed_all.reshape(dp * count_of_rows, width)
    mixed_all = mixed_all.reshape(dp * count_of_rows, width)
    gate_up = onto(normed_all, gate_up_all).astype(BF16)
    gate_float = gate_up[:, :hidden_width].astype(F32)
    up_float = gate_up[:, hidden_width:].astype(F32)
    sigmoid_gate = jax.nn.sigmoid(gate_float)
    activated = (gate_float * sigmoid_gate * up_float).astype(BF16)
    dactivated = back_onto(cot_all, down_all)
    gate_delta = (
        dactivated * up_float * sigmoid_gate * (1.0 + gate_float * (1.0 - sigmoid_gate))
    ).astype(BF16)
    up_delta = (dactivated * gate_float * sigmoid_gate).astype(BF16)
    deltas = jnp.concatenate([gate_delta, up_delta], axis=1)
    activated_parts = [activated[:, a * half_hidden : (a + 1) * half_hidden] for a in range(gx)]
    mlp_part = sum(back_product(part, down_all[a]) for a, part in enumerate(activated_parts))
    dnormed_part = back_onto(deltas, gate_up_all)
    dnormed_two, mlp_out = sum_tokens(
        sizes,
        dnormed_part.astype(BF16).reshape(dp, count_of_rows, width),
        mlp_part.astype(BF16).reshape(dp, count_of_rows, width),
    )
    layer_out = (hidden + mlp_out).astype(BF16)

    gate_up_grad = jnp.stack([weight_product(deltas, part).astype(BF16) for part in parts(normed_all)])
    gate_up_grad = gate_up_grad.reshape(gx, 2, gy, share, fan)
    down_grad = jnp.stack([weight_product(cot_all, part).astype(BF16) for part in activated_parts])
    down_grad = down_grad.reshape(gx, gy, down_cols, half_hidden)

    dhidden_norm, mlpgain_part = normalize_back(dnormed_two, mlp_gain, rms_two, unit_two)
    dhidden = cotangent.astype(F32) + dhidden_norm
    dhidden_bf = dhidden.astype(BF16)
    mixture_gradient = back_onto(dhidden_bf, out_rows).astype(BF16)
    dquery_rot, dkey_seq, dvalue_seq = attend_back(
        rotated_query, key_all, value_all, allowed, logsum, attention_mixture, mixture_gradient
    )
    dkv = sum_plane(
        sizes,
        jnp.concatenate([dkey_seq, dvalue_seq], axis=1)
        .astype(BF16)
        .reshape(gx, gy, count_of_rows, 2 * kv_width),
    )
    dquery = unrotate(dquery_rot, cos_table, sin_table).astype(BF16)
    dkey = unrotate(dkv[:, :kv_width], cos_table, sin_table).astype(BF16)
    dvalue_bf = dkv[:, kv_width:].astype(BF16)
    dqkv = jnp.concatenate(
        [
            dquery.reshape(count_of_rows, gy, q_cols),
            dkey.reshape(count_of_rows, gy, k_cols),
            dvalue_bf.reshape(count_of_rows, gy, v_cols),
        ],
        axis=2,
    )
    dall = jnp.concatenate([dqkv, dhidden_bf.reshape(count_of_rows, gy, o_cols)], axis=2)
    dall = dall.reshape(count_of_rows, gy, dp, att_share).transpose(2, 0, 1, 3)
    dall = trade_tokens(sizes, dall.reshape(dp, count_of_rows, gy * att_share))
    dall = dall.reshape(dp * count_of_rows, gy * att_share)
    places = rank * att_share + lax.broadcasted_iota(jnp.int32, (gy, att_share, 1), 1)
    from_normed = (places < qkv_cols).reshape(gy * att_share, 1)
    att_grad = jnp.stack(
        [
            jnp.where(from_normed, weight_product(dall, one), weight_product(dall, two)).astype(BF16)
            for one, two in zip(parts(normed_one_all), parts(mixed_all))
        ]
    ).reshape(gx, gy, att_share, fan)
    dnormed_one = back_onto(dqkv.reshape(count_of_rows, gy * qkv_cols), qkv_rows)
    dresidual, attgain_part = normalize_back(dnormed_one, attn_gain, rms_one, unit_one)
    input_grad = (dhidden + dresidual).astype(BF16)
    gain_parts = jnp.concatenate([attgain_part, mlpgain_part])
    gain_rows = -(-gain_parts.shape[0] // 1024) * 8
    gain_parts = jnp.pad(gain_parts, (0, gain_rows * 128 - gain_parts.shape[0])).reshape(gain_rows, 128)

    gate_up_sum, down_sum, att_sum, gain_sum = reduce_weights(
        sizes, gate_up_grad, down_grad, att_grad, gain_parts
    )
    gate_grad = gate_up_sum[:, 0].reshape(dp * share, fan).T.astype(F32)
    up_grad = gate_up_sum[:, 1].reshape(dp * share, fan).T.astype(F32)
    down_grad = (
        down_sum.reshape(dp, down_cols, groups, share)
        .transpose(2, 0, 3, 1)
        .reshape(down_weight.shape)
        .astype(F32)
    )
    att_sum = att_sum.reshape(all_cols, fan).T.astype(F32)
    gains = jnp.sum(gain_sum, axis=0).reshape(-1)
    return (
        layer_out,
        input_grad,
        att_sum[:, :q_cols],
        att_sum[:, q_cols : q_cols + k_cols],
        att_sum[:, q_cols + k_cols : qkv_cols],
        att_sum[:, qkv_cols:],
        gate_grad,
        up_grad,
        down_grad,
        gains[:width],
        gains[width : 2 * width],
    )


def solution(mesh):
    sizes = (mesh.shape["dp"], mesh.shape["gx"], mesh.shape["gy"])
    tokens = P(("dp", "gx", "gy"), None)
    block = P("gx", "gy")
    return jax.shard_map(
        functools.partial(on_device, sizes),
        mesh=mesh,
        in_specs=(tokens, P("dp"), P(), block, block, block, block, P(), block, block, block, tokens),
        out_specs=(tokens, tokens) + (block,) * 7 + (P(), P()),
        check_vma=False,
    )
```

```python
import functools

import jax
import jax.numpy as jnp
from jax import lax
from jax.experimental import pallas as pl
from jax.experimental.pallas import tpu as pltpu
from jax.sharding import PartitionSpec as P

QUERY_HEADS = 15
KEY_VALUE_HEADS = 5
GROUPS = QUERY_HEADS // KEY_VALUE_HEADS
HEAD_WIDTH = 64
SEQUENCE_LENGTH = 1024

THETA = 100000.0
EPSILON = 1e-05
MASKED = -1e30

F32 = jnp.float32
BF16 = jnp.bfloat16
MESH = pl.DeviceIdType.MESH
ANY = pl.BlockSpec(memory_space=pl.ANY)
VMEM = pl.BlockSpec(memory_space=pltpu.VMEM)


def plain_product(left, right):
    return jnp.dot(left, right, preferred_element_type=F32)


def weight_product(left, right):
    return lax.dot_general(left, right, (((0,), (0,)), ((), ())), preferred_element_type=F32)


def back_product(left, right):
    return lax.dot_general(left, right, (((1,), (1,)), ((), ())), preferred_element_type=F32)


class Net:
    def __init__(self, sizes, send_sems, recv_sems):
        self.dp, self.gx, self.gy = sizes
        self.cores = 2 if self.dp % 2 == 0 else 1
        self.hops = self.dp // self.cores
        self.d = lax.axis_index("dp")
        self.x = lax.axis_index("gx")
        self.y = lax.axis_index("gy")
        self.core = lax.rem(self.d, self.cores)
        self.hop = self.d // self.cores
        self.send_sems, self.recv_sems = send_sems, recv_sems
        self.sent, self.slots, self.pending = 0, 0, []

    def at_gx(self, j):
        return lax.rem(self.x + j, self.gx)

    def at_gy(self, k):
        return lax.rem(self.y + k, self.gy)

    def at_hop(self, i):
        return lax.rem(self.hop + i, self.hops)

    def gx_peer(self, j):
        return {"gx": self.at_gx(j)}

    def gy_peer(self, k):
        return {"gy": self.at_gy(k)}

    def hop_peer(self, i):
        return {"dp": self.at_hop(i) * self.cores + self.core}

    def core_peer(self):
        return {"dp": self.hop * self.cores + 1 - self.core}

    def dp_peer(self, i):
        return {"dp": lax.rem(self.d + i, self.dp)}

    def plane_peers(self):
        return [self.gx_peer(j) for j in range(1, self.gx)] + [
            self.gy_peer(k) for k in range(1, self.gy)
        ]

    def share_peers(self):
        peers = [self.hop_peer(i) for i in range(1, self.hops)]
        return peers + ([self.core_peer()] if self.cores == 2 else [])

    def greet(self, peers):
        barrier = pltpu.get_barrier_semaphore()
        for peer in peers:
            pl.semaphore_signal(barrier, inc=1, device_id=peer, device_id_type=MESH)
        pl.semaphore_wait(barrier, len(peers))

    def block(self, count):
        first = self.slots
        self.slots += count
        return first

    def copy(self, src, dst, slot, peer):
        return pltpu.make_async_remote_copy(
            src_ref=src,
            dst_ref=dst,
            send_sem=self.send_sems.at[self.sent],
            recv_sem=self.recv_sems.at[slot],
            device_id=peer,
            device_id_type=MESH,
        )

    def send(self, src, dst, slot, peer):
        copy = self.copy(src, dst, slot, peer)
        copy.start()
        self.sent += 1
        self.pending.append(copy)

    def arrive(self, dst, slot):
        pltpu.make_async_remote_copy(
            src_ref=dst,
            dst_ref=dst,
            send_sem=self.send_sems.at[0],
            recv_sem=self.recv_sems.at[slot],
            device_id=self.gy_peer(1),
            device_id_type=MESH,
        ).wait_recv()

    def drain(self):
        for copy in self.pending:
            copy.wait_send()


def far_first(count):
    order = list(range(1, count))
    return sorted(order, key=lambda k: -min(k, count - k))


class PlaneGather:
    def __init__(self, net, src, out):
        self.net, self.src, self.out = net, src, out
        self.gy_slot = net.block(net.gy)
        self.gx_slot = net.block(net.gx * net.gy)

    def start(self):
        net = self.net
        own = self.out(net.x, net.y)
        for k in range(1, net.gy):
            net.send(self.src, own, self.gy_slot + net.y, net.gy_peer(k))
        for j in range(1, net.gx):
            net.send(self.src, own, self.gx_slot + net.x * net.gy + net.y, net.gx_peer(j))

    def relay(self, k):
        net = self.net
        row = net.at_gy(k)
        piece = self.out(net.x, row)
        net.arrive(piece, self.gy_slot + row)
        for j in range(1, net.gx):
            net.send(piece, piece, self.gx_slot + net.x * net.gy + row, net.gx_peer(j))

    def settle(self, j, k):
        net = self.net
        side, row = net.at_gx(j), net.at_gy(k)
        net.arrive(self.out(side, row), self.gx_slot + side * net.gy + row)


class Share:
    def __init__(self, net, out):
        self.net, self.out = net, out
        self.hop_slot = net.block(net.hops)
        self.core_slot = net.block(net.dp)

    def start(self, src):
        net = self.net
        own = self.out(net.d)
        for i in range(1, net.hops):
            net.send(src, own, self.hop_slot + net.hop, net.hop_peer(i))
        if net.cores == 2:
            net.send(src, own, self.core_slot + net.d, net.core_peer())

    def relay(self):
        net = self.net
        for i in range(1, net.hops):
            hop = net.at_hop(i)
            rank = hop * net.cores + net.core
            piece = self.out(rank)
            net.arrive(piece, self.hop_slot + hop)
            if net.cores == 2:
                net.send(piece, piece, self.core_slot + rank, net.core_peer())

    def settle(self):
        net = self.net
        if net.cores == 2:
            for hop in range(net.hops):
                rank = hop * net.cores + 1 - net.core
                net.arrive(self.out(rank), self.core_slot + rank)


class PlaneSum:
    def __init__(self, net, src, landing_x, stage, landing_y):
        self.net, self.src = net, src
        self.landing_x, self.stage, self.landing_y = landing_x, stage, landing_y
        self.gx_slot = net.block(net.gx * net.gy)
        self.gy_slot = net.block(net.gy)

    def start(self, k):
        net = self.net
        row = net.at_gy(k)
        for j in range(1, net.gx):
            net.send(
                self.src(net.at_gx(j), row),
                self.landing_x.at[net.x, row],
                self.gx_slot + net.x * net.gy + row,
                net.gx_peer(j),
            )

    def relay(self, k):
        net = self.net
        row = net.at_gy(k)
        total = self.src(net.x, row)[...].astype(F32)
        for j in range(1, net.gx):
            side = net.at_gx(j)
            net.arrive(self.landing_x.at[side, row], self.gx_slot + side * net.gy + row)
            total = total + self.landing_x[side, row].astype(F32)
        if k == 0:
            self.landing_y[net.y] = total.astype(self.landing_y.dtype)
        else:
            self.stage[row] = total.astype(self.stage.dtype)
            net.send(
                self.stage.at[row], self.landing_y.at[net.y], self.gy_slot + net.y, net.gy_peer(k)
            )

    def total(self):
        net = self.net
        for k in range(1, net.gy):
            row = net.at_gy(k)
            net.arrive(self.landing_y.at[row], self.gy_slot + row)
        total = self.landing_y[0].astype(F32)
        for row in range(1, net.gy):
            total = total + self.landing_y[row].astype(F32)
        return total


def call(kernel, sizes, number, name, out_shapes, out_specs, in_specs, scratch, sends, slots):
    def body(*refs):
        net = Net(sizes, refs[-2], refs[-1])
        kernel(net, *refs[:-2])
        net.drain()
        assert net.sent <= sends and net.slots <= slots, (net.sent, net.slots)

    return pl.pallas_call(
        body,
        name=name,
        out_shape=out_shapes,
        in_specs=in_specs,
        out_specs=out_specs,
        scratch_shapes=list(scratch)
        + [pltpu.SemaphoreType.DMA((sends,)), pltpu.SemaphoreType.DMA((slots,))],
        compiler_params=pltpu.CompilerParams(collective_id=number, has_side_effects=True),
    )


def local(copies):
    for copy in copies:
        copy.start()


def wait_local(copies):
    for copy in copies:
        copy.wait()


def gather_weights(sizes, att, gate_up, down, cot, normed):
    dp, gx, gy = sizes
    hops = dp // 2
    share_count = (gx * gy + 2) * (hops - 1 + hops) + gx * gy + 2
    sends = share_count + 3 * (gx * gy) + 4
    slots = (gx * gy + 2) * (hops + dp) + 3 * (gy + gx * gy)

    def kernel(net, att_ref, gu_ref, dn_ref, cot_ref, nm_ref, att_out, gu_out, dn_out, cot_out, nm_out, sems):
        net.greet(net.plane_peers() + net.share_peers())
        att_plane = PlaneGather(net, att_ref, lambda a, b: att_out.at[a, b, net.d])
        gu_plane = PlaneGather(net, gu_ref, lambda a, b: gu_out.at[a, :, b])
        dn_plane = PlaneGather(net, dn_ref, lambda a, b: dn_out.at[a, b])
        first_hop = net.block(gx * gy * net.hops)
        first_core = net.block(gx * gy * net.dp)

        def shared(a, b):
            item = Share.__new__(Share)
            item.net = net
            item.out = lambda rank: att_out.at[a, b, rank]
            place = a * gy + b
            item.hop_slot = first_hop + place * net.hops
            item.core_slot = first_core + place * net.dp
            return item

        tokens = [(cot_ref, Share(net, lambda r: cot_out.at[r])), (nm_ref, Share(net, lambda r: nm_out.at[r]))]
        own = [
            pltpu.make_async_copy(att_ref, att_out.at[net.x, net.y, net.d], sems.at[0]),
            pltpu.make_async_copy(gu_ref, gu_out.at[net.x, :, net.y], sems.at[1]),
            pltpu.make_async_copy(dn_ref, dn_out.at[net.x, net.y], sems.at[2]),
            pltpu.make_async_copy(cot_ref, cot_out.at[net.d], sems.at[3]),
            pltpu.make_async_copy(nm_ref, nm_out.at[net.d], sems.at[4]),
        ]
        att_plane.start()
        shared(net.x, net.y).start(att_ref)
        gu_plane.start()
        dn_plane.start()
        local(own)
        for k in range(1, gy):
            att_plane.relay(k)
            row = net.at_gy(k)
            shared(net.x, row).start(att_out.at[net.x, row, net.d])
        for j in range(1, gx):
            for k in range(gy):
                att_plane.settle(j, k)
                side, row = net.at_gx(j), net.at_gy(k)
                shared(side, row).start(att_out.at[side, row, net.d])
        for ref, item in tokens:
            item.start(ref)
        for k in range(1, gy):
            gu_plane.relay(k)
            dn_plane.relay(k)
        places = [(j, k) for j in range(gx) for k in range(gy)]
        for j, k in places:
            shared(net.at_gx(j), net.at_gy(k)).relay()
        for _, item in tokens:
            item.relay()
        for j in range(1, gx):
            for k in range(gy):
                gu_plane.settle(j, k)
                dn_plane.settle(j, k)
        for j, k in places:
            shared(net.at_gx(j), net.at_gy(k)).settle()
        for _, item in tokens:
            item.settle()
        wait_local(own)

    shapes = (
        jax.ShapeDtypeStruct((gx, gy, dp) + att.shape, BF16),
        jax.ShapeDtypeStruct((gx, 2, gy) + gate_up.shape[1:], BF16),
        jax.ShapeDtypeStruct((gx, gy) + down.shape, BF16),
        jax.ShapeDtypeStruct((dp,) + cot.shape, BF16),
        jax.ShapeDtypeStruct((dp,) + normed.shape, BF16),
    )
    return call(
        kernel, sizes, 1, "gather_weights", shapes, [ANY] * 5, [VMEM] * 5,
        [pltpu.SemaphoreType.DMA((5,))], sends, slots,
    )(att, gate_up, down, cot, normed)


def turned(values):
    return jnp.transpose(values)


def head_rows(ref, first, lead=()):
    return jnp.concatenate(
        [ref[:, h * HEAD_WIDTH : (h + 1) * HEAD_WIDTH] for h in range(first, first + GROUPS)], axis=0
    )


def key_columns(ref, place):
    columns = ref[:, :, :, place * HEAD_WIDTH : (place + 1) * HEAD_WIDTH]
    return columns.reshape(-1, HEAD_WIDTH)


def put_heads(ref, first, rows, values):
    for n in range(GROUPS):
        lanes = slice((first + n) * HEAD_WIDTH, (first + n + 1) * HEAD_WIDTH)
        ref[:, lanes] = values[n * rows : (n + 1) * rows].astype(ref.dtype)


def attend_heads(q_ref, kv_ref, bias_ref, mixed_ref, logsum_ref):
    rows = q_ref.shape[0]
    bias = jnp.concatenate([bias_ref[...]] * GROUPS, axis=1)
    for k in range(KEY_VALUE_HEADS):
        query = head_rows(q_ref, k * GROUPS)
        scores = back_product(key_columns(kv_ref, k), query) * HEAD_WIDTH ** (-0.5) + bias
        highest = jnp.max(scores, axis=0, keepdims=True)
        weights = jnp.exp(scores - highest)
        sums = jnp.sum(weights, axis=0, keepdims=True)
        logsum_ref[k : k + 1, :] = highest + jnp.log(sums)
        probs = (weights * (1.0 / sums)).astype(BF16)
        mixed = weight_product(key_columns(kv_ref, KEY_VALUE_HEADS + k), probs)
        put_heads(mixed_ref, k * GROUPS, rows, turned(mixed))


def attend_heads_back(q_ref, kv_ref, bias_ref, logsum_ref, mixed_ref, dmixed_ref, dq_ref, dkv_ref):
    rows = q_ref.shape[0]
    bias = jnp.concatenate([bias_ref[...]] * GROUPS, axis=1)
    blocks = kv_ref.shape[:3]
    for k in range(KEY_VALUE_HEADS):
        query = head_rows(q_ref, k * GROUPS)
        mixed = head_rows(mixed_ref, k * GROUPS)
        dmixed = head_rows(dmixed_ref, k * GROUPS)
        keys = key_columns(kv_ref, k)
        scores = back_product(keys, query) * HEAD_WIDTH ** (-0.5) + bias
        weights = jnp.exp(scores - logsum_ref[k : k + 1, :])
        delta = jnp.sum(turned(mixed.astype(F32) * dmixed.astype(F32)), axis=0, keepdims=True)
        dprobs = back_product(key_columns(kv_ref, KEY_VALUE_HEADS + k), dmixed)
        dscores = (weights * (dprobs - delta)).astype(BF16)
        dquery = weight_product(keys, dscores) * HEAD_WIDTH ** (-0.5)
        put_heads(dq_ref, k * GROUPS, rows, turned(dquery))
        dkeys = plain_product(dscores, query) * HEAD_WIDTH ** (-0.5)
        dvalues = plain_product(weights.astype(BF16), dmixed)
        lanes = slice(k * HEAD_WIDTH, (k + 1) * HEAD_WIDTH)
        dkv_ref[:, :, :, lanes] = dkeys.astype(BF16).reshape(blocks + (HEAD_WIDTH,))
        place = KEY_VALUE_HEADS + k
        lanes = slice(place * HEAD_WIDTH, (place + 1) * HEAD_WIDTH)
        dkv_ref[:, :, :, lanes] = dvalues.astype(BF16).reshape(blocks + (HEAD_WIDTH,))


def attend(sizes, query, piece, bias):
    dp, gx, gy = sizes

    def kernel(net, q_ref, src, bias_ref, out, mixed_ref, logsum_ref, sems):
        net.greet(net.plane_peers())
        plane = PlaneGather(net, src, lambda a, b: out.at[a, b])
        own = [pltpu.make_async_copy(src, out.at[net.x, net.y], sems.at[0])]
        plane.start()
        local(own)
        for k in range(1, gy):
            plane.relay(k)
        for j in range(1, gx):
            for k in range(gy):
                plane.settle(j, k)
        wait_local(own)
        attend_heads(q_ref, out, bias_ref, mixed_ref, logsum_ref)

    rows = query.shape[0]
    shapes = (
        jax.ShapeDtypeStruct((gx, gy) + piece.shape, piece.dtype),
        jax.ShapeDtypeStruct(query.shape, BF16),
        jax.ShapeDtypeStruct((KEY_VALUE_HEADS, GROUPS * rows), F32),
    )
    return call(
        kernel, sizes, 2, "attend", shapes, [VMEM] * 3, [VMEM] * 3,
        [pltpu.SemaphoreType.DMA((1,))], gx * gy + gy, gy + gx * gy,
    )(query, piece, bias)


def attend_back(query, kv_all, bias, logsum, mixed, dmixed):
    return pl.pallas_call(
        attend_heads_back,
        name="attend_back",
        out_shape=(
            jax.ShapeDtypeStruct(query.shape, F32),
            jax.ShapeDtypeStruct(kv_all.shape, BF16),
        ),
        in_specs=[VMEM] * 6,
        out_specs=[VMEM] * 2,
    )(query, kv_all, bias, logsum, mixed, dmixed)


def mlp(normed_all, cot_all, gate_up, down):
    gx, both, fan = gate_up.shape
    rows, width = normed_all.shape
    hidden = both // 2
    part = down.shape[2]
    step = rows // 2 if rows % 32 == 0 else rows

    def kernel(n_ref, c_ref, gu_ref, dt_ref, dn_ref, mo_ref, gg_ref, dg_ref, act_ref, delta_ref):
        def tokens(i, carry):
            span = pl.ds(pl.multiple_of(i * step, step), step)
            normed, cot = n_ref[span, :], c_ref[span, :]
            gate_up_rows = sum(
                back_product(normed[:, a * fan : (a + 1) * fan], gu_ref[a]) for a in range(gx)
            ).astype(BF16)
            gate = gate_up_rows[:, :hidden].astype(F32)
            up = gate_up_rows[:, hidden:].astype(F32)
            dact = jnp.concatenate([plain_product(cot, dt_ref[a]) for a in range(gx)], axis=1)
            sigmoid = jax.nn.sigmoid(gate)
            act = (gate * sigmoid * up).astype(BF16)
            gate_delta = (dact * up * sigmoid * (1.0 + gate * (1.0 - sigmoid))).astype(BF16)
            up_delta = (dact * gate * sigmoid).astype(BF16)
            deltas = jnp.concatenate([gate_delta, up_delta], axis=1)
            delta_ref[span, :] = deltas
            for a in range(gx):
                act_ref[a, span, :] = act[:, a * part : (a + 1) * part]
                dn_ref[span, a * fan : (a + 1) * fan] = plain_product(deltas, gu_ref[a]).astype(BF16)
            mo_ref[span, :] = sum(
                back_product(act[:, a * part : (a + 1) * part], dt_ref[a]) for a in range(gx)
            ).astype(BF16)
            return carry

        lax.fori_loop(0, rows // step, tokens, 0)
        for a in range(gx):
            gg_ref[a] = weight_product(delta_ref[...], n_ref[:, a * fan : (a + 1) * fan]).astype(BF16)
            dg_ref[a] = weight_product(c_ref[...], act_ref[a]).astype(BF16)

    return pl.pallas_call(
        kernel,
        name="mlp",
        out_shape=(
            jax.ShapeDtypeStruct(normed_all.shape, BF16),
            jax.ShapeDtypeStruct(normed_all.shape, BF16),
            jax.ShapeDtypeStruct(gate_up.shape, BF16),
            jax.ShapeDtypeStruct(down.shape, BF16),
        ),
        in_specs=[VMEM] * 4,
        out_specs=[VMEM] * 4,
        scratch_shapes=[pltpu.VMEM((gx, rows, part), BF16), pltpu.VMEM((rows, both), BF16)],
    )(normed_all, cot_all, gate_up, down)


def share_tokens(sizes, *pieces):
    dp, gx, gy = sizes
    count = len(pieces)

    def kernel(net, *refs):
        srcs, outs, sems = refs[:count], refs[count : 2 * count], refs[2 * count]
        net.greet(net.share_peers())
        items = [Share(net, lambda r, out=out: out.at[r]) for out in outs]
        own = [
            pltpu.make_async_copy(src, out.at[net.d], sems.at[n])
            for n, (src, out) in enumerate(zip(srcs, outs))
        ]
        for item, src in zip(items, srcs):
            item.start(src)
        local(own)
        for item in items:
            item.relay()
        for item in items:
            item.settle()
        wait_local(own)

    shapes = tuple(jax.ShapeDtypeStruct((dp,) + p.shape, p.dtype) for p in pieces)
    return call(
        kernel, sizes, 3, "share_tokens", shapes, [ANY] * count, [VMEM] * count,
        [pltpu.SemaphoreType.DMA((count,))], count * dp, count * (dp // 2 + dp),
    )(*pieces)


def sum_tokens(sizes, *parts):
    dp, gx, gy = sizes
    count = len(parts)
    hops = dp // 2
    shape = parts[0].shape[1:]

    def kernel(net, *refs):
        srcs, outs, scratch = refs[:count], refs[count : 2 * count], refs[2 * count :]
        landing_core, stage, landing_hop = scratch[:count], scratch[count : 2 * count], scratch[2 * count :]
        net.greet(net.share_peers())
        core_slots = [net.block(net.hops) for _ in range(count)]
        hop_slots = [net.block(net.hops) for _ in range(count)]
        order = list(range(1, net.hops)) + [0]
        for n in range(count):
            for i in order:
                hop = net.at_hop(i)
                net.send(
                    srcs[n].at[hop * 2 + 1 - net.core], landing_core[n].at[hop],
                    core_slots[n] + hop, net.core_peer(),
                )
        for n in range(count):
            for i in order:
                hop = net.at_hop(i)
                net.arrive(landing_core[n].at[hop], core_slots[n] + hop)
                total = srcs[n][hop * 2 + net.core].astype(F32) + landing_core[n][hop].astype(F32)
                if i == 0:
                    outs[n][...] = total
                else:
                    stage[n][hop] = total.astype(BF16)
                    net.send(
                        stage[n].at[hop], landing_hop[n].at[net.hop],
                        hop_slots[n] + net.hop, net.hop_peer(i),
                    )
        for n in range(count):
            for i in range(1, net.hops):
                hop = net.at_hop(i)
                net.arrive(landing_hop[n].at[hop], hop_slots[n] + hop)
                outs[n][...] += landing_hop[n][hop].astype(F32)

    shapes = tuple(jax.ShapeDtypeStruct(shape, F32) for _ in parts)
    slab = pltpu.VMEM((hops,) + shape, BF16)
    return call(
        kernel, sizes, 4, "sum_tokens", shapes, [VMEM] * count, [VMEM] * count,
        [slab] * (3 * count), count * dp, count * dp,
    )(*parts)


def sum_plane(sizes, blocks):
    dp, gx, gy = sizes
    shape = blocks.shape[2:]

    def kernel(net, src, out, landing_x, stage, landing_y):
        net.greet(net.plane_peers())
        item = PlaneSum(net, lambda a, b: src.at[a, b], landing_x, stage, landing_y)
        order = far_first(gy) + [0]
        for k in order:
            item.start(k)
        for k in order:
            item.relay(k)
        out[...] = item.total()

    slab = pltpu.VMEM((gy,) + shape, BF16)
    return call(
        kernel, sizes, 5, "sum_plane", jax.ShapeDtypeStruct(shape, F32), VMEM, [VMEM],
        [pltpu.VMEM((gx, gy) + shape, BF16), slab, slab], gx * gy + gy, gx * gy + gy,
    )(blocks)


def trade_tokens(sizes, blocks):
    dp, gx, gy = sizes

    def kernel(net, src, out, sems):
        peers = [net.dp_peer(i) for i in range(1, dp)]
        net.greet(peers)
        slot = net.block(dp)
        for i in range(1, dp):
            rank = lax.rem(net.d + i, dp)
            net.send(src.at[rank], out.at[net.d], slot + net.d, net.dp_peer(i))
        own = pltpu.make_async_copy(src.at[net.d], out.at[net.d], sems.at[0])
        own.start()
        for i in range(1, dp):
            rank = lax.rem(net.d + i, dp)
            net.arrive(out.at[rank], slot + rank)
        own.wait()

    return call(
        kernel, sizes, 6, "trade_tokens", jax.ShapeDtypeStruct(blocks.shape, blocks.dtype), ANY, [VMEM],
        [pltpu.SemaphoreType.DMA((1,))], dp, dp,
    )(blocks)


def reduce_weights(sizes, gate_up, down, att, gains):
    dp, gx, gy = sizes
    halves = gate_up.shape[1]
    pieces = [gate_up.shape[3:]] * halves + [down.shape[2:], att.shape[2:]]
    count = len(pieces)

    def kernel(net, gu_ref, dn_ref, att_ref, gain_ref, *refs):
        gu_out, dn_out, att_out, gain_out = refs[:4]
        refs = refs[4:]
        landing_x, stage, landing_y, result = (refs[n * (count + 1) : (n + 1) * (count + 1)] for n in range(4))
        sems = refs[-1]
        net.greet(net.plane_peers() + net.share_peers())
        sources = [lambda a, b, n=n: gu_ref.at[a, n, b] for n in range(halves)]
        sources += [lambda a, b: dn_ref.at[a, b], lambda a, b: att_ref.at[a, b], lambda a, b: gain_ref]
        outs = [lambda r, n=n: gu_out.at[r, n] for n in range(halves)]
        outs += [lambda r: dn_out.at[r], lambda r: att_out.at[r], lambda r: gain_out.at[r]]
        sums = [
            PlaneSum(net, sources[n], landing_x[n], stage[n], landing_y[n]) for n in range(count + 1)
        ]
        shares = [Share(net, out) for out in outs]
        order = far_first(gy) + [0]
        for k in order:
            for item in sums:
                item.start(k)
        for k in order:
            for item in sums:
                item.relay(k)
        own = []
        for n, (item, share) in enumerate(zip(sums, shares)):
            result[n][...] = item.total().astype(result[n].dtype)
            share.start(result[n])
            own.append(pltpu.make_async_copy(result[n], share.out(net.d), sems.at[n]))
            own[-1].start()
        for share in shares:
            share.relay()
        for share in shares:
            share.settle()
        wait_local(own)

    shapes = (
        jax.ShapeDtypeStruct((dp, halves) + pieces[0], BF16),
        jax.ShapeDtypeStruct((dp,) + pieces[-2], BF16),
        jax.ShapeDtypeStruct((dp,) + pieces[-1], BF16),
        jax.ShapeDtypeStruct((dp,) + gains.shape, F32),
    )
    kinds = [(piece, BF16) for piece in pieces] + [(gains.shape, F32)]
    scratch = [pltpu.VMEM((gx, gy) + p, t) for p, t in kinds]
    scratch += [pltpu.VMEM((gy,) + p, t) for p, t in kinds] * 2
    scratch += [pltpu.VMEM(p, t) for p, t in kinds]
    scratch += [pltpu.SemaphoreType.DMA((count + 1,))]
    return call(
        kernel, sizes, 7, "reduce_weights", shapes, [ANY] * 4, [VMEM] * 4, scratch,
        (count + 1) * (gx * gy + gy + dp), (count + 1) * (gx * gy + gy + dp + dp // 2),
    )(gate_up, down, att, gains)


def rope_angles(positions):
    half_dim = HEAD_WIDTH // 2
    inverse = THETA ** (-(jnp.arange(half_dim, dtype=F32) * 2.0 / HEAD_WIDTH))
    angles = positions[:, None] * inverse[None, :]
    return (jnp.cos(angles)[:, None, :], jnp.sin(angles)[:, None, :])


def rotate(values, cos_table, sin_table):
    item_count = values.shape[0]
    shaped = values.reshape(item_count, -1, HEAD_WIDTH)
    half_dim = HEAD_WIDTH // 2
    front_part = shaped[:, :, :half_dim]
    back_part = shaped[:, :, half_dim:]
    turned = jnp.concatenate(
        [
            front_part * cos_table - back_part * sin_table,
            back_part * cos_table + front_part * sin_table,
        ],
        axis=2,
    )
    return turned.reshape(item_count, -1)


def unrotate(values, cos_table, sin_table):
    return rotate(values, cos_table, -sin_table)


def normalize(values, gain):
    rms_rows = lax.rsqrt(jnp.mean(values * values, axis=1, keepdims=True) + EPSILON)
    unit_rows = values * rms_rows
    return (rms_rows, unit_rows, (unit_rows * gain).astype(BF16))


def normalize_back(dnormed, gain, rms_rows, unit_rows):
    scaled = dnormed * gain
    dvalues = rms_rows * (scaled - unit_rows * jnp.mean(scaled * unit_rows, axis=1, keepdims=True))
    return (dvalues, jnp.sum(dnormed * unit_rows, axis=0))


def on_device(
    sizes,
    inputs,
    segments,
    attn_gain,
    query_weight,
    key_weight,
    value_weight,
    output_weight,
    mlp_gain,
    gate_weight,
    up_weight,
    down_weight,
    cotangent,
):
    dp, gx, gy = sizes
    count_of_rows, width = inputs.shape
    rank = lax.axis_index("dp")
    begin_row = (lax.axis_index("gx") * gy + lax.axis_index("gy")) * count_of_rows
    seq_begin = begin_row // SEQUENCE_LENGTH * SEQUENCE_LENGTH
    local_places = begin_row - seq_begin + jnp.arange(count_of_rows)
    cos_table, sin_table = rope_angles(local_places.astype(F32))
    query_segs = lax.dynamic_slice_in_dim(segments, begin_row, count_of_rows, 0)
    allowed = (jnp.arange(SEQUENCE_LENGTH)[:, None] <= local_places[None, :]) & (
        query_segs[None, :] == segments[:, None]
    )
    bias = jnp.where(allowed, 0.0, MASKED).astype(F32)
    residual = inputs.astype(F32)
    rms_one, unit_one, normed_one = normalize(residual, attn_gain)

    fan = query_weight.shape[0]
    q_cols, k_cols, v_cols = query_weight.shape[1], key_weight.shape[1], value_weight.shape[1]
    o_cols = output_weight.shape[1]
    qkv_cols = q_cols + k_cols + v_cols
    all_cols = qkv_cols + o_cols
    att_share = all_cols // dp
    packed = jnp.concatenate([query_weight, key_weight, value_weight, output_weight], axis=1).T
    att_part = lax.dynamic_slice_in_dim(packed, rank * att_share, att_share, 0)
    share = gate_weight.shape[1] // dp
    groups = gy // gx
    gate_up_part = jnp.stack(
        [
            lax.dynamic_slice_in_dim(gate_weight, rank * share, share, 1).T,
            lax.dynamic_slice_in_dim(up_weight, rank * share, share, 1).T,
        ]
    )
    down_cols = down_weight.shape[1]
    down_part = lax.dynamic_slice_in_dim(
        down_weight.reshape(groups, dp, share, down_cols), rank, 1, 1
    ).reshape(groups * share, down_cols).T

    att_all, gate_up_all, down_all, cot_all, normed_one_all = gather_weights(
        sizes, att_part, gate_up_part, down_part, cotangent, normed_one
    )
    att_all = att_all.reshape(gx, gy, all_cols, fan)
    qkv_rows = att_all[:, :, :qkv_cols].reshape(gx, gy * qkv_cols, fan)
    out_rows = att_all[:, :, qkv_cols:].reshape(gx, gy * o_cols, fan)
    hidden_width = gy * share
    gate_up_all = gate_up_all.reshape(gx, 2 * hidden_width, fan)
    half_hidden = groups * share
    down_all = down_all.reshape(gx, gy * down_cols, half_hidden)
    cot_all = cot_all.reshape(dp * count_of_rows, width)
    normed_one_all = normed_one_all.reshape(dp * count_of_rows, width)

    def parts(rows):
        return [rows[:, a * fan : (a + 1) * fan] for a in range(gx)]

    def onto(rows, weights):
        return sum(back_product(part, weights[a]) for a, part in enumerate(parts(rows)))

    def back_onto(rows, weights):
        return jnp.concatenate([plain_product(rows, weights[a]) for a in range(gx)], axis=1)

    qkv = onto(normed_one, qkv_rows).astype(BF16).reshape(count_of_rows, gy, qkv_cols)
    query_rows = qkv[:, :, :q_cols].reshape(count_of_rows, -1)
    key_rows = qkv[:, :, q_cols : q_cols + k_cols].reshape(count_of_rows, -1)
    value_rows = qkv[:, :, q_cols + k_cols :].reshape(count_of_rows, -1)
    rotated_query = rotate(query_rows.astype(F32), cos_table, sin_table).astype(BF16)
    rotated_key = rotate(key_rows.astype(F32), cos_table, sin_table).astype(BF16)
    kv_width = rotated_key.shape[1]
    kv_all, attention_mixture, logsum = attend(
        sizes, rotated_query, jnp.concatenate([rotated_key, value_rows], axis=1), bias
    )
    attn_out = lax.optimization_barrier(onto(attention_mixture, out_rows).astype(BF16))
    hidden = residual + attn_out.astype(F32)
    rms_two, unit_two, normed_two = normalize(hidden, mlp_gain)

    normed_all, mixed_all = share_tokens(sizes, normed_two, attention_mixture)
    normed_all = normed_all.reshape(dp * count_of_rows, width)
    mixed_all = mixed_all.reshape(dp * count_of_rows, width)
    dnormed_part, mlp_part, gate_up_grad, down_grad = mlp(normed_all, cot_all, gate_up_all, down_all)
    dnormed_two, mlp_out = sum_tokens(
        sizes,
        dnormed_part.reshape(dp, count_of_rows, width),
        mlp_part.reshape(dp, count_of_rows, width),
    )
    layer_out = (hidden + mlp_out).astype(BF16)

    gate_up_grad = gate_up_grad.reshape(gx, 2, gy, share, fan)
    down_grad = down_grad.reshape(gx, gy, down_cols, half_hidden)

    dhidden_norm, mlpgain_part = normalize_back(dnormed_two, mlp_gain, rms_two, unit_two)
    dhidden = cotangent.astype(F32) + dhidden_norm
    dhidden_bf = dhidden.astype(BF16)
    mixture_gradient = back_onto(dhidden_bf, out_rows).astype(BF16)
    dquery_rot, dkv = attend_back(
        rotated_query, kv_all, bias, logsum, attention_mixture, mixture_gradient
    )
    dkv = sum_plane(sizes, dkv)
    dquery = unrotate(dquery_rot, cos_table, sin_table).astype(BF16)
    dkey = unrotate(dkv[:, :kv_width], cos_table, sin_table).astype(BF16)
    dvalue_bf = dkv[:, kv_width:].astype(BF16)
    dqkv = jnp.concatenate(
        [
            dquery.reshape(count_of_rows, gy, q_cols),
            dkey.reshape(count_of_rows, gy, k_cols),
            dvalue_bf.reshape(count_of_rows, gy, v_cols),
        ],
        axis=2,
    )
    dall = jnp.concatenate([dqkv, dhidden_bf.reshape(count_of_rows, gy, o_cols)], axis=2)
    dall = dall.reshape(count_of_rows, gy, dp, att_share).transpose(2, 0, 1, 3)
    dall = trade_tokens(sizes, dall.reshape(dp, count_of_rows, gy * att_share))
    dall = dall.reshape(dp * count_of_rows, gy * att_share)
    places = rank * att_share + lax.broadcasted_iota(jnp.int32, (gy, att_share, 1), 1)
    from_normed = (places < qkv_cols).reshape(gy * att_share, 1)
    att_grad = jnp.stack(
        [
            jnp.where(from_normed, weight_product(dall, one), weight_product(dall, two)).astype(BF16)
            for one, two in zip(parts(normed_one_all), parts(mixed_all))
        ]
    ).reshape(gx, gy, att_share, fan)
    dnormed_one = back_onto(dqkv.reshape(count_of_rows, gy * qkv_cols), qkv_rows)
    dresidual, attgain_part = normalize_back(dnormed_one, attn_gain, rms_one, unit_one)
    input_grad = (dhidden + dresidual).astype(BF16)
    gain_parts = jnp.concatenate([attgain_part, mlpgain_part])
    gain_rows = -(-gain_parts.shape[0] // 1024) * 8
    gain_parts = jnp.pad(gain_parts, (0, gain_rows * 128 - gain_parts.shape[0])).reshape(gain_rows, 128)

    gate_up_sum, down_sum, att_sum, gain_sum = reduce_weights(
        sizes, gate_up_grad, down_grad, att_grad, gain_parts
    )
    gate_grad = gate_up_sum[:, 0].reshape(dp * share, fan).T.astype(F32)
    up_grad = gate_up_sum[:, 1].reshape(dp * share, fan).T.astype(F32)
    down_grad = (
        down_sum.reshape(dp, down_cols, groups, share)
        .transpose(2, 0, 3, 1)
        .reshape(down_weight.shape)
        .astype(F32)
    )
    att_sum = att_sum.reshape(all_cols, fan).T.astype(F32)
    gains = jnp.sum(gain_sum, axis=0).reshape(-1)
    return (
        layer_out,
        input_grad,
        att_sum[:, :q_cols],
        att_sum[:, q_cols : q_cols + k_cols],
        att_sum[:, q_cols + k_cols : qkv_cols],
        att_sum[:, qkv_cols:],
        gate_grad,
        up_grad,
        down_grad,
        gains[:width],
        gains[width : 2 * width],
    )


def solution(mesh):
    sizes = (mesh.shape["dp"], mesh.shape["gx"], mesh.shape["gy"])
    tokens = P(("dp", "gx", "gy"), None)
    block = P("gx", "gy")
    return jax.shard_map(
        functools.partial(on_device, sizes),
        mesh=mesh,
        in_specs=(tokens, P("dp"), P(), block, block, block, block, P(), block, block, block, tokens),
        out_specs=(tokens, tokens) + (block,) * 7 + (P(), P()),
        check_vma=False,
    )
```

```python
import functools

import jax
import jax.numpy as jnp
from jax import lax
from jax.experimental import pallas as pl
from jax.experimental.pallas import tpu as pltpu
from jax.sharding import PartitionSpec as P

QUERY_HEADS = 15
KEY_VALUE_HEADS = 5
GROUPS = QUERY_HEADS // KEY_VALUE_HEADS
HEAD_WIDTH = 64
SEQUENCE_LENGTH = 1024

THETA = 100000.0
EPSILON = 1e-05
MASKED = -1e30

F32 = jnp.float32
BF16 = jnp.bfloat16
MESH = pl.DeviceIdType.MESH
ANY = pl.BlockSpec(memory_space=pl.ANY)
VMEM = pl.BlockSpec(memory_space=pltpu.VMEM)


def plain_product(left, right):
    return jnp.dot(left, right, preferred_element_type=F32)


def weight_product(left, right):
    return lax.dot_general(left, right, (((0,), (0,)), ((), ())), preferred_element_type=F32)


def back_product(left, right):
    return lax.dot_general(left, right, (((1,), (1,)), ((), ())), preferred_element_type=F32)


class Net:
    def __init__(self, sizes, send_sems, recv_sems):
        self.dp, self.gx, self.gy = sizes
        self.cores = 2 if self.dp % 2 == 0 else 1
        self.hops = self.dp // self.cores
        self.d = lax.axis_index("dp")
        self.x = lax.axis_index("gx")
        self.y = lax.axis_index("gy")
        self.core = lax.rem(self.d, self.cores)
        self.hop = self.d // self.cores
        self.send_sems, self.recv_sems = send_sems, recv_sems
        self.sent, self.slots, self.pending = 0, 0, []

    def at_gx(self, j):
        return lax.rem(self.x + j, self.gx)

    def at_gy(self, k):
        return lax.rem(self.y + k, self.gy)

    def at_hop(self, i):
        return lax.rem(self.hop + i, self.hops)

    def gx_peer(self, j):
        return {"gx": self.at_gx(j)}

    def gy_peer(self, k):
        return {"gy": self.at_gy(k)}

    def hop_peer(self, i):
        return {"dp": self.at_hop(i) * self.cores + self.core}

    def core_peer(self):
        return {"dp": self.hop * self.cores + 1 - self.core}

    def dp_peer(self, i):
        return {"dp": lax.rem(self.d + i, self.dp)}

    def plane_peers(self):
        return [self.gx_peer(j) for j in range(1, self.gx)] + [
            self.gy_peer(k) for k in range(1, self.gy)
        ]

    def share_peers(self):
        peers = [self.hop_peer(i) for i in range(1, self.hops)]
        return peers + ([self.core_peer()] if self.cores == 2 else [])

    def greet(self, peers):
        barrier = pltpu.get_barrier_semaphore()
        for peer in peers:
            pl.semaphore_signal(barrier, inc=1, device_id=peer, device_id_type=MESH)
        pl.semaphore_wait(barrier, len(peers))

    def block(self, count):
        first = self.slots
        self.slots += count
        return first

    def copy(self, src, dst, slot, peer):
        return pltpu.make_async_remote_copy(
            src_ref=src,
            dst_ref=dst,
            send_sem=self.send_sems.at[self.sent],
            recv_sem=self.recv_sems.at[slot],
            device_id=peer,
            device_id_type=MESH,
        )

    def send(self, src, dst, slot, peer):
        copy = self.copy(src, dst, slot, peer)
        copy.start()
        self.sent += 1
        self.pending.append(copy)

    def arrive(self, dst, slot):
        pltpu.make_async_remote_copy(
            src_ref=dst,
            dst_ref=dst,
            send_sem=self.send_sems.at[0],
            recv_sem=self.recv_sems.at[slot],
            device_id=self.gy_peer(1),
            device_id_type=MESH,
        ).wait_recv()

    def drain(self):
        for copy in self.pending:
            copy.wait_send()


def far_first(count):
    order = list(range(1, count))
    return sorted(order, key=lambda k: -min(k, count - k))


class PlaneGather:
    def __init__(self, net, src, out):
        self.net, self.src, self.out = net, src, out
        self.gy_slot = net.block(net.gy)
        self.gx_slot = net.block(net.gx * net.gy)

    def start(self):
        self.start_gy()
        self.start_gx()

    def start_gy(self):
        net = self.net
        own = self.out(net.x, net.y)
        for k in range(1, net.gy):
            net.send(self.src, own, self.gy_slot + net.y, net.gy_peer(k))

    def start_gx(self):
        net = self.net
        own = self.out(net.x, net.y)
        for j in range(1, net.gx):
            net.send(self.src, own, self.gx_slot + net.x * net.gy + net.y, net.gx_peer(j))

    def relay(self, k):
        net = self.net
        row = net.at_gy(k)
        piece = self.out(net.x, row)
        net.arrive(piece, self.gy_slot + row)
        for j in range(1, net.gx):
            net.send(piece, piece, self.gx_slot + net.x * net.gy + row, net.gx_peer(j))

    def settle(self, j, k):
        net = self.net
        side, row = net.at_gx(j), net.at_gy(k)
        net.arrive(self.out(side, row), self.gx_slot + side * net.gy + row)


class Share:
    def __init__(self, net, out):
        self.net, self.out = net, out
        self.hop_slot = net.block(net.hops)
        self.core_slot = net.block(net.dp)

    def start(self, src):
        net = self.net
        own = self.out(net.d)
        for i in range(1, net.hops):
            net.send(src, own, self.hop_slot + net.hop, net.hop_peer(i))
        if net.cores == 2:
            net.send(src, own, self.core_slot + net.d, net.core_peer())

    def relay(self):
        net = self.net
        for i in range(1, net.hops):
            hop = net.at_hop(i)
            rank = hop * net.cores + net.core
            piece = self.out(rank)
            net.arrive(piece, self.hop_slot + hop)
            if net.cores == 2:
                net.send(piece, piece, self.core_slot + rank, net.core_peer())

    def settle(self):
        net = self.net
        if net.cores == 2:
            for hop in range(net.hops):
                rank = hop * net.cores + 1 - net.core
                net.arrive(self.out(rank), self.core_slot + rank)


class PlaneSum:
    def __init__(self, net, src, landing_x, stage, landing_y):
        self.net, self.src = net, src
        self.landing_x, self.stage, self.landing_y = landing_x, stage, landing_y
        self.gx_slot = net.block(net.gx * net.gy)
        self.gy_slot = net.block(net.gy)

    def start(self, k):
        net = self.net
        row = net.at_gy(k)
        for j in range(1, net.gx):
            net.send(
                self.src(net.at_gx(j), row),
                self.landing_x.at[net.x, row],
                self.gx_slot + net.x * net.gy + row,
                net.gx_peer(j),
            )

    def relay(self, k):
        net = self.net
        row = net.at_gy(k)
        total = self.src(net.x, row)[...].astype(F32)
        for j in range(1, net.gx):
            side = net.at_gx(j)
            net.arrive(self.landing_x.at[side, row], self.gx_slot + side * net.gy + row)
            total = total + self.landing_x[side, row].astype(F32)
        if k == 0:
            self.landing_y[net.y] = total.astype(self.landing_y.dtype)
        else:
            self.stage[row] = total.astype(self.stage.dtype)
            net.send(
                self.stage.at[row], self.landing_y.at[net.y], self.gy_slot + net.y, net.gy_peer(k)
            )

    def total(self):
        net = self.net
        for k in range(1, net.gy):
            row = net.at_gy(k)
            net.arrive(self.landing_y.at[row], self.gy_slot + row)
        total = self.landing_y[0].astype(F32)
        for row in range(1, net.gy):
            total = total + self.landing_y[row].astype(F32)
        return total


def call(kernel, sizes, number, name, out_shapes, out_specs, in_specs, scratch, sends, slots):
    def body(*refs):
        net = Net(sizes, refs[-2], refs[-1])
        kernel(net, *refs[:-2])
        net.drain()
        assert net.sent <= sends and net.slots <= slots, (net.sent, net.slots)

    return pl.pallas_call(
        body,
        name=name,
        out_shape=out_shapes,
        in_specs=in_specs,
        out_specs=out_specs,
        scratch_shapes=list(scratch)
        + [pltpu.SemaphoreType.DMA((sends,)), pltpu.SemaphoreType.DMA((slots,))],
        compiler_params=pltpu.CompilerParams(collective_id=number, has_side_effects=True),
    )


def local(copies):
    for copy in copies:
        copy.start()


def wait_local(copies):
    for copy in copies:
        copy.wait()


def gather_weights(sizes, att):
    dp, gx, gy = sizes
    hops = dp // 2

    def kernel(net, att_ref, att_out, sems):
        net.greet(net.plane_peers() + net.share_peers())
        att_plane = PlaneGather(net, att_ref, lambda a, b: att_out.at[a, b, net.d])
        first_hop = net.block(gx * gy * net.hops)
        first_core = net.block(gx * gy * net.dp)

        def shared(a, b):
            item = Share.__new__(Share)
            item.net = net
            item.out = lambda rank: att_out.at[a, b, rank]
            place = a * gy + b
            item.hop_slot = first_hop + place * net.hops
            item.core_slot = first_core + place * net.dp
            return item

        own = [pltpu.make_async_copy(att_ref, att_out.at[net.x, net.y, net.d], sems.at[0])]
        att_plane.start()
        shared(net.x, net.y).start(att_ref)
        local(own)
        for k in range(1, gy):
            att_plane.relay(k)
            row = net.at_gy(k)
            shared(net.x, row).start(att_out.at[net.x, row, net.d])
        for j in range(1, gx):
            for k in range(gy):
                att_plane.settle(j, k)
                side, row = net.at_gx(j), net.at_gy(k)
                shared(side, row).start(att_out.at[side, row, net.d])
        places = [(j, k) for j in range(gx) for k in range(gy)]
        for j, k in places:
            shared(net.at_gx(j), net.at_gy(k)).relay()
        for j, k in places:
            shared(net.at_gx(j), net.at_gy(k)).settle()
        wait_local(own)

    shape = jax.ShapeDtypeStruct((gx, gy, dp) + att.shape, BF16)
    return call(
        kernel, sizes, 1, "gather_weights", shape, ANY, [VMEM], [pltpu.SemaphoreType.DMA((1,))],
        gx * gy * (hops + dp) + gx * gy + gy, gx * gy * (hops + dp) + gy + gx * gy,
    )(att)


def turned(values):
    return jnp.transpose(values)


def head_rows(ref, first, lead=()):
    return jnp.concatenate(
        [ref[:, h * HEAD_WIDTH : (h + 1) * HEAD_WIDTH] for h in range(first, first + GROUPS)], axis=0
    )


def key_columns(ref, place):
    columns = ref[:, :, :, place * HEAD_WIDTH : (place + 1) * HEAD_WIDTH]
    return columns.reshape(-1, HEAD_WIDTH)


def put_heads(ref, first, rows, values):
    for n in range(GROUPS):
        lanes = slice((first + n) * HEAD_WIDTH, (first + n + 1) * HEAD_WIDTH)
        ref[:, lanes] = values[n * rows : (n + 1) * rows].astype(ref.dtype)


def attend_heads(key_heads, q_ref, kv_ref, bias_ref, mixed_ref, logsum_ref):
    rows = q_ref.shape[0]
    bias = jnp.concatenate([bias_ref[...]] * GROUPS, axis=1)
    for k in key_heads:
        query = head_rows(q_ref, k * GROUPS)
        scores = back_product(key_columns(kv_ref, k), query) * HEAD_WIDTH ** (-0.5) + bias
        highest = jnp.max(scores, axis=0, keepdims=True)
        weights = jnp.exp(scores - highest)
        sums = jnp.sum(weights, axis=0, keepdims=True)
        logsum_ref[k : k + 1, :] = highest + jnp.log(sums)
        probs = (weights * (1.0 / sums)).astype(BF16)
        mixed = weight_product(key_columns(kv_ref, KEY_VALUE_HEADS + k), probs)
        put_heads(mixed_ref, k * GROUPS, rows, turned(mixed))


def attend_heads_back(q_ref, kv_ref, bias_ref, logsum_ref, mixed_ref, dmixed_ref, dq_ref, dkv_ref):
    rows = q_ref.shape[0]
    bias = jnp.concatenate([bias_ref[...]] * GROUPS, axis=1)
    blocks = kv_ref.shape[:3]
    for k in range(KEY_VALUE_HEADS):
        query = head_rows(q_ref, k * GROUPS)
        mixed = head_rows(mixed_ref, k * GROUPS)
        dmixed = head_rows(dmixed_ref, k * GROUPS)
        keys = key_columns(kv_ref, k)
        scores = back_product(keys, query) * HEAD_WIDTH ** (-0.5) + bias
        weights = jnp.exp(scores - logsum_ref[k : k + 1, :])
        delta = jnp.sum(turned(mixed.astype(F32) * dmixed.astype(F32)), axis=0, keepdims=True)
        dprobs = back_product(key_columns(kv_ref, KEY_VALUE_HEADS + k), dmixed)
        dscores = (weights * (dprobs - delta)).astype(BF16)
        dquery = weight_product(keys, dscores) * HEAD_WIDTH ** (-0.5)
        put_heads(dq_ref, k * GROUPS, rows, turned(dquery))
        dkeys = plain_product(dscores, query) * HEAD_WIDTH ** (-0.5)
        dvalues = plain_product(weights.astype(BF16), dmixed)
        lanes = slice(k * HEAD_WIDTH, (k + 1) * HEAD_WIDTH)
        dkv_ref[:, :, :, lanes] = dkeys.astype(BF16).reshape(blocks + (HEAD_WIDTH,))
        place = KEY_VALUE_HEADS + k
        lanes = slice(place * HEAD_WIDTH, (place + 1) * HEAD_WIDTH)
        dkv_ref[:, :, :, lanes] = dvalues.astype(BF16).reshape(blocks + (HEAD_WIDTH,))


def turn_pairs(values, cos, sin):
    lanes = cos.shape[1]
    half = HEAD_WIDTH // 2
    front = lax.broadcasted_iota(jnp.int32, cos.shape, 1) % HEAD_WIDTH < half
    pieces = []
    for first in range(0, values.shape[1], lanes):
        part = values[:, first : first + lanes]
        other = jnp.where(front, pltpu.roll(part, lanes - half, 1), pltpu.roll(part, half, 1))
        pieces.append(part * cos + other * sin)
    return jnp.concatenate(pieces, axis=1)


def forward(sizes, cols, att, normed, inputs, gain, cos, sin, bias, gate_up, down, cot):
    dp, gx, gy = sizes
    q_cols, k_cols, v_cols, o_cols = cols
    qkv_cols = q_cols + k_cols + v_cols
    rows, width = inputs.shape
    fan = att.shape[3]
    lanes = cos.shape[1]
    q_width, k_width, v_width = gy * q_cols, gy * k_cols, gy * v_cols
    q_pad, k_pad = -(-q_width // lanes) * lanes, -(-k_width // lanes) * lanes

    def kernel(
        net, att_ref, nm_ref, in_ref, gain_ref, cos_ref, sin_ref, bias_ref, gu_ref, dn_ref, cot_ref,
        q_ref, kv_out, mixed_ref, logsum_ref, hidden_ref,
        gu_out, dn_out, cot_out, nm_out, mixed_out, two_out,
        q_wide, k_wide, kv_ref, two_ref, sems,
    ):
        q_wide[...] = jnp.zeros_like(q_wide)
        k_wide[...] = jnp.zeros_like(k_wide)
        for b in range(gy):
            block = sum(
                back_product(nm_ref[:, a * fan : (a + 1) * fan], att_ref[a, b, :qkv_cols, :])
                for a in range(gx)
            ).astype(BF16)
            q_wide[:, b * q_cols : (b + 1) * q_cols] = block[:, :q_cols].astype(F32)
            k_wide[:, b * k_cols : (b + 1) * k_cols] = block[:, q_cols : q_cols + k_cols].astype(F32)
            first = k_width + b * v_cols
            kv_ref[:, first : first + v_cols] = block[:, q_cols + k_cols :]
        cos_rows, sin_rows = cos_ref[...], sin_ref[...]
        kv_ref[:, :k_width] = turn_pairs(k_wide[...], cos_rows, sin_rows)[:, :k_width].astype(BF16)

        net.greet(net.plane_peers() + net.share_peers())
        kv = PlaneGather(net, kv_ref, lambda a, b: kv_out.at[a, b])
        gu = PlaneGather(net, gu_ref, lambda a, b: gu_out.at[a, :, b])
        dn = PlaneGather(net, dn_ref, lambda a, b: dn_out.at[a, b])
        cot_share, nm_share, mixed_share, two_share = (
            Share(net, lambda r, out=out: out.at[r]) for out in (cot_out, nm_out, mixed_out, two_out)
        )
        own = [
            pltpu.make_async_copy(kv_ref, kv_out.at[net.x, net.y], sems.at[0]),
            pltpu.make_async_copy(gu_ref, gu_out.at[net.x, :, net.y], sems.at[1]),
            pltpu.make_async_copy(dn_ref, dn_out.at[net.x, net.y], sems.at[2]),
            pltpu.make_async_copy(cot_ref, cot_out.at[net.d], sems.at[3]),
            pltpu.make_async_copy(nm_ref, nm_out.at[net.d], sems.at[4]),
        ]
        kv.start()
        gu.start_gy()
        dn.start_gy()
        local(own)
        cot_share.start(cot_ref)
        nm_share.start(nm_ref)
        q_ref[...] = turn_pairs(q_wide[...], cos_rows, sin_rows)[:, :q_width].astype(BF16)
        for k in range(1, gy):
            kv.relay(k)
        gu.start_gx()
        dn.start_gx()
        for j in range(1, gx):
            for k in range(gy):
                kv.settle(j, k)
        wait_local(own)

        turns = list(range(1, gy))
        heads = list(range(KEY_VALUE_HEADS))
        for n, k in enumerate(turns):
            mine = heads[n * len(heads) // len(turns) : (n + 1) * len(heads) // len(turns)]
            attend_heads(mine, q_ref, kv_out, bias_ref, mixed_ref, logsum_ref)
            if n + 1 < len(turns):
                gu.relay(k)
                dn.relay(k)
        last = pltpu.make_async_copy(mixed_ref, mixed_out.at[net.d], sems.at[5])
        last.start()
        mixed_share.start(mixed_ref)
        for b in range(gy):
            block = sum(
                back_product(mixed_ref[:, a * fan : (a + 1) * fan], att_ref[a, b, qkv_cols:, :])
                for a in range(gx)
            ).astype(BF16)
            span = slice(b * o_cols, (b + 1) * o_cols)
            hidden_ref[:, span] = in_ref[:, span].astype(F32) + block.astype(F32)
        hidden = hidden_ref[...]
        scale = lax.rsqrt(jnp.sum(hidden * hidden, axis=1, keepdims=True) / width + EPSILON)
        two_ref[...] = (hidden * scale * gain_ref[...]).astype(BF16)
        local_two = pltpu.make_async_copy(two_ref, two_out.at[net.d], sems.at[6])
        local_two.start()
        two_share.start(two_ref)
        gu.relay(turns[-1])
        dn.relay(turns[-1])
        shares = (cot_share, nm_share, mixed_share, two_share)
        for share in shares:
            share.relay()
        for share in shares:
            share.settle()
        for j in range(1, gx):
            for k in range(gy):
                gu.settle(j, k)
                dn.settle(j, k)
        wait_local([last, local_two])

    shared = jax.ShapeDtypeStruct((dp,) + inputs.shape, BF16)
    shapes = (
        jax.ShapeDtypeStruct((rows, q_width), BF16),
        jax.ShapeDtypeStruct((gx, gy, rows, k_width + v_width), BF16),
        jax.ShapeDtypeStruct((rows, q_width), BF16),
        jax.ShapeDtypeStruct((KEY_VALUE_HEADS, GROUPS * rows), F32),
        jax.ShapeDtypeStruct(inputs.shape, F32),
        jax.ShapeDtypeStruct((gx, 2, gy) + gate_up.shape[1:], BF16),
        jax.ShapeDtypeStruct((gx, gy) + down.shape, BF16),
        shared, shared, shared, shared,
    )
    scratch = [
        pltpu.VMEM((rows, q_pad), F32),
        pltpu.VMEM((rows, k_pad), F32),
        pltpu.VMEM((rows, k_width + v_width), BF16),
        pltpu.VMEM(inputs.shape, BF16),
        pltpu.SemaphoreType.DMA((7,)),
    ]
    count = 3 * (gx * gy + gy) + 4 * 2 * dp
    return call(
        kernel, sizes, 2, "forward", shapes, [VMEM] * 5 + [ANY] * 6, [VMEM] * 10, scratch, count, count,
    )(att, normed, inputs, gain, cos, sin, bias, gate_up, down, cot)


def attend_back(query, kv_all, bias, logsum, mixed, dmixed):
    return pl.pallas_call(
        attend_heads_back,
        name="attend_back",
        out_shape=(
            jax.ShapeDtypeStruct(query.shape, F32),
            jax.ShapeDtypeStruct(kv_all.shape, BF16),
        ),
        in_specs=[VMEM] * 6,
        out_specs=[VMEM] * 2,
    )(query, kv_all, bias, logsum, mixed, dmixed)


def mlp(normed_all, cot_all, gate_up, down):
    gx, both, fan = gate_up.shape
    rows, width = normed_all.shape
    hidden = both // 2
    part = down.shape[2]
    step = rows // 2 if rows % 32 == 0 else rows

    def kernel(n_ref, c_ref, gu_ref, dt_ref, dn_ref, mo_ref, gg_ref, dg_ref, act_ref, delta_ref):
        def tokens(i, carry):
            span = pl.ds(pl.multiple_of(i * step, step), step)
            normed, cot = n_ref[span, :], c_ref[span, :]
            gate_up_rows = sum(
                back_product(normed[:, a * fan : (a + 1) * fan], gu_ref[a]) for a in range(gx)
            ).astype(BF16)
            gate = gate_up_rows[:, :hidden].astype(F32)
            up = gate_up_rows[:, hidden:].astype(F32)
            dact = jnp.concatenate([plain_product(cot, dt_ref[a]) for a in range(gx)], axis=1)
            sigmoid = jax.nn.sigmoid(gate)
            act = (gate * sigmoid * up).astype(BF16)
            gate_delta = (dact * up * sigmoid * (1.0 + gate * (1.0 - sigmoid))).astype(BF16)
            up_delta = (dact * gate * sigmoid).astype(BF16)
            deltas = jnp.concatenate([gate_delta, up_delta], axis=1)
            delta_ref[span, :] = deltas
            for a in range(gx):
                act_ref[a, span, :] = act[:, a * part : (a + 1) * part]
                dn_ref[span, a * fan : (a + 1) * fan] = plain_product(deltas, gu_ref[a]).astype(BF16)
            mo_ref[span, :] = sum(
                back_product(act[:, a * part : (a + 1) * part], dt_ref[a]) for a in range(gx)
            ).astype(BF16)
            return carry

        lax.fori_loop(0, rows // step, tokens, 0)
        for a in range(gx):
            gg_ref[a] = weight_product(delta_ref[...], n_ref[:, a * fan : (a + 1) * fan]).astype(BF16)
            dg_ref[a] = weight_product(c_ref[...], act_ref[a]).astype(BF16)

    return pl.pallas_call(
        kernel,
        name="mlp",
        out_shape=(
            jax.ShapeDtypeStruct(normed_all.shape, BF16),
            jax.ShapeDtypeStruct(normed_all.shape, BF16),
            jax.ShapeDtypeStruct(gate_up.shape, BF16),
            jax.ShapeDtypeStruct(down.shape, BF16),
        ),
        in_specs=[VMEM] * 4,
        out_specs=[VMEM] * 4,
        scratch_shapes=[pltpu.VMEM((gx, rows, part), BF16), pltpu.VMEM((rows, both), BF16)],
    )(normed_all, cot_all, gate_up, down)


def sum_tokens(sizes, *parts):
    dp, gx, gy = sizes
    count = len(parts)
    hops = dp // 2
    shape = parts[0].shape[1:]

    def kernel(net, *refs):
        srcs, outs, scratch = refs[:count], refs[count : 2 * count], refs[2 * count :]
        landing_core, stage, landing_hop = scratch[:count], scratch[count : 2 * count], scratch[2 * count :]
        net.greet(net.share_peers())
        core_slots = [net.block(net.hops) for _ in range(count)]
        hop_slots = [net.block(net.hops) for _ in range(count)]
        order = list(range(1, net.hops)) + [0]
        for n in range(count):
            for i in order:
                hop = net.at_hop(i)
                net.send(
                    srcs[n].at[hop * 2 + 1 - net.core], landing_core[n].at[hop],
                    core_slots[n] + hop, net.core_peer(),
                )
        for n in range(count):
            for i in order:
                hop = net.at_hop(i)
                net.arrive(landing_core[n].at[hop], core_slots[n] + hop)
                total = srcs[n][hop * 2 + net.core].astype(F32) + landing_core[n][hop].astype(F32)
                if i == 0:
                    outs[n][...] = total
                else:
                    stage[n][hop] = total.astype(BF16)
                    net.send(
                        stage[n].at[hop], landing_hop[n].at[net.hop],
                        hop_slots[n] + net.hop, net.hop_peer(i),
                    )
        for n in range(count):
            for i in range(1, net.hops):
                hop = net.at_hop(i)
                net.arrive(landing_hop[n].at[hop], hop_slots[n] + hop)
                outs[n][...] += landing_hop[n][hop].astype(F32)

    shapes = tuple(jax.ShapeDtypeStruct(shape, F32) for _ in parts)
    slab = pltpu.VMEM((hops,) + shape, BF16)
    return call(
        kernel, sizes, 4, "sum_tokens", shapes, [VMEM] * count, [VMEM] * count,
        [slab] * (3 * count), count * dp, count * dp,
    )(*parts)


def sum_plane(sizes, blocks):
    dp, gx, gy = sizes
    shape = blocks.shape[2:]

    def kernel(net, src, out, landing_x, stage, landing_y):
        net.greet(net.plane_peers())
        item = PlaneSum(net, lambda a, b: src.at[a, b], landing_x, stage, landing_y)
        order = far_first(gy) + [0]
        for k in order:
            item.start(k)
        for k in order:
            item.relay(k)
        out[...] = item.total()

    slab = pltpu.VMEM((gy,) + shape, BF16)
    return call(
        kernel, sizes, 5, "sum_plane", jax.ShapeDtypeStruct(shape, F32), VMEM, [VMEM],
        [pltpu.VMEM((gx, gy) + shape, BF16), slab, slab], gx * gy + gy, gx * gy + gy,
    )(blocks)


def trade_tokens(sizes, blocks):
    dp, gx, gy = sizes

    def kernel(net, src, out, sems):
        peers = [net.dp_peer(i) for i in range(1, dp)]
        net.greet(peers)
        slot = net.block(dp)
        for i in range(1, dp):
            rank = lax.rem(net.d + i, dp)
            net.send(src.at[rank], out.at[net.d], slot + net.d, net.dp_peer(i))
        own = pltpu.make_async_copy(src.at[net.d], out.at[net.d], sems.at[0])
        own.start()
        for i in range(1, dp):
            rank = lax.rem(net.d + i, dp)
            net.arrive(out.at[rank], slot + rank)
        own.wait()

    return call(
        kernel, sizes, 6, "trade_tokens", jax.ShapeDtypeStruct(blocks.shape, blocks.dtype), ANY, [VMEM],
        [pltpu.SemaphoreType.DMA((1,))], dp, dp,
    )(blocks)


def reduce_weights(sizes, gate_up, down, att, gains):
    dp, gx, gy = sizes
    halves = gate_up.shape[1]
    pieces = [gate_up.shape[3:]] * halves + [down.shape[2:], att.shape[2:]]
    count = len(pieces)

    def kernel(net, gu_ref, dn_ref, att_ref, gain_ref, *refs):
        gu_out, dn_out, att_out, gain_out = refs[:4]
        refs = refs[4:]
        landing_x, stage, landing_y, result = (refs[n * (count + 1) : (n + 1) * (count + 1)] for n in range(4))
        sems = refs[-1]
        net.greet(net.plane_peers() + net.share_peers())
        sources = [lambda a, b, n=n: gu_ref.at[a, n, b] for n in range(halves)]
        sources += [lambda a, b: dn_ref.at[a, b], lambda a, b: att_ref.at[a, b], lambda a, b: gain_ref]
        outs = [lambda r, n=n: gu_out.at[r, n] for n in range(halves)]
        outs += [lambda r: dn_out.at[r], lambda r: att_out.at[r], lambda r: gain_out.at[r]]
        sums = [
            PlaneSum(net, sources[n], landing_x[n], stage[n], landing_y[n]) for n in range(count + 1)
        ]
        shares = [Share(net, out) for out in outs]
        order = far_first(gy) + [0]
        for k in order:
            for item in sums:
                item.start(k)
        for k in order:
            for item in sums:
                item.relay(k)
        own = []
        for n, (item, share) in enumerate(zip(sums, shares)):
            result[n][...] = item.total().astype(result[n].dtype)
            share.start(result[n])
            own.append(pltpu.make_async_copy(result[n], share.out(net.d), sems.at[n]))
            own[-1].start()
        for share in shares:
            share.relay()
        for share in shares:
            share.settle()
        wait_local(own)

    shapes = (
        jax.ShapeDtypeStruct((dp, halves) + pieces[0], BF16),
        jax.ShapeDtypeStruct((dp,) + pieces[-2], BF16),
        jax.ShapeDtypeStruct((dp,) + pieces[-1], BF16),
        jax.ShapeDtypeStruct((dp,) + gains.shape, F32),
    )
    kinds = [(piece, BF16) for piece in pieces] + [(gains.shape, F32)]
    scratch = [pltpu.VMEM((gx, gy) + p, t) for p, t in kinds]
    scratch += [pltpu.VMEM((gy,) + p, t) for p, t in kinds] * 2
    scratch += [pltpu.VMEM(p, t) for p, t in kinds]
    scratch += [pltpu.SemaphoreType.DMA((count + 1,))]
    return call(
        kernel, sizes, 7, "reduce_weights", shapes, [ANY] * 4, [VMEM] * 4, scratch,
        (count + 1) * (gx * gy + gy + dp), (count + 1) * (gx * gy + gy + dp + dp // 2),
    )(gate_up, down, att, gains)


def rope_angles(positions):
    half_dim = HEAD_WIDTH // 2
    inverse = THETA ** (-(jnp.arange(half_dim, dtype=F32) * 2.0 / HEAD_WIDTH))
    angles = positions[:, None] * inverse[None, :]
    return (jnp.cos(angles)[:, None, :], jnp.sin(angles)[:, None, :])


def rotate(values, cos_table, sin_table):
    item_count = values.shape[0]
    shaped = values.reshape(item_count, -1, HEAD_WIDTH)
    half_dim = HEAD_WIDTH // 2
    front_part = shaped[:, :, :half_dim]
    back_part = shaped[:, :, half_dim:]
    turned = jnp.concatenate(
        [
            front_part * cos_table - back_part * sin_table,
            back_part * cos_table + front_part * sin_table,
        ],
        axis=2,
    )
    return turned.reshape(item_count, -1)


def unrotate(values, cos_table, sin_table):
    return rotate(values, cos_table, -sin_table)


def normalize(values, gain):
    rms_rows = lax.rsqrt(jnp.mean(values * values, axis=1, keepdims=True) + EPSILON)
    unit_rows = values * rms_rows
    return (rms_rows, unit_rows, (unit_rows * gain).astype(BF16))


def normalize_back(dnormed, gain, rms_rows, unit_rows):
    scaled = dnormed * gain
    dvalues = rms_rows * (scaled - unit_rows * jnp.mean(scaled * unit_rows, axis=1, keepdims=True))
    return (dvalues, jnp.sum(dnormed * unit_rows, axis=0))


def on_device(
    sizes,
    inputs,
    segments,
    attn_gain,
    query_weight,
    key_weight,
    value_weight,
    output_weight,
    mlp_gain,
    gate_weight,
    up_weight,
    down_weight,
    cotangent,
):
    dp, gx, gy = sizes
    count_of_rows, width = inputs.shape
    rank = lax.axis_index("dp")
    begin_row = (lax.axis_index("gx") * gy + lax.axis_index("gy")) * count_of_rows
    seq_begin = begin_row // SEQUENCE_LENGTH * SEQUENCE_LENGTH
    local_places = begin_row - seq_begin + jnp.arange(count_of_rows)
    cos_table, sin_table = rope_angles(local_places.astype(F32))
    query_segs = lax.dynamic_slice_in_dim(segments, begin_row, count_of_rows, 0)
    allowed = (jnp.arange(SEQUENCE_LENGTH)[:, None] <= local_places[None, :]) & (
        query_segs[None, :] == segments[:, None]
    )
    bias = jnp.where(allowed, 0.0, MASKED).astype(F32)
    residual = inputs.astype(F32)
    rms_one, unit_one, normed_one = normalize(residual, attn_gain)

    fan = query_weight.shape[0]
    q_cols, k_cols, v_cols = query_weight.shape[1], key_weight.shape[1], value_weight.shape[1]
    o_cols = output_weight.shape[1]
    qkv_cols = q_cols + k_cols + v_cols
    all_cols = qkv_cols + o_cols
    att_share = all_cols // dp
    packed = jnp.concatenate([query_weight, key_weight, value_weight, output_weight], axis=1).T
    att_part = lax.dynamic_slice_in_dim(packed, rank * att_share, att_share, 0)
    share = gate_weight.shape[1] // dp
    groups = gy // gx
    gate_up_part = jnp.stack(
        [
            lax.dynamic_slice_in_dim(gate_weight, rank * share, share, 1).T,
            lax.dynamic_slice_in_dim(up_weight, rank * share, share, 1).T,
        ]
    )
    down_cols = down_weight.shape[1]
    down_part = lax.dynamic_slice_in_dim(
        down_weight.reshape(groups, dp, share, down_cols), rank, 1, 1
    ).reshape(groups * share, down_cols).T

    att_all = gather_weights(sizes, att_part).reshape(gx, gy, all_cols, fan)
    cos_wide = jnp.tile(cos_table[:, 0], (1, 4))
    sin_wide = jnp.tile(jnp.concatenate([-sin_table[:, 0], sin_table[:, 0]], axis=1), (1, 2))
    (
        rotated_query, kv_all, attention_mixture, logsum, hidden,
        gate_up_all, down_all, cot_all, normed_one_all, mixed_all, normed_all,
    ) = forward(
        sizes, (q_cols, k_cols, v_cols, o_cols), att_all, normed_one, inputs, mlp_gain.reshape(1, -1),
        cos_wide, sin_wide, bias, gate_up_part, down_part, cotangent,
    )
    kv_width = gy * k_cols
    qkv_rows = att_all[:, :, :qkv_cols].reshape(gx, gy * qkv_cols, fan)
    out_rows = att_all[:, :, qkv_cols:].reshape(gx, gy * o_cols, fan)
    hidden_width = gy * share
    gate_up_all = gate_up_all.reshape(gx, 2 * hidden_width, fan)
    half_hidden = groups * share
    down_all = down_all.reshape(gx, gy * down_cols, half_hidden)
    cot_all, normed_one_all, mixed_all, normed_all = (
        rows.reshape(dp * count_of_rows, width) for rows in (cot_all, normed_one_all, mixed_all, normed_all)
    )
    rms_two, unit_two, _ = normalize(hidden, mlp_gain)

    def parts(rows):
        return [rows[:, a * fan : (a + 1) * fan] for a in range(gx)]

    def back_onto(rows, weights):
        return jnp.concatenate([plain_product(rows, weights[a]) for a in range(gx)], axis=1)

    dnormed_part, mlp_part, gate_up_grad, down_grad = mlp(normed_all, cot_all, gate_up_all, down_all)
    dnormed_two, mlp_out = sum_tokens(
        sizes,
        dnormed_part.reshape(dp, count_of_rows, width),
        mlp_part.reshape(dp, count_of_rows, width),
    )
    layer_out = (hidden + mlp_out).astype(BF16)

    gate_up_grad = gate_up_grad.reshape(gx, 2, gy, share, fan)
    down_grad = down_grad.reshape(gx, gy, down_cols, half_hidden)

    dhidden_norm, mlpgain_part = normalize_back(dnormed_two, mlp_gain, rms_two, unit_two)
    dhidden = cotangent.astype(F32) + dhidden_norm
    dhidden_bf = dhidden.astype(BF16)
    mixture_gradient = back_onto(dhidden_bf, out_rows).astype(BF16)
    dquery_rot, dkv = attend_back(
        rotated_query, kv_all, bias, logsum, attention_mixture, mixture_gradient
    )
    dkv = sum_plane(sizes, dkv)
    dquery = unrotate(dquery_rot, cos_table, sin_table).astype(BF16)
    dkey = unrotate(dkv[:, :kv_width], cos_table, sin_table).astype(BF16)
    dvalue_bf = dkv[:, kv_width:].astype(BF16)
    dqkv = jnp.concatenate(
        [
            dquery.reshape(count_of_rows, gy, q_cols),
            dkey.reshape(count_of_rows, gy, k_cols),
            dvalue_bf.reshape(count_of_rows, gy, v_cols),
        ],
        axis=2,
    )
    dall = jnp.concatenate([dqkv, dhidden_bf.reshape(count_of_rows, gy, o_cols)], axis=2)
    dall = dall.reshape(count_of_rows, gy, dp, att_share).transpose(2, 0, 1, 3)
    dall = trade_tokens(sizes, dall.reshape(dp, count_of_rows, gy * att_share))
    dall = dall.reshape(dp * count_of_rows, gy * att_share)
    places = rank * att_share + lax.broadcasted_iota(jnp.int32, (gy, att_share, 1), 1)
    from_normed = (places < qkv_cols).reshape(gy * att_share, 1)
    att_grad = jnp.stack(
        [
            jnp.where(from_normed, weight_product(dall, one), weight_product(dall, two)).astype(BF16)
            for one, two in zip(parts(normed_one_all), parts(mixed_all))
        ]
    ).reshape(gx, gy, att_share, fan)
    dnormed_one = back_onto(dqkv.reshape(count_of_rows, gy * qkv_cols), qkv_rows)
    dresidual, attgain_part = normalize_back(dnormed_one, attn_gain, rms_one, unit_one)
    input_grad = (dhidden + dresidual).astype(BF16)
    gain_parts = jnp.concatenate([attgain_part, mlpgain_part])
    gain_rows = -(-gain_parts.shape[0] // 1024) * 8
    gain_parts = jnp.pad(gain_parts, (0, gain_rows * 128 - gain_parts.shape[0])).reshape(gain_rows, 128)

    gate_up_sum, down_sum, att_sum, gain_sum = reduce_weights(
        sizes, gate_up_grad, down_grad, att_grad, gain_parts
    )
    gate_grad = gate_up_sum[:, 0].reshape(dp * share, fan).T.astype(F32)
    up_grad = gate_up_sum[:, 1].reshape(dp * share, fan).T.astype(F32)
    down_grad = (
        down_sum.reshape(dp, down_cols, groups, share)
        .transpose(2, 0, 3, 1)
        .reshape(down_weight.shape)
        .astype(F32)
    )
    att_sum = att_sum.reshape(all_cols, fan).T.astype(F32)
    gains = jnp.sum(gain_sum, axis=0).reshape(-1)
    return (
        layer_out,
        input_grad,
        att_sum[:, :q_cols],
        att_sum[:, q_cols : q_cols + k_cols],
        att_sum[:, q_cols + k_cols : qkv_cols],
        att_sum[:, qkv_cols:],
        gate_grad,
        up_grad,
        down_grad,
        gains[:width],
        gains[width : 2 * width],
    )


def solution(mesh):
    sizes = (mesh.shape["dp"], mesh.shape["gx"], mesh.shape["gy"])
    tokens = P(("dp", "gx", "gy"), None)
    block = P("gx", "gy")
    return jax.shard_map(
        functools.partial(on_device, sizes),
        mesh=mesh,
        in_specs=(tokens, P("dp"), P(), block, block, block, block, P(), block, block, block, tokens),
        out_specs=(tokens, tokens) + (block,) * 7 + (P(), P()),
        check_vma=False,
    )
```

```python
import functools

import jax
import jax.numpy as jnp
from jax import lax
from jax.experimental import pallas as pl
from jax.experimental.pallas import tpu as pltpu
from jax.sharding import PartitionSpec as P

QUERY_HEADS = 15
KEY_VALUE_HEADS = 5
GROUPS = QUERY_HEADS // KEY_VALUE_HEADS
HEAD_WIDTH = 64
SEQUENCE_LENGTH = 1024

THETA = 100000.0
EPSILON = 1e-05
MASKED = -1e30

F32 = jnp.float32
BF16 = jnp.bfloat16
MESH = pl.DeviceIdType.MESH
ANY = pl.BlockSpec(memory_space=pl.ANY)
VMEM = pl.BlockSpec(memory_space=pltpu.VMEM)


def plain_product(left, right):
    return jnp.dot(left, right, preferred_element_type=F32)


def weight_product(left, right):
    return lax.dot_general(left, right, (((0,), (0,)), ((), ())), preferred_element_type=F32)


def back_product(left, right):
    return lax.dot_general(left, right, (((1,), (1,)), ((), ())), preferred_element_type=F32)


class Net:
    def __init__(self, sizes, send_sems, recv_sems):
        self.dp, self.gx, self.gy = sizes
        self.cores = 2 if self.dp % 2 == 0 else 1
        self.hops = self.dp // self.cores
        self.d = lax.axis_index("dp")
        self.x = lax.axis_index("gx")
        self.y = lax.axis_index("gy")
        self.core = lax.rem(self.d, self.cores)
        self.hop = self.d // self.cores
        self.send_sems, self.recv_sems = send_sems, recv_sems
        self.sent, self.slots, self.pending = 0, 0, []

    def at_gx(self, j):
        return lax.rem(self.x + j, self.gx)

    def at_gy(self, k):
        return lax.rem(self.y + k, self.gy)

    def at_hop(self, i):
        return lax.rem(self.hop + i, self.hops)

    def gx_peer(self, j):
        return {"gx": self.at_gx(j)}

    def gy_peer(self, k):
        return {"gy": self.at_gy(k)}

    def hop_peer(self, i):
        return {"dp": self.at_hop(i) * self.cores + self.core}

    def core_peer(self):
        return {"dp": self.hop * self.cores + 1 - self.core}

    def dp_peer(self, i):
        return {"dp": lax.rem(self.d + i, self.dp)}

    def plane_peers(self):
        return [self.gx_peer(j) for j in range(1, self.gx)] + [
            self.gy_peer(k) for k in range(1, self.gy)
        ]

    def share_peers(self):
        peers = [self.hop_peer(i) for i in range(1, self.hops)]
        return peers + ([self.core_peer()] if self.cores == 2 else [])

    def greet(self, peers):
        barrier = pltpu.get_barrier_semaphore()
        for peer in peers:
            pl.semaphore_signal(barrier, inc=1, device_id=peer, device_id_type=MESH)
        pl.semaphore_wait(barrier, len(peers))

    def block(self, count):
        first = self.slots
        self.slots += count
        return first

    def copy(self, src, dst, slot, peer):
        return pltpu.make_async_remote_copy(
            src_ref=src,
            dst_ref=dst,
            send_sem=self.send_sems.at[self.sent],
            recv_sem=self.recv_sems.at[slot],
            device_id=peer,
            device_id_type=MESH,
        )

    def send(self, src, dst, slot, peer):
        copy = self.copy(src, dst, slot, peer)
        copy.start()
        self.sent += 1
        self.pending.append(copy)

    def arrive(self, dst, slot):
        pltpu.make_async_remote_copy(
            src_ref=dst,
            dst_ref=dst,
            send_sem=self.send_sems.at[0],
            recv_sem=self.recv_sems.at[slot],
            device_id=self.gy_peer(1),
            device_id_type=MESH,
        ).wait_recv()

    def drain(self):
        for copy in self.pending:
            copy.wait_send()


def far_first(count):
    order = list(range(1, count))
    return sorted(order, key=lambda k: -min(k, count - k))


class PlaneGather:
    def __init__(self, net, src, out):
        self.net, self.src, self.out = net, src, out
        self.gy_slot = net.block(net.gy)
        self.gx_slot = net.block(net.gx * net.gy)

    def start(self):
        self.start_gy()
        self.start_gx()

    def start_gy(self):
        net = self.net
        own = self.out(net.x, net.y)
        for k in range(1, net.gy):
            net.send(self.src, own, self.gy_slot + net.y, net.gy_peer(k))

    def start_gx(self):
        net = self.net
        own = self.out(net.x, net.y)
        for j in range(1, net.gx):
            net.send(self.src, own, self.gx_slot + net.x * net.gy + net.y, net.gx_peer(j))

    def relay(self, k):
        net = self.net
        row = net.at_gy(k)
        piece = self.out(net.x, row)
        net.arrive(piece, self.gy_slot + row)
        for j in range(1, net.gx):
            net.send(piece, piece, self.gx_slot + net.x * net.gy + row, net.gx_peer(j))

    def settle(self, j, k):
        net = self.net
        side, row = net.at_gx(j), net.at_gy(k)
        net.arrive(self.out(side, row), self.gx_slot + side * net.gy + row)


class Share:
    def __init__(self, net, out):
        self.net, self.out = net, out
        self.hop_slot = net.block(net.hops)
        self.core_slot = net.block(net.dp)

    def start(self, src):
        net = self.net
        own = self.out(net.d)
        for i in range(1, net.hops):
            net.send(src, own, self.hop_slot + net.hop, net.hop_peer(i))
        if net.cores == 2:
            net.send(src, own, self.core_slot + net.d, net.core_peer())

    def relay(self):
        net = self.net
        for i in range(1, net.hops):
            hop = net.at_hop(i)
            rank = hop * net.cores + net.core
            piece = self.out(rank)
            net.arrive(piece, self.hop_slot + hop)
            if net.cores == 2:
                net.send(piece, piece, self.core_slot + rank, net.core_peer())

    def settle(self):
        net = self.net
        if net.cores == 2:
            for hop in range(net.hops):
                rank = hop * net.cores + 1 - net.core
                net.arrive(self.out(rank), self.core_slot + rank)


class PlaneSum:
    def __init__(self, net, src, landing_x, stage, landing_y):
        self.net, self.src = net, src
        self.landing_x, self.stage, self.landing_y = landing_x, stage, landing_y
        self.gx_slot = net.block(net.gx * net.gy)
        self.gy_slot = net.block(net.gy)

    def start(self, k):
        net = self.net
        row = net.at_gy(k)
        for j in range(1, net.gx):
            net.send(
                self.src(net.at_gx(j), row),
                self.landing_x.at[net.x, row],
                self.gx_slot + net.x * net.gy + row,
                net.gx_peer(j),
            )

    def relay(self, k):
        net = self.net
        row = net.at_gy(k)
        total = self.src(net.x, row)[...].astype(F32)
        for j in range(1, net.gx):
            side = net.at_gx(j)
            net.arrive(self.landing_x.at[side, row], self.gx_slot + side * net.gy + row)
            total = total + self.landing_x[side, row].astype(F32)
        if k == 0:
            self.landing_y[net.y] = total.astype(self.landing_y.dtype)
        else:
            self.stage[row] = total.astype(self.stage.dtype)
            net.send(
                self.stage.at[row], self.landing_y.at[net.y], self.gy_slot + net.y, net.gy_peer(k)
            )

    def total(self):
        net = self.net
        for k in range(1, net.gy):
            row = net.at_gy(k)
            net.arrive(self.landing_y.at[row], self.gy_slot + row)
        total = self.landing_y[0].astype(F32)
        for row in range(1, net.gy):
            total = total + self.landing_y[row].astype(F32)
        return total


def call(kernel, sizes, number, name, out_shapes, out_specs, in_specs, scratch, sends, slots):
    def body(*refs):
        net = Net(sizes, refs[-2], refs[-1])
        kernel(net, *refs[:-2])
        net.drain()
        assert net.sent <= sends and net.slots <= slots, (net.sent, net.slots)

    return pl.pallas_call(
        body,
        name=name,
        out_shape=out_shapes,
        in_specs=in_specs,
        out_specs=out_specs,
        scratch_shapes=list(scratch)
        + [pltpu.SemaphoreType.DMA((sends,)), pltpu.SemaphoreType.DMA((slots,))],
        compiler_params=pltpu.CompilerParams(collective_id=number, has_side_effects=True),
    )


def local(copies):
    for copy in copies:
        copy.start()


def wait_local(copies):
    for copy in copies:
        copy.wait()


def gather_weights(sizes, att):
    dp, gx, gy = sizes
    hops = dp // 2

    def kernel(net, att_ref, att_out, sems):
        net.greet(net.plane_peers() + net.share_peers())
        att_plane = PlaneGather(net, att_ref, lambda a, b: att_out.at[a, b, net.d])
        first_hop = net.block(gx * gy * net.hops)
        first_core = net.block(gx * gy * net.dp)

        def shared(a, b):
            item = Share.__new__(Share)
            item.net = net
            item.out = lambda rank: att_out.at[a, b, rank]
            place = a * gy + b
            item.hop_slot = first_hop + place * net.hops
            item.core_slot = first_core + place * net.dp
            return item

        own = [pltpu.make_async_copy(att_ref, att_out.at[net.x, net.y, net.d], sems.at[0])]
        att_plane.start()
        shared(net.x, net.y).start(att_ref)
        local(own)
        for k in range(1, gy):
            att_plane.relay(k)
            row = net.at_gy(k)
            shared(net.x, row).start(att_out.at[net.x, row, net.d])
        for j in range(1, gx):
            for k in range(gy):
                att_plane.settle(j, k)
                side, row = net.at_gx(j), net.at_gy(k)
                shared(side, row).start(att_out.at[side, row, net.d])
        places = [(j, k) for j in range(gx) for k in range(gy)]
        for j, k in places:
            shared(net.at_gx(j), net.at_gy(k)).relay()
        for j, k in places:
            shared(net.at_gx(j), net.at_gy(k)).settle()
        wait_local(own)

    shape = jax.ShapeDtypeStruct((gx, gy, dp) + att.shape, BF16)
    return call(
        kernel, sizes, 1, "gather_weights", shape, ANY, [VMEM], [pltpu.SemaphoreType.DMA((1,))],
        gx * gy * (hops + dp) + gx * gy + gy, gx * gy * (hops + dp) + gy + gx * gy,
    )(att)


def turned(values):
    return jnp.transpose(values)


def head_rows(ref, first, lead=()):
    return jnp.concatenate(
        [ref[:, h * HEAD_WIDTH : (h + 1) * HEAD_WIDTH] for h in range(first, first + GROUPS)], axis=0
    )


def key_columns(ref, place):
    columns = ref[:, :, :, place * HEAD_WIDTH : (place + 1) * HEAD_WIDTH]
    return columns.reshape(-1, HEAD_WIDTH)


def put_heads(ref, first, rows, values):
    for n in range(GROUPS):
        lanes = slice((first + n) * HEAD_WIDTH, (first + n + 1) * HEAD_WIDTH)
        ref[:, lanes] = values[n * rows : (n + 1) * rows].astype(ref.dtype)


def attend_heads(key_heads, q_ref, kv_ref, bias_ref, mixed_ref, logsum_ref):
    rows = q_ref.shape[0]
    bias = jnp.concatenate([bias_ref[...]] * GROUPS, axis=1)
    for k in key_heads:
        query = head_rows(q_ref, k * GROUPS)
        scores = back_product(key_columns(kv_ref, k), query) * HEAD_WIDTH ** (-0.5) + bias
        highest = jnp.max(scores, axis=0, keepdims=True)
        weights = jnp.exp(scores - highest)
        sums = jnp.sum(weights, axis=0, keepdims=True)
        logsum_ref[k : k + 1, :] = highest + jnp.log(sums)
        probs = (weights * (1.0 / sums)).astype(BF16)
        mixed = weight_product(key_columns(kv_ref, KEY_VALUE_HEADS + k), probs)
        put_heads(mixed_ref, k * GROUPS, rows, turned(mixed))


def attend_heads_back(q_ref, kv_ref, bias_ref, logsum_ref, mixed_ref, dmixed_ref, dq_ref, dkv_ref):
    rows = q_ref.shape[0]
    bias = jnp.concatenate([bias_ref[...]] * GROUPS, axis=1)
    blocks = kv_ref.shape[:3]
    for k in range(KEY_VALUE_HEADS):
        query = head_rows(q_ref, k * GROUPS)
        mixed = head_rows(mixed_ref, k * GROUPS)
        dmixed = head_rows(dmixed_ref, k * GROUPS)
        keys = key_columns(kv_ref, k)
        scores = back_product(keys, query) * HEAD_WIDTH ** (-0.5) + bias
        weights = jnp.exp(scores - logsum_ref[k : k + 1, :])
        delta = jnp.sum(turned(mixed.astype(F32) * dmixed.astype(F32)), axis=0, keepdims=True)
        dprobs = back_product(key_columns(kv_ref, KEY_VALUE_HEADS + k), dmixed)
        dscores = (weights * (dprobs - delta)).astype(BF16)
        dquery = weight_product(keys, dscores) * HEAD_WIDTH ** (-0.5)
        put_heads(dq_ref, k * GROUPS, rows, turned(dquery))
        dkeys = plain_product(dscores, query) * HEAD_WIDTH ** (-0.5)
        dvalues = plain_product(weights.astype(BF16), dmixed)
        lanes = slice(k * HEAD_WIDTH, (k + 1) * HEAD_WIDTH)
        dkv_ref[:, :, :, lanes] = dkeys.astype(BF16).reshape(blocks + (HEAD_WIDTH,))
        place = KEY_VALUE_HEADS + k
        lanes = slice(place * HEAD_WIDTH, (place + 1) * HEAD_WIDTH)
        dkv_ref[:, :, :, lanes] = dvalues.astype(BF16).reshape(blocks + (HEAD_WIDTH,))


def turn_pairs(values, cos, sin):
    lanes = cos.shape[1]
    half = HEAD_WIDTH // 2
    front = lax.broadcasted_iota(jnp.int32, cos.shape, 1) % HEAD_WIDTH < half
    pieces = []
    for first in range(0, values.shape[1], lanes):
        part = values[:, first : first + lanes]
        other = jnp.where(front, pltpu.roll(part, lanes - half, 1), pltpu.roll(part, half, 1))
        pieces.append(part * cos + other * sin)
    return jnp.concatenate(pieces, axis=1)


def forward(sizes, cols, att, normed, inputs, gain, cos, sin, bias, gate_up, down, cot):
    dp, gx, gy = sizes
    q_cols, k_cols, v_cols, o_cols = cols
    qkv_cols = q_cols + k_cols + v_cols
    rows, width = inputs.shape
    fan = att.shape[3]
    lanes = cos.shape[1]
    q_width, k_width, v_width = gy * q_cols, gy * k_cols, gy * v_cols
    q_pad, k_pad = -(-q_width // lanes) * lanes, -(-k_width // lanes) * lanes

    def kernel(
        net, att_ref, nm_ref, in_ref, gain_ref, cos_ref, sin_ref, bias_ref, gu_ref, dn_ref, cot_ref,
        q_ref, kv_out, mixed_ref, logsum_ref, hidden_ref,
        gu_out, dn_out, cot_out, nm_out, mixed_out, two_out,
        q_wide, k_wide, kv_ref, two_ref, sems,
    ):
        q_wide[...] = jnp.zeros_like(q_wide)
        k_wide[...] = jnp.zeros_like(k_wide)
        for b in range(gy):
            block = sum(
                back_product(nm_ref[:, a * fan : (a + 1) * fan], att_ref[a, b, :qkv_cols, :])
                for a in range(gx)
            ).astype(BF16)
            q_wide[:, b * q_cols : (b + 1) * q_cols] = block[:, :q_cols].astype(F32)
            k_wide[:, b * k_cols : (b + 1) * k_cols] = block[:, q_cols : q_cols + k_cols].astype(F32)
            first = k_width + b * v_cols
            kv_ref[:, first : first + v_cols] = block[:, q_cols + k_cols :]
        cos_rows, sin_rows = cos_ref[...], sin_ref[...]
        kv_ref[:, :k_width] = turn_pairs(k_wide[...], cos_rows, sin_rows)[:, :k_width].astype(BF16)

        net.greet(net.plane_peers() + net.share_peers())
        kv = PlaneGather(net, kv_ref, lambda a, b: kv_out.at[a, b])
        gu = PlaneGather(net, gu_ref, lambda a, b: gu_out.at[a, :, b])
        dn = PlaneGather(net, dn_ref, lambda a, b: dn_out.at[a, b])
        cot_share, nm_share, mixed_share, two_share = (
            Share(net, lambda r, out=out: out.at[r]) for out in (cot_out, nm_out, mixed_out, two_out)
        )
        own = [
            pltpu.make_async_copy(kv_ref, kv_out.at[net.x, net.y], sems.at[0]),
            pltpu.make_async_copy(gu_ref, gu_out.at[net.x, :, net.y], sems.at[1]),
            pltpu.make_async_copy(dn_ref, dn_out.at[net.x, net.y], sems.at[2]),
            pltpu.make_async_copy(cot_ref, cot_out.at[net.d], sems.at[3]),
            pltpu.make_async_copy(nm_ref, nm_out.at[net.d], sems.at[4]),
        ]
        kv.start()
        gu.start_gy()
        dn.start_gy()
        local(own)
        cot_share.start(cot_ref)
        nm_share.start(nm_ref)
        q_ref[...] = turn_pairs(q_wide[...], cos_rows, sin_rows)[:, :q_width].astype(BF16)
        for k in range(1, gy):
            kv.relay(k)
        gu.start_gx()
        dn.start_gx()
        for j in range(1, gx):
            for k in range(gy):
                kv.settle(j, k)
        wait_local(own)

        turns = list(range(1, gy))
        heads = list(range(KEY_VALUE_HEADS))
        for n, k in enumerate(turns):
            mine = heads[n * len(heads) // len(turns) : (n + 1) * len(heads) // len(turns)]
            attend_heads(mine, q_ref, kv_out, bias_ref, mixed_ref, logsum_ref)
            if n + 1 < len(turns):
                gu.relay(k)
                dn.relay(k)
        last = pltpu.make_async_copy(mixed_ref, mixed_out.at[net.d], sems.at[5])
        last.start()
        mixed_share.start(mixed_ref)
        for b in range(gy):
            block = sum(
                back_product(mixed_ref[:, a * fan : (a + 1) * fan], att_ref[a, b, qkv_cols:, :])
                for a in range(gx)
            ).astype(BF16)
            span = slice(b * o_cols, (b + 1) * o_cols)
            hidden_ref[:, span] = in_ref[:, span].astype(F32) + block.astype(F32)
        hidden = hidden_ref[...]
        scale = lax.rsqrt(jnp.sum(hidden * hidden, axis=1, keepdims=True) / width + EPSILON)
        two_ref[...] = (hidden * scale * gain_ref[...]).astype(BF16)
        local_two = pltpu.make_async_copy(two_ref, two_out.at[net.d], sems.at[6])
        local_two.start()
        two_share.start(two_ref)
        gu.relay(turns[-1])
        dn.relay(turns[-1])
        shares = (cot_share, nm_share, mixed_share, two_share)
        for share in shares:
            share.relay()
        for share in shares:
            share.settle()
        for j in range(1, gx):
            for k in range(gy):
                gu.settle(j, k)
                dn.settle(j, k)
        wait_local([last, local_two])

    shared = jax.ShapeDtypeStruct((dp,) + inputs.shape, BF16)
    shapes = (
        jax.ShapeDtypeStruct((rows, q_width), BF16),
        jax.ShapeDtypeStruct((gx, gy, rows, k_width + v_width), BF16),
        jax.ShapeDtypeStruct((rows, q_width), BF16),
        jax.ShapeDtypeStruct((KEY_VALUE_HEADS, GROUPS * rows), F32),
        jax.ShapeDtypeStruct(inputs.shape, F32),
        jax.ShapeDtypeStruct((gx, 2, gy) + gate_up.shape[1:], BF16),
        jax.ShapeDtypeStruct((gx, gy) + down.shape, BF16),
        shared, shared, shared, shared,
    )
    scratch = [
        pltpu.VMEM((rows, q_pad), F32),
        pltpu.VMEM((rows, k_pad), F32),
        pltpu.VMEM((rows, k_width + v_width), BF16),
        pltpu.VMEM(inputs.shape, BF16),
        pltpu.SemaphoreType.DMA((7,)),
    ]
    count = 3 * (gx * gy + gy) + 4 * 2 * dp
    return call(
        kernel, sizes, 2, "forward", shapes, [VMEM] * 5 + [ANY] * 6, [VMEM] * 10, scratch, count, count,
    )(att, normed, inputs, gain, cos, sin, bias, gate_up, down, cot)


def mlp(normed_all, cot_all, gate_up, down):
    gx, both, fan = gate_up.shape
    rows, width = normed_all.shape
    hidden = both // 2
    part = down.shape[2]
    step = rows // 2 if rows % 32 == 0 else rows

    def kernel(n_ref, c_ref, gu_ref, dt_ref, dn_ref, mo_ref, gg_ref, dg_ref, act_ref, delta_ref):
        def tokens(i, carry):
            span = pl.ds(pl.multiple_of(i * step, step), step)
            normed, cot = n_ref[span, :], c_ref[span, :]
            gate_up_rows = sum(
                back_product(normed[:, a * fan : (a + 1) * fan], gu_ref[a]) for a in range(gx)
            ).astype(BF16)
            gate = gate_up_rows[:, :hidden].astype(F32)
            up = gate_up_rows[:, hidden:].astype(F32)
            dact = jnp.concatenate([plain_product(cot, dt_ref[a]) for a in range(gx)], axis=1)
            sigmoid = jax.nn.sigmoid(gate)
            act = (gate * sigmoid * up).astype(BF16)
            gate_delta = (dact * up * sigmoid * (1.0 + gate * (1.0 - sigmoid))).astype(BF16)
            up_delta = (dact * gate * sigmoid).astype(BF16)
            deltas = jnp.concatenate([gate_delta, up_delta], axis=1)
            delta_ref[span, :] = deltas
            for a in range(gx):
                act_ref[a, span, :] = act[:, a * part : (a + 1) * part]
                dn_ref[span, a * fan : (a + 1) * fan] = plain_product(deltas, gu_ref[a]).astype(BF16)
            mo_ref[span, :] = sum(
                back_product(act[:, a * part : (a + 1) * part], dt_ref[a]) for a in range(gx)
            ).astype(BF16)
            return carry

        lax.fori_loop(0, rows // step, tokens, 0)
        for a in range(gx):
            gg_ref[a] = weight_product(delta_ref[...], n_ref[:, a * fan : (a + 1) * fan]).astype(BF16)
            dg_ref[a] = weight_product(c_ref[...], act_ref[a]).astype(BF16)

    return pl.pallas_call(
        kernel,
        name="mlp",
        out_shape=(
            jax.ShapeDtypeStruct(normed_all.shape, BF16),
            jax.ShapeDtypeStruct(normed_all.shape, BF16),
            jax.ShapeDtypeStruct(gate_up.shape, BF16),
            jax.ShapeDtypeStruct(down.shape, BF16),
        ),
        in_specs=[VMEM] * 4,
        out_specs=[VMEM] * 4,
        scratch_shapes=[pltpu.VMEM((gx, rows, part), BF16), pltpu.VMEM((rows, both), BF16)],
    )(normed_all, cot_all, gate_up, down)


def sum_tokens(sizes, *parts):
    dp, gx, gy = sizes
    count = len(parts)
    hops = dp // 2
    shape = parts[0].shape[1:]

    def kernel(net, *refs):
        srcs, outs, scratch = refs[:count], refs[count : 2 * count], refs[2 * count :]
        landing_core, stage, landing_hop = scratch[:count], scratch[count : 2 * count], scratch[2 * count :]
        net.greet(net.share_peers())
        core_slots = [net.block(net.hops) for _ in range(count)]
        hop_slots = [net.block(net.hops) for _ in range(count)]
        order = list(range(1, net.hops)) + [0]
        for n in range(count):
            for i in order:
                hop = net.at_hop(i)
                net.send(
                    srcs[n].at[hop * 2 + 1 - net.core], landing_core[n].at[hop],
                    core_slots[n] + hop, net.core_peer(),
                )
        for n in range(count):
            for i in order:
                hop = net.at_hop(i)
                net.arrive(landing_core[n].at[hop], core_slots[n] + hop)
                total = srcs[n][hop * 2 + net.core].astype(F32) + landing_core[n][hop].astype(F32)
                if i == 0:
                    outs[n][...] = total
                else:
                    stage[n][hop] = total.astype(BF16)
                    net.send(
                        stage[n].at[hop], landing_hop[n].at[net.hop],
                        hop_slots[n] + net.hop, net.hop_peer(i),
                    )
        for n in range(count):
            for i in range(1, net.hops):
                hop = net.at_hop(i)
                net.arrive(landing_hop[n].at[hop], hop_slots[n] + hop)
                outs[n][...] += landing_hop[n][hop].astype(F32)

    shapes = tuple(jax.ShapeDtypeStruct(shape, F32) for _ in parts)
    slab = pltpu.VMEM((hops,) + shape, BF16)
    return call(
        kernel, sizes, 4, "sum_tokens", shapes, [VMEM] * count, [VMEM] * count,
        [slab] * (3 * count), count * dp, count * dp,
    )(*parts)


def backward(
    sizes, cols, query, kv_all, bias, logsum, mixed, dmixed, dhidden, att, normed_all, mixed_all,
    inputs, gain, mlpgain, cos, sin, gate_up, down,
):
    dp, gx, gy = sizes
    q_cols, k_cols, v_cols, o_cols = cols
    qkv_cols = q_cols + k_cols + v_cols
    all_cols = qkv_cols + o_cols
    att_share = all_cols // dp
    rows, width = inputs.shape
    fan = att.shape[3]
    lanes = cos.shape[1]
    q_width, k_width = gy * q_cols, gy * k_cols
    q_pad, k_pad = -(-q_width // lanes) * lanes, -(-k_width // lanes) * lanes
    kv_width = kv_all.shape[3]
    pieces = [
        (gate_up.shape[3:], BF16), (gate_up.shape[3:], BF16), (down.shape[2:], BF16),
        ((att_share, fan), BF16), ((8, width), F32), ((rows, kv_width), BF16),
    ]
    count = len(pieces)

    def kernel(net, *refs):
        (
            q_ref, kv_ref, bias_ref, logsum_ref, mixed_ref, dmixed_ref, dhidden_ref, att_ref, nm_ref,
            mx_ref, in_ref, gain_ref, mlpgain_ref, cos_ref, sin_ref, gu_ref, dn_ref,
        ) = refs[:17]
        input_grad, gu_out, dn_out, att_out, gain_out = refs[17:22]
        q_wide, k_wide, dkv_ref, p_ref, trade_src, trade_in, dn_one, att_grad, gains = refs[22:31]
        refs = refs[31:]
        landing_x, stage, landing_y = (refs[n * count : (n + 1) * count] for n in range(3))
        result, sems = refs[3 * count : 4 * count - 1], refs[4 * count - 1]

        net.greet(net.plane_peers() + [net.dp_peer(i) for i in range(1, dp)])
        sources = [
            lambda a, b: gu_ref.at[a, 0, b], lambda a, b: gu_ref.at[a, 1, b], lambda a, b: dn_ref.at[a, b],
            lambda a, b: att_grad.at[a, b], lambda a, b: gains, lambda a, b: dkv_ref.at[a, b],
        ]
        sums = [
            PlaneSum(net, sources[n], landing_x[n], stage[n], landing_y[n]) for n in range(count)
        ]
        outs = [
            lambda r: gu_out.at[r, 0], lambda r: gu_out.at[r, 1], lambda r: dn_out.at[r],
            lambda r: att_out.at[r], lambda r: gain_out.at[r],
        ]
        shares = [Share(net, out) for out in outs]
        mlp_sums, att_sums, dkv_sum = sums[:3], sums[3:5], sums[5]
        order = far_first(gy) + [0]

        def begin(items, turns):
            for k in turns:
                for item in items:
                    item.start(k)

        def relay(items, turns):
            for k in turns:
                for item in items:
                    item.relay(k)

        own = []

        def finish(first, items):
            for n, item in enumerate(items, first):
                result[n][...] = item.total().astype(result[n].dtype)
                shares[n].start(result[n])
                own.append(pltpu.make_async_copy(result[n], shares[n].out(net.d), sems.at[n]))
                own[-1].start()

        begin(mlp_sums, order[:1])
        q_wide[...] = jnp.zeros_like(q_wide)
        k_wide[...] = jnp.zeros_like(k_wide)
        attend_heads_back(
            q_ref, kv_ref, bias_ref, logsum_ref, mixed_ref, dmixed_ref, q_wide, dkv_ref
        )
        begin([dkv_sum], order)
        begin(mlp_sums, order[1:2])
        relay(mlp_sums, order[:1])
        relay([dkv_sum], order)
        begin(mlp_sums, order[2:])
        cos_rows, sin_rows = cos_ref[...], -sin_ref[...]
        dquery = turn_pairs(q_wide[...], cos_rows, sin_rows)[:, :q_width].astype(BF16)
        dhidden = dhidden_ref[...]
        dhidden_bf = dhidden.astype(BF16)
        for b in range(gy):
            p_ref[b, :, :q_cols] = dquery[:, b * q_cols : (b + 1) * q_cols]
            p_ref[b, :, qkv_cols:] = dhidden_bf[:, b * o_cols : (b + 1) * o_cols]
        dkv = dkv_sum.total()
        k_wide[:, :k_width] = dkv[:, :k_width]
        dkey = turn_pairs(k_wide[...], cos_rows, sin_rows)[:, :k_width].astype(BF16)
        dvalue = dkv[:, k_width:].astype(BF16)
        for b in range(gy):
            p_ref[b, :, q_cols : q_cols + k_cols] = dkey[:, b * k_cols : (b + 1) * k_cols]
            p_ref[b, :, q_cols + k_cols : qkv_cols] = dvalue[:, b * v_cols : (b + 1) * v_cols]
        for r in range(dp):
            for b in range(gy):
                trade_src[r, :, b * att_share : (b + 1) * att_share] = p_ref[
                    b, :, r * att_share : (r + 1) * att_share
                ]
        trade_slot = net.block(dp)
        for i in range(1, dp):
            rank = lax.rem(net.d + i, dp)
            net.send(trade_src.at[rank], trade_in.at[net.d], trade_slot + net.d, net.dp_peer(i))
        trade_in[net.d] = trade_src[net.d]
        relay(mlp_sums, order[1:2])

        for a in range(gx):
            dn_one[:, a * fan : (a + 1) * fan] = sum(
                plain_product(p_ref[b, :, :qkv_cols], att_ref[a, b, :qkv_cols, :]) for b in range(gy)
            )
        dnormed = dn_one[...]
        values = in_ref[...].astype(F32)
        rms = lax.rsqrt(jnp.sum(values * values, axis=1, keepdims=True) / width + EPSILON)
        unit = values * rms
        scaled = dnormed * gain_ref[...]
        level = jnp.sum(scaled * unit, axis=1, keepdims=True) / width
        input_grad[...] = (dhidden + rms * (scaled - unit * level)).astype(BF16)
        gains[...] = jnp.zeros_like(gains)
        gains[0:1, :] = jnp.sum(dnormed * unit, axis=0, keepdims=True)
        gains[1:2, :] = mlpgain_ref[...]

        for i in range(1, dp):
            rank = lax.rem(net.d + i, dp)
            net.arrive(trade_in.at[rank], trade_slot + rank)
        dall = trade_in[...].reshape(dp * rows, gy * att_share)
        places = lax.broadcasted_iota(jnp.int32, (gy * att_share, fan), 0) % att_share
        from_normed = places + net.d * att_share < qkv_cols
        for a in range(gx):
            span = slice(a * fan, (a + 1) * fan)
            grad = jnp.where(
                from_normed,
                weight_product(dall, nm_ref[:, span]),
                weight_product(dall, mx_ref[:, span]),
            ).astype(BF16)
            for b in range(gy):
                att_grad[a, b] = grad[b * att_share : (b + 1) * att_share]
        begin(att_sums, order)
        relay(mlp_sums, order[2:])
        finish(0, mlp_sums)
        relay(att_sums, order)
        finish(3, att_sums)
        for share in shares:
            share.relay()
        for share in shares:
            share.settle()
        wait_local(own)

    shapes = (
        jax.ShapeDtypeStruct(inputs.shape, BF16),
        jax.ShapeDtypeStruct((dp, 2) + pieces[0][0], BF16),
        jax.ShapeDtypeStruct((dp,) + pieces[2][0], BF16),
        jax.ShapeDtypeStruct((dp,) + pieces[3][0], BF16),
        jax.ShapeDtypeStruct((dp,) + pieces[4][0], F32),
    )
    scratch = [
        pltpu.VMEM((rows, q_pad), F32),
        pltpu.VMEM((rows, k_pad), F32),
        pltpu.VMEM(kv_all.shape, BF16),
        pltpu.VMEM((gy, rows, all_cols), BF16),
        pltpu.VMEM((dp, rows, gy * att_share), BF16),
        pltpu.VMEM((dp, rows, gy * att_share), BF16),
        pltpu.VMEM((rows, width), F32),
        pltpu.VMEM((gx, gy, att_share, fan), BF16),
        pltpu.VMEM((8, width), F32),
    ]
    scratch += [pltpu.VMEM((gx, gy) + p, t) for p, t in pieces]
    scratch += [pltpu.VMEM((gy,) + p, t) for p, t in pieces] * 2
    scratch += [pltpu.VMEM(p, t) for p, t in pieces[:-1]]
    scratch += [pltpu.SemaphoreType.DMA((count - 1,))]
    sems = count * (gx * gy + gy) + (count - 1) * 2 * dp + dp
    return call(
        kernel, sizes, 5, "backward", shapes, [VMEM] + [ANY] * 4, [VMEM] * 17, scratch, sems, sems,
    )(
        query, kv_all, bias, logsum, mixed, dmixed, dhidden, att, normed_all, mixed_all,
        inputs, gain, mlpgain, cos, sin, gate_up, down,
    )


def rope_angles(positions):
    half_dim = HEAD_WIDTH // 2
    inverse = THETA ** (-(jnp.arange(half_dim, dtype=F32) * 2.0 / HEAD_WIDTH))
    angles = positions[:, None] * inverse[None, :]
    return (jnp.cos(angles)[:, None, :], jnp.sin(angles)[:, None, :])


def normalize(values, gain):
    rms_rows = lax.rsqrt(jnp.mean(values * values, axis=1, keepdims=True) + EPSILON)
    unit_rows = values * rms_rows
    return (rms_rows, unit_rows, (unit_rows * gain).astype(BF16))


def normalize_back(dnormed, gain, rms_rows, unit_rows):
    scaled = dnormed * gain
    dvalues = rms_rows * (scaled - unit_rows * jnp.mean(scaled * unit_rows, axis=1, keepdims=True))
    return (dvalues, jnp.sum(dnormed * unit_rows, axis=0))


def on_device(
    sizes,
    inputs,
    segments,
    attn_gain,
    query_weight,
    key_weight,
    value_weight,
    output_weight,
    mlp_gain,
    gate_weight,
    up_weight,
    down_weight,
    cotangent,
):
    dp, gx, gy = sizes
    count_of_rows, width = inputs.shape
    rank = lax.axis_index("dp")
    begin_row = (lax.axis_index("gx") * gy + lax.axis_index("gy")) * count_of_rows
    seq_begin = begin_row // SEQUENCE_LENGTH * SEQUENCE_LENGTH
    local_places = begin_row - seq_begin + jnp.arange(count_of_rows)
    cos_table, sin_table = rope_angles(local_places.astype(F32))
    query_segs = lax.dynamic_slice_in_dim(segments, begin_row, count_of_rows, 0)
    allowed = (jnp.arange(SEQUENCE_LENGTH)[:, None] <= local_places[None, :]) & (
        query_segs[None, :] == segments[:, None]
    )
    bias = jnp.where(allowed, 0.0, MASKED).astype(F32)
    residual = inputs.astype(F32)
    _, _, normed_one = normalize(residual, attn_gain)

    fan = query_weight.shape[0]
    q_cols, k_cols, v_cols = query_weight.shape[1], key_weight.shape[1], value_weight.shape[1]
    o_cols = output_weight.shape[1]
    qkv_cols = q_cols + k_cols + v_cols
    all_cols = qkv_cols + o_cols
    att_share = all_cols // dp
    packed = jnp.concatenate([query_weight, key_weight, value_weight, output_weight], axis=1).T
    att_part = lax.dynamic_slice_in_dim(packed, rank * att_share, att_share, 0)
    share = gate_weight.shape[1] // dp
    groups = gy // gx
    gate_up_part = jnp.stack(
        [
            lax.dynamic_slice_in_dim(gate_weight, rank * share, share, 1).T,
            lax.dynamic_slice_in_dim(up_weight, rank * share, share, 1).T,
        ]
    )
    down_cols = down_weight.shape[1]
    down_part = lax.dynamic_slice_in_dim(
        down_weight.reshape(groups, dp, share, down_cols), rank, 1, 1
    ).reshape(groups * share, down_cols).T

    att_all = gather_weights(sizes, att_part).reshape(gx, gy, all_cols, fan)
    cos_wide = jnp.tile(cos_table[:, 0], (1, 4))
    sin_wide = jnp.tile(jnp.concatenate([-sin_table[:, 0], sin_table[:, 0]], axis=1), (1, 2))
    (
        rotated_query, kv_all, attention_mixture, logsum, hidden,
        gate_up_all, down_all, cot_all, normed_one_all, mixed_all, normed_all,
    ) = forward(
        sizes, (q_cols, k_cols, v_cols, o_cols), att_all, normed_one, inputs, mlp_gain.reshape(1, -1),
        cos_wide, sin_wide, bias, gate_up_part, down_part, cotangent,
    )
    out_rows = att_all[:, :, qkv_cols:].reshape(gx, gy * o_cols, fan)
    hidden_width = gy * share
    gate_up_all = gate_up_all.reshape(gx, 2 * hidden_width, fan)
    half_hidden = groups * share
    down_all = down_all.reshape(gx, gy * down_cols, half_hidden)
    cot_all, normed_one_all, mixed_all, normed_all = (
        rows.reshape(dp * count_of_rows, width) for rows in (cot_all, normed_one_all, mixed_all, normed_all)
    )
    rms_two, unit_two, _ = normalize(hidden, mlp_gain)

    def parts(rows):
        return [rows[:, a * fan : (a + 1) * fan] for a in range(gx)]

    def back_onto(rows, weights):
        return jnp.concatenate([plain_product(rows, weights[a]) for a in range(gx)], axis=1)

    dnormed_part, mlp_part, gate_up_grad, down_grad = mlp(normed_all, cot_all, gate_up_all, down_all)
    dnormed_two, mlp_out = sum_tokens(
        sizes,
        dnormed_part.reshape(dp, count_of_rows, width),
        mlp_part.reshape(dp, count_of_rows, width),
    )
    layer_out = (hidden + mlp_out).astype(BF16)

    gate_up_grad = gate_up_grad.reshape(gx, 2, gy, share, fan)
    down_grad = down_grad.reshape(gx, gy, down_cols, half_hidden)

    dhidden_norm, mlpgain_part = normalize_back(dnormed_two, mlp_gain, rms_two, unit_two)
    dhidden = cotangent.astype(F32) + dhidden_norm
    dhidden_bf = dhidden.astype(BF16)
    mixture_gradient = back_onto(dhidden_bf, out_rows).astype(BF16)
    input_grad, gate_up_sum, down_sum, att_sum, gain_sum = backward(
        sizes, (q_cols, k_cols, v_cols, o_cols), rotated_query, kv_all, bias, logsum, attention_mixture,
        mixture_gradient, dhidden, att_all, normed_one_all, mixed_all, inputs, attn_gain.reshape(1, -1),
        mlpgain_part.reshape(1, -1), cos_wide, sin_wide, gate_up_grad, down_grad,
    )
    gate_grad = gate_up_sum[:, 0].reshape(dp * share, fan).T.astype(F32)
    up_grad = gate_up_sum[:, 1].reshape(dp * share, fan).T.astype(F32)
    down_grad = (
        down_sum.reshape(dp, down_cols, groups, share)
        .transpose(2, 0, 3, 1)
        .reshape(down_weight.shape)
        .astype(F32)
    )
    att_sum = att_sum.reshape(all_cols, fan).T.astype(F32)
    gains = jnp.sum(gain_sum, axis=0)
    return (
        layer_out,
        input_grad,
        att_sum[:, :q_cols],
        att_sum[:, q_cols : q_cols + k_cols],
        att_sum[:, q_cols + k_cols : qkv_cols],
        att_sum[:, qkv_cols:],
        gate_grad,
        up_grad,
        down_grad,
        gains[0],
        gains[1],
    )


def solution(mesh):
    sizes = (mesh.shape["dp"], mesh.shape["gx"], mesh.shape["gy"])
    tokens = P(("dp", "gx", "gy"), None)
    block = P("gx", "gy")
    return jax.shard_map(
        functools.partial(on_device, sizes),
        mesh=mesh,
        in_specs=(tokens, P("dp"), P(), block, block, block, block, P(), block, block, block, tokens),
        out_specs=(tokens, tokens) + (block,) * 7 + (P(), P()),
        check_vma=False,
    )
```

```python
import functools

import jax
import jax.numpy as jnp
from jax import lax
from jax.experimental import pallas as pl
from jax.experimental.pallas import tpu as pltpu
from jax.sharding import PartitionSpec as P

QUERY_HEADS = 15
KEY_VALUE_HEADS = 5
GROUPS = QUERY_HEADS // KEY_VALUE_HEADS
HEAD_WIDTH = 64
SEQUENCE_LENGTH = 1024

THETA = 100000.0
EPSILON = 1e-05
MASKED = -1e30

F32 = jnp.float32
BF16 = jnp.bfloat16
MESH = pl.DeviceIdType.MESH
ANY = pl.BlockSpec(memory_space=pl.ANY)
VMEM = pl.BlockSpec(memory_space=pltpu.VMEM)


def plain_product(left, right):
    return jnp.dot(left, right, preferred_element_type=F32)


def weight_product(left, right):
    return lax.dot_general(left, right, (((0,), (0,)), ((), ())), preferred_element_type=F32)


def back_product(left, right):
    return lax.dot_general(left, right, (((1,), (1,)), ((), ())), preferred_element_type=F32)


class Net:
    def __init__(self, sizes, send_sems, recv_sems):
        self.dp, self.gx, self.gy = sizes
        self.cores = 2 if self.dp % 2 == 0 else 1
        self.hops = self.dp // self.cores
        self.d = lax.axis_index("dp")
        self.x = lax.axis_index("gx")
        self.y = lax.axis_index("gy")
        self.core = lax.rem(self.d, self.cores)
        self.hop = self.d // self.cores
        self.send_sems, self.recv_sems = send_sems, recv_sems
        self.sent, self.slots, self.pending = 0, 0, []

    def at_gx(self, j):
        return lax.rem(self.x + j, self.gx)

    def at_gy(self, k):
        return lax.rem(self.y + k, self.gy)

    def at_hop(self, i):
        return lax.rem(self.hop + i, self.hops)

    def gx_peer(self, j):
        return {"gx": self.at_gx(j)}

    def gy_peer(self, k):
        return {"gy": self.at_gy(k)}

    def hop_peer(self, i):
        return {"dp": self.at_hop(i) * self.cores + self.core}

    def core_peer(self):
        return {"dp": self.hop * self.cores + 1 - self.core}

    def dp_peer(self, i):
        return {"dp": lax.rem(self.d + i, self.dp)}

    def plane_peers(self):
        return [self.gx_peer(j) for j in range(1, self.gx)] + [
            self.gy_peer(k) for k in range(1, self.gy)
        ]

    def share_peers(self):
        peers = [self.hop_peer(i) for i in range(1, self.hops)]
        return peers + ([self.core_peer()] if self.cores == 2 else [])

    def greet(self, peers):
        barrier = pltpu.get_barrier_semaphore()
        for peer in peers:
            pl.semaphore_signal(barrier, inc=1, device_id=peer, device_id_type=MESH)
        pl.semaphore_wait(barrier, len(peers))

    def block(self, count):
        first = self.slots
        self.slots += count
        return first

    def copy(self, src, dst, slot, peer):
        return pltpu.make_async_remote_copy(
            src_ref=src,
            dst_ref=dst,
            send_sem=self.send_sems.at[self.sent],
            recv_sem=self.recv_sems.at[slot],
            device_id=peer,
            device_id_type=MESH,
        )

    def send(self, src, dst, slot, peer):
        copy = self.copy(src, dst, slot, peer)
        copy.start()
        self.sent += 1
        self.pending.append(copy)

    def arrive(self, dst, slot):
        pltpu.make_async_remote_copy(
            src_ref=dst,
            dst_ref=dst,
            send_sem=self.send_sems.at[0],
            recv_sem=self.recv_sems.at[slot],
            device_id=self.gy_peer(1),
            device_id_type=MESH,
        ).wait_recv()

    def drain(self):
        for copy in self.pending:
            copy.wait_send()


def far_first(count):
    order = list(range(1, count))
    return sorted(order, key=lambda k: -min(k, count - k))


class PlaneGather:
    def __init__(self, net, src, out):
        self.net, self.src, self.out = net, src, out
        self.gy_slot = net.block(net.gy)
        self.gx_slot = net.block(net.gx * net.gy)

    def start(self):
        self.start_gy()
        self.start_gx()

    def start_gy(self):
        net = self.net
        own = self.out(net.x, net.y)
        for k in range(1, net.gy):
            net.send(self.src, own, self.gy_slot + net.y, net.gy_peer(k))

    def start_gx(self):
        net = self.net
        own = self.out(net.x, net.y)
        for j in range(1, net.gx):
            net.send(self.src, own, self.gx_slot + net.x * net.gy + net.y, net.gx_peer(j))

    def relay(self, k):
        net = self.net
        row = net.at_gy(k)
        piece = self.out(net.x, row)
        net.arrive(piece, self.gy_slot + row)
        for j in range(1, net.gx):
            net.send(piece, piece, self.gx_slot + net.x * net.gy + row, net.gx_peer(j))

    def settle(self, j, k):
        net = self.net
        side, row = net.at_gx(j), net.at_gy(k)
        net.arrive(self.out(side, row), self.gx_slot + side * net.gy + row)


class Share:
    def __init__(self, net, out):
        self.net, self.out = net, out
        self.hop_slot = net.block(net.hops)
        self.core_slot = net.block(net.dp)

    def start(self, src):
        net = self.net
        own = self.out(net.d)
        for i in range(1, net.hops):
            net.send(src, own, self.hop_slot + net.hop, net.hop_peer(i))
        if net.cores == 2:
            net.send(src, own, self.core_slot + net.d, net.core_peer())

    def relay(self):
        net = self.net
        for i in range(1, net.hops):
            hop = net.at_hop(i)
            rank = hop * net.cores + net.core
            piece = self.out(rank)
            net.arrive(piece, self.hop_slot + hop)
            if net.cores == 2:
                net.send(piece, piece, self.core_slot + rank, net.core_peer())

    def settle(self):
        net = self.net
        if net.cores == 2:
            for hop in range(net.hops):
                rank = hop * net.cores + 1 - net.core
                net.arrive(self.out(rank), self.core_slot + rank)


class PlaneSum:
    def __init__(self, net, src, landing_x, stage, landing_y):
        self.net, self.src = net, src
        self.landing_x, self.stage, self.landing_y = landing_x, stage, landing_y
        self.gx_slot = net.block(net.gx * net.gy)
        self.gy_slot = net.block(net.gy)

    def start(self, k):
        net = self.net
        row = net.at_gy(k)
        for j in range(1, net.gx):
            net.send(
                self.src(net.at_gx(j), row),
                self.landing_x.at[net.x, row],
                self.gx_slot + net.x * net.gy + row,
                net.gx_peer(j),
            )

    def relay(self, k):
        net = self.net
        row = net.at_gy(k)
        total = self.src(net.x, row)[...].astype(F32)
        for j in range(1, net.gx):
            side = net.at_gx(j)
            net.arrive(self.landing_x.at[side, row], self.gx_slot + side * net.gy + row)
            total = total + self.landing_x[side, row].astype(F32)
        if k == 0:
            self.landing_y[net.y] = total.astype(self.landing_y.dtype)
        else:
            self.stage[row] = total.astype(self.stage.dtype)
            net.send(
                self.stage.at[row], self.landing_y.at[net.y], self.gy_slot + net.y, net.gy_peer(k)
            )

    def total(self):
        net = self.net
        for k in range(1, net.gy):
            row = net.at_gy(k)
            net.arrive(self.landing_y.at[row], self.gy_slot + row)
        total = self.landing_y[0].astype(F32)
        for row in range(1, net.gy):
            total = total + self.landing_y[row].astype(F32)
        return total


class TokenSum:
    def __init__(self, net, src, mine, landing_core, landing_hop, sems):
        self.net, self.src, self.mine, self.sems = net, src, mine, sems
        self.landing_core, self.landing_hop = landing_core, landing_hop
        self.core_slot = net.block(net.hops)
        self.hop_slot = net.block(net.hops)
        self.order = list(range(1, net.hops)) + [0]

    def fetch(self, n):
        net = self.net
        rank = net.at_hop(self.order[n]) * net.cores + net.core
        return pltpu.make_async_copy(self.src.at[rank], self.mine.at[n % 2], self.sems.at[n % 2])

    def start(self):
        net = self.net
        for n in range(min(2, net.hops)):
            self.fetch(n).start()
        for i in self.order:
            hop = net.at_hop(i)
            net.send(
                self.src.at[hop * net.cores + 1 - net.core], self.landing_core.at[hop],
                self.core_slot + hop, net.core_peer(),
            )

    def relay(self):
        net = self.net
        for n, i in enumerate(self.order):
            hop = net.at_hop(i)
            self.fetch(n).wait()
            net.arrive(self.landing_core.at[hop], self.core_slot + hop)
            if i > 0:
                total = self.mine[n % 2].astype(F32) + self.landing_core[hop].astype(F32)
                self.landing_core[hop] = total.astype(BF16)
                net.send(
                    self.landing_core.at[hop], self.landing_hop.at[net.hop],
                    self.hop_slot + net.hop, net.hop_peer(i),
                )
            if n + 2 < net.hops:
                self.fetch(n + 2).start()

    def total(self):
        net = self.net
        own = self.mine[(net.hops - 1) % 2].astype(F32)
        total = own + self.landing_core[net.hop].astype(F32)
        for i in range(1, net.hops):
            hop = net.at_hop(i)
            net.arrive(self.landing_hop.at[hop], self.hop_slot + hop)
            total = total + self.landing_hop[hop].astype(F32)
        return total


def call(kernel, sizes, number, name, out_shapes, out_specs, in_specs, scratch, sends, slots):
    def body(*refs):
        net = Net(sizes, refs[-2], refs[-1])
        kernel(net, *refs[:-2])
        net.drain()
        assert net.sent <= sends and net.slots <= slots, (net.sent, net.slots)

    return pl.pallas_call(
        body,
        name=name,
        out_shape=out_shapes,
        in_specs=in_specs,
        out_specs=out_specs,
        scratch_shapes=list(scratch)
        + [pltpu.SemaphoreType.DMA((sends,)), pltpu.SemaphoreType.DMA((slots,))],
        compiler_params=pltpu.CompilerParams(collective_id=number, has_side_effects=True),
    )


def local(copies):
    for copy in copies:
        copy.start()


def wait_local(copies):
    for copy in copies:
        copy.wait()


def gather_weights(sizes, att, gate_up):
    dp, gx, gy = sizes
    hops = dp // 2

    def kernel(net, att_ref, gu_ref, att_out, gu_out, sems):
        net.greet(net.plane_peers() + net.share_peers())
        att_plane = PlaneGather(net, att_ref, lambda a, b: att_out.at[a, b, net.d])
        gu_plane = PlaneGather(net, gu_ref, lambda a, b: gu_out.at[a, :, b])
        first_hop = net.block(gx * gy * net.hops)
        first_core = net.block(gx * gy * net.dp)

        def shared(a, b):
            item = Share.__new__(Share)
            item.net = net
            item.out = lambda rank: att_out.at[a, b, rank]
            place = a * gy + b
            item.hop_slot = first_hop + place * net.hops
            item.core_slot = first_core + place * net.dp
            return item

        own = [
            pltpu.make_async_copy(att_ref, att_out.at[net.x, net.y, net.d], sems.at[0]),
            pltpu.make_async_copy(gu_ref, gu_out.at[net.x, :, net.y], sems.at[1]),
        ]
        att_plane.start()
        shared(net.x, net.y).start(att_ref)
        gu_plane.start_gy()
        local(own)
        for k in range(1, gy):
            att_plane.relay(k)
            row = net.at_gy(k)
            shared(net.x, row).start(att_out.at[net.x, row, net.d])
        gu_plane.start_gx()
        for j in range(1, gx):
            for k in range(gy):
                att_plane.settle(j, k)
                side, row = net.at_gx(j), net.at_gy(k)
                shared(side, row).start(att_out.at[side, row, net.d])
        places = [(j, k) for j in range(gx) for k in range(gy)]
        for n, (j, k) in enumerate(places):
            shared(net.at_gx(j), net.at_gy(k)).relay()
            if n % 2 == 1 and n // 2 + 1 < gy:
                gu_plane.relay(n // 2 + 1)
        for j, k in places:
            shared(net.at_gx(j), net.at_gy(k)).settle()
        for j in range(1, gx):
            for k in range(gy):
                gu_plane.settle(j, k)
        wait_local(own)

    shapes = (
        jax.ShapeDtypeStruct((gx, gy, dp) + att.shape, BF16),
        jax.ShapeDtypeStruct((gx, 2, gy) + gate_up.shape[1:], BF16),
    )
    count = gx * gy * (hops + dp) + 2 * (gx * gy + gy)
    return call(
        kernel, sizes, 1, "gather_weights", shapes, [ANY] * 2, [VMEM] * 2,
        [pltpu.SemaphoreType.DMA((2,))], count, count,
    )(att, gate_up)


def turned(values):
    return jnp.transpose(values)


def head_rows(ref, first, lead=()):
    return jnp.concatenate(
        [ref[:, h * HEAD_WIDTH : (h + 1) * HEAD_WIDTH] for h in range(first, first + GROUPS)], axis=0
    )


def key_columns(ref, place):
    columns = ref[:, :, :, place * HEAD_WIDTH : (place + 1) * HEAD_WIDTH]
    return columns.reshape(-1, HEAD_WIDTH)


def put_heads(ref, first, rows, values):
    for n in range(GROUPS):
        lanes = slice((first + n) * HEAD_WIDTH, (first + n + 1) * HEAD_WIDTH)
        ref[:, lanes] = values[n * rows : (n + 1) * rows].astype(ref.dtype)


def attend_heads(key_heads, q_ref, kv_ref, bias_ref, mixed_ref, logsum_ref):
    rows = q_ref.shape[0]
    bias = jnp.concatenate([bias_ref[...]] * GROUPS, axis=1)
    for k in key_heads:
        query = head_rows(q_ref, k * GROUPS)
        scores = back_product(key_columns(kv_ref, k), query) * HEAD_WIDTH ** (-0.5) + bias
        highest = jnp.max(scores, axis=0, keepdims=True)
        weights = jnp.exp(scores - highest)
        sums = jnp.sum(weights, axis=0, keepdims=True)
        logsum_ref[k : k + 1, :] = highest + jnp.log(sums)
        probs = (weights * (1.0 / sums)).astype(BF16)
        mixed = weight_product(key_columns(kv_ref, KEY_VALUE_HEADS + k), probs)
        put_heads(mixed_ref, k * GROUPS, rows, turned(mixed))


def attend_heads_back(q_ref, kv_ref, bias_ref, logsum_ref, mixed_ref, dmixed_ref, dq_ref, dkv_ref):
    rows = q_ref.shape[0]
    bias = jnp.concatenate([bias_ref[...]] * GROUPS, axis=1)
    blocks = kv_ref.shape[:3]
    for k in range(KEY_VALUE_HEADS):
        query = head_rows(q_ref, k * GROUPS)
        mixed = head_rows(mixed_ref, k * GROUPS)
        dmixed = head_rows(dmixed_ref, k * GROUPS)
        keys = key_columns(kv_ref, k)
        scores = back_product(keys, query) * HEAD_WIDTH ** (-0.5) + bias
        weights = jnp.exp(scores - logsum_ref[k : k + 1, :])
        delta = jnp.sum(turned(mixed.astype(F32) * dmixed.astype(F32)), axis=0, keepdims=True)
        dprobs = back_product(key_columns(kv_ref, KEY_VALUE_HEADS + k), dmixed)
        dscores = (weights * (dprobs - delta)).astype(BF16)
        dquery = weight_product(keys, dscores) * HEAD_WIDTH ** (-0.5)
        put_heads(dq_ref, k * GROUPS, rows, turned(dquery))
        dkeys = plain_product(dscores, query) * HEAD_WIDTH ** (-0.5)
        dvalues = plain_product(weights.astype(BF16), dmixed)
        lanes = slice(k * HEAD_WIDTH, (k + 1) * HEAD_WIDTH)
        dkv_ref[:, :, :, lanes] = dkeys.astype(BF16).reshape(blocks + (HEAD_WIDTH,))
        place = KEY_VALUE_HEADS + k
        lanes = slice(place * HEAD_WIDTH, (place + 1) * HEAD_WIDTH)
        dkv_ref[:, :, :, lanes] = dvalues.astype(BF16).reshape(blocks + (HEAD_WIDTH,))


def turn_pairs(values, cos, sin):
    lanes = cos.shape[1]
    half = HEAD_WIDTH // 2
    front = lax.broadcasted_iota(jnp.int32, cos.shape, 1) % HEAD_WIDTH < half
    pieces = []
    for first in range(0, values.shape[1], lanes):
        part = values[:, first : first + lanes]
        other = jnp.where(front, pltpu.roll(part, lanes - half, 1), pltpu.roll(part, half, 1))
        pieces.append(part * cos + other * sin)
    return jnp.concatenate(pieces, axis=1)


def forward(sizes, cols, att, normed, inputs, gain, cos, sin, bias, down, cot):
    dp, gx, gy = sizes
    q_cols, k_cols, v_cols, o_cols = cols
    qkv_cols = q_cols + k_cols + v_cols
    rows, width = inputs.shape
    fan = att.shape[3]
    lanes = cos.shape[1]
    q_width, k_width, v_width = gy * q_cols, gy * k_cols, gy * v_cols
    q_pad, k_pad = -(-q_width // lanes) * lanes, -(-k_width // lanes) * lanes

    def kernel(
        net, att_ref, nm_ref, in_ref, gain_ref, cos_ref, sin_ref, bias_ref, dn_ref, cot_ref,
        q_ref, kv_out, mixed_ref, logsum_ref, hidden_ref,
        dn_out, cot_out, nm_out, mixed_out, two_out,
        q_wide, k_wide, kv_ref, two_ref, sems,
    ):
        q_wide[...] = jnp.zeros_like(q_wide)
        k_wide[...] = jnp.zeros_like(k_wide)
        for b in range(gy):
            block = sum(
                back_product(nm_ref[:, a * fan : (a + 1) * fan], att_ref[a, b, :qkv_cols, :])
                for a in range(gx)
            ).astype(BF16)
            q_wide[:, b * q_cols : (b + 1) * q_cols] = block[:, :q_cols].astype(F32)
            k_wide[:, b * k_cols : (b + 1) * k_cols] = block[:, q_cols : q_cols + k_cols].astype(F32)
            first = k_width + b * v_cols
            kv_ref[:, first : first + v_cols] = block[:, q_cols + k_cols :]
        cos_rows, sin_rows = cos_ref[...], sin_ref[...]
        kv_ref[:, :k_width] = turn_pairs(k_wide[...], cos_rows, sin_rows)[:, :k_width].astype(BF16)

        net.greet(net.plane_peers() + net.share_peers())
        kv = PlaneGather(net, kv_ref, lambda a, b: kv_out.at[a, b])
        dn = PlaneGather(net, dn_ref, lambda a, b: dn_out.at[a, b])
        cot_share, nm_share, mixed_share, two_share = (
            Share(net, lambda r, out=out: out.at[r]) for out in (cot_out, nm_out, mixed_out, two_out)
        )
        own = [
            pltpu.make_async_copy(kv_ref, kv_out.at[net.x, net.y], sems.at[0]),
            pltpu.make_async_copy(dn_ref, dn_out.at[net.x, net.y], sems.at[2]),
            pltpu.make_async_copy(cot_ref, cot_out.at[net.d], sems.at[3]),
            pltpu.make_async_copy(nm_ref, nm_out.at[net.d], sems.at[4]),
        ]
        kv.start()
        dn.start_gy()
        local(own)
        cot_share.start(cot_ref)
        nm_share.start(nm_ref)
        q_ref[...] = turn_pairs(q_wide[...], cos_rows, sin_rows)[:, :q_width].astype(BF16)
        for k in range(1, gy):
            kv.relay(k)
        dn.start_gx()
        for j in range(1, gx):
            for k in range(gy):
                kv.settle(j, k)
        wait_local(own)

        turns = list(range(1, gy))
        heads = list(range(KEY_VALUE_HEADS))
        for n, k in enumerate(turns):
            mine = heads[n * len(heads) // len(turns) : (n + 1) * len(heads) // len(turns)]
            attend_heads(mine, q_ref, kv_out, bias_ref, mixed_ref, logsum_ref)
            if n + 1 < len(turns):
                dn.relay(k)
        last = pltpu.make_async_copy(mixed_ref, mixed_out.at[net.d], sems.at[5])
        last.start()
        mixed_share.start(mixed_ref)
        for b in range(gy):
            block = sum(
                back_product(mixed_ref[:, a * fan : (a + 1) * fan], att_ref[a, b, qkv_cols:, :])
                for a in range(gx)
            ).astype(BF16)
            span = slice(b * o_cols, (b + 1) * o_cols)
            hidden_ref[:, span] = in_ref[:, span].astype(F32) + block.astype(F32)
        hidden = hidden_ref[...]
        scale = lax.rsqrt(jnp.sum(hidden * hidden, axis=1, keepdims=True) / width + EPSILON)
        two_ref[...] = (hidden * scale * gain_ref[...]).astype(BF16)
        local_two = pltpu.make_async_copy(two_ref, two_out.at[net.d], sems.at[6])
        local_two.start()
        two_share.start(two_ref)
        dn.relay(turns[-1])
        shares = (cot_share, nm_share, mixed_share, two_share)
        for share in shares:
            share.relay()
        for share in shares:
            share.settle()
        for j in range(1, gx):
            for k in range(gy):
                dn.settle(j, k)
        wait_local([last, local_two])

    shared = jax.ShapeDtypeStruct((dp,) + inputs.shape, BF16)
    shapes = (
        jax.ShapeDtypeStruct((rows, q_width), BF16),
        jax.ShapeDtypeStruct((gx, gy, rows, k_width + v_width), BF16),
        jax.ShapeDtypeStruct((rows, q_width), BF16),
        jax.ShapeDtypeStruct((KEY_VALUE_HEADS, GROUPS * rows), F32),
        jax.ShapeDtypeStruct(inputs.shape, F32),
        jax.ShapeDtypeStruct((gx, gy) + down.shape, BF16),
        shared, shared, shared, shared,
    )
    scratch = [
        pltpu.VMEM((rows, q_pad), F32),
        pltpu.VMEM((rows, k_pad), F32),
        pltpu.VMEM((rows, k_width + v_width), BF16),
        pltpu.VMEM(inputs.shape, BF16),
        pltpu.SemaphoreType.DMA((7,)),
    ]
    count = 3 * (gx * gy + gy) + 4 * 2 * dp
    return call(
        kernel, sizes, 2, "forward", shapes, [VMEM] * 5 + [ANY] * 5, [VMEM] * 9, scratch, count, count,
    )(att, normed, inputs, gain, cos, sin, bias, down, cot)


def mlp(normed_all, cot_all, gate_up, down):
    gx, both, fan = gate_up.shape
    rows, width = normed_all.shape
    hidden = both // 2
    part = down.shape[2]
    step = rows // 2 if rows % 32 == 0 else rows

    def kernel(n_ref, c_ref, gu_ref, dt_ref, dn_ref, mo_ref, gg_ref, dg_ref, act_ref, delta_ref):
        def tokens(i, carry):
            span = pl.ds(pl.multiple_of(i * step, step), step)
            normed, cot = n_ref[span, :], c_ref[span, :]
            gate_up_rows = sum(
                back_product(normed[:, a * fan : (a + 1) * fan], gu_ref[a]) for a in range(gx)
            ).astype(BF16)
            gate = gate_up_rows[:, :hidden].astype(F32)
            up = gate_up_rows[:, hidden:].astype(F32)
            dact = jnp.concatenate([plain_product(cot, dt_ref[a]) for a in range(gx)], axis=1)
            sigmoid = jax.nn.sigmoid(gate)
            act = (gate * sigmoid * up).astype(BF16)
            gate_delta = (dact * up * sigmoid * (1.0 + gate * (1.0 - sigmoid))).astype(BF16)
            up_delta = (dact * gate * sigmoid).astype(BF16)
            deltas = jnp.concatenate([gate_delta, up_delta], axis=1)
            delta_ref[span, :] = deltas
            for a in range(gx):
                act_ref[a, span, :] = act[:, a * part : (a + 1) * part]
                dn_ref[span, a * fan : (a + 1) * fan] = plain_product(deltas, gu_ref[a]).astype(BF16)
            mo_ref[span, :] = sum(
                back_product(act[:, a * part : (a + 1) * part], dt_ref[a]) for a in range(gx)
            ).astype(BF16)
            return carry

        lax.fori_loop(0, rows // step, tokens, 0)
        for a in range(gx):
            gg_ref[a] = weight_product(delta_ref[...], n_ref[:, a * fan : (a + 1) * fan]).astype(BF16)
            dg_ref[a] = weight_product(c_ref[...], act_ref[a]).astype(BF16)

    return pl.pallas_call(
        kernel,
        name="mlp",
        out_shape=(
            jax.ShapeDtypeStruct(normed_all.shape, BF16),
            jax.ShapeDtypeStruct(normed_all.shape, BF16),
            jax.ShapeDtypeStruct(gate_up.shape, BF16),
            jax.ShapeDtypeStruct(down.shape, BF16),
        ),
        in_specs=[VMEM] * 4,
        out_specs=[VMEM] * 4,
        scratch_shapes=[pltpu.VMEM((gx, rows, part), BF16), pltpu.VMEM((rows, both), BF16)],
    )(normed_all, cot_all, gate_up, down)


def backward(
    sizes, cols, query, kv_all, bias, logsum, mixed, dnormed_part, mlp_part, hidden, cot, att, normed_all,
    mixed_all, inputs, gain, mlp_gain, cos, sin, gate_up, down,
):
    dp, gx, gy = sizes
    q_cols, k_cols, v_cols, o_cols = cols
    qkv_cols = q_cols + k_cols + v_cols
    all_cols = qkv_cols + o_cols
    att_share = all_cols // dp
    rows, width = inputs.shape
    fan = att.shape[3]
    lanes = cos.shape[1]
    q_width, k_width = gy * q_cols, gy * k_cols
    q_pad, k_pad = -(-q_width // lanes) * lanes, -(-k_width // lanes) * lanes
    kv_width = kv_all.shape[3]
    pieces = [
        (gate_up.shape[3:], BF16), (gate_up.shape[3:], BF16), (down.shape[2:], BF16),
        ((att_share, fan), BF16), ((8, width), F32), ((rows, kv_width), BF16),
    ]
    count = len(pieces)

    def kernel(net, *refs):
        (
            q_ref, kv_ref, bias_ref, logsum_ref, mixed_ref, two_ref, mo_ref, hidden_ref, cot_ref, att_ref,
            nm_ref, mx_ref, in_ref, gain_ref, two_gain_ref, cos_ref, sin_ref, gu_ref, dn_ref,
        ) = refs[:19]
        layer_out, input_grad, gu_out, dn_out, att_out, gain_out = refs[19:25]
        q_wide, k_wide, dkv_ref, p_ref, trade_src, trade_in, dn_one, att_grad, gains = refs[25:34]
        dmixed_ref, dhidden_ref = refs[34:36]
        two_scratch, mo_scratch = refs[36:40], refs[40:44]
        refs = refs[44:]
        landing_x, stage, landing_y = (refs[n * count : (n + 1) * count] for n in range(3))
        result, sems = refs[3 * count : 4 * count - 1], refs[4 * count - 1]

        net.greet(net.plane_peers() + [net.dp_peer(i) for i in range(1, dp)])
        sources = [
            lambda a, b: gu_ref.at[a, 0, b], lambda a, b: gu_ref.at[a, 1, b], lambda a, b: dn_ref.at[a, b],
            lambda a, b: att_grad.at[a, b], lambda a, b: gains, lambda a, b: dkv_ref.at[a, b],
        ]
        sums = [
            PlaneSum(net, sources[n], landing_x[n], stage[n], landing_y[n]) for n in range(count)
        ]
        outs = [
            lambda r: gu_out.at[r, 0], lambda r: gu_out.at[r, 1], lambda r: dn_out.at[r],
            lambda r: att_out.at[r], lambda r: gain_out.at[r],
        ]
        shares = [Share(net, out) for out in outs]
        mlp_sums, att_sums, dkv_sum = sums[:3], sums[3:5], sums[5]
        order = far_first(gy) + [0]

        def begin(items, turns):
            for k in turns:
                for item in items:
                    item.start(k)

        def relay(items, turns):
            for k in turns:
                for item in items:
                    item.relay(k)

        own = []

        def finish(first, items):
            for n, item in enumerate(items, first):
                result[n][...] = item.total().astype(result[n].dtype)
                shares[n].start(result[n])
                own.append(pltpu.make_async_copy(result[n], shares[n].out(net.d), sems.at[n]))
                own[-1].start()

        two_sum, mo_sum = TokenSum(net, two_ref, *two_scratch), TokenSum(net, mo_ref, *mo_scratch)
        two_sum.start()
        begin(mlp_sums, order[:2])
        two_sum.relay()
        mo_sum.start()
        hidden = hidden_ref[...]
        rms_two = lax.rsqrt(jnp.sum(hidden * hidden, axis=1, keepdims=True) / width + EPSILON)
        unit_two = hidden * rms_two
        dnormed_two = two_sum.total()
        scaled_two = dnormed_two * two_gain_ref[...]
        level_two = jnp.sum(scaled_two * unit_two, axis=1, keepdims=True) / width
        dhidden_ref[...] = cot_ref[...].astype(F32) + rms_two * (scaled_two - unit_two * level_two)
        gains[...] = jnp.zeros_like(gains)
        gains[1:2, :] = jnp.sum(dnormed_two * unit_two, axis=0, keepdims=True)
        mo_sum.relay()
        dhidden_bf = dhidden_ref[...].astype(BF16)
        for a in range(gx):
            dmixed_ref[:, a * fan : (a + 1) * fan] = sum(
                plain_product(dhidden_bf[:, b * o_cols : (b + 1) * o_cols], att_ref[a, b, qkv_cols:, :])
                for b in range(gy)
            ).astype(BF16)
        relay(mlp_sums, order[:1])
        q_wide[...] = jnp.zeros_like(q_wide)
        k_wide[...] = jnp.zeros_like(k_wide)
        attend_heads_back(
            q_ref, kv_ref, bias_ref, logsum_ref, mixed_ref, dmixed_ref, q_wide, dkv_ref
        )
        begin([dkv_sum], order)
        begin(mlp_sums, order[2:3])
        relay(mlp_sums, order[1:2])
        layer_out[...] = (hidden_ref[...] + mo_sum.total()).astype(BF16)
        relay([dkv_sum], order)
        begin(mlp_sums, order[3:])
        cos_rows, sin_rows = cos_ref[...], -sin_ref[...]
        dquery = turn_pairs(q_wide[...], cos_rows, sin_rows)[:, :q_width].astype(BF16)
        dhidden = dhidden_ref[...]
        for b in range(gy):
            p_ref[b, :, :q_cols] = dquery[:, b * q_cols : (b + 1) * q_cols]
            p_ref[b, :, qkv_cols:] = dhidden_bf[:, b * o_cols : (b + 1) * o_cols]
        dkv = dkv_sum.total()
        k_wide[:, :k_width] = dkv[:, :k_width]
        dkey = turn_pairs(k_wide[...], cos_rows, sin_rows)[:, :k_width].astype(BF16)
        dvalue = dkv[:, k_width:].astype(BF16)
        for b in range(gy):
            p_ref[b, :, q_cols : q_cols + k_cols] = dkey[:, b * k_cols : (b + 1) * k_cols]
            p_ref[b, :, q_cols + k_cols : qkv_cols] = dvalue[:, b * v_cols : (b + 1) * v_cols]
        for r in range(dp):
            for b in range(gy):
                trade_src[r, :, b * att_share : (b + 1) * att_share] = p_ref[
                    b, :, r * att_share : (r + 1) * att_share
                ]
        trade_slot = net.block(dp)
        for i in range(1, dp):
            rank = lax.rem(net.d + i, dp)
            net.send(trade_src.at[rank], trade_in.at[net.d], trade_slot + net.d, net.dp_peer(i))
        trade_in[net.d] = trade_src[net.d]
        relay(mlp_sums, order[2:3])

        for a in range(gx):
            dn_one[:, a * fan : (a + 1) * fan] = sum(
                plain_product(p_ref[b, :, :qkv_cols], att_ref[a, b, :qkv_cols, :]) for b in range(gy)
            )
        dnormed = dn_one[...]
        values = in_ref[...].astype(F32)
        rms = lax.rsqrt(jnp.sum(values * values, axis=1, keepdims=True) / width + EPSILON)
        unit = values * rms
        scaled = dnormed * gain_ref[...]
        level = jnp.sum(scaled * unit, axis=1, keepdims=True) / width
        input_grad[...] = (dhidden + rms * (scaled - unit * level)).astype(BF16)
        gains[0:1, :] = jnp.sum(dnormed * unit, axis=0, keepdims=True)

        for i in range(1, dp):
            rank = lax.rem(net.d + i, dp)
            net.arrive(trade_in.at[rank], trade_slot + rank)
        dall = trade_in[...].reshape(dp * rows, gy * att_share)
        places = lax.broadcasted_iota(jnp.int32, (gy * att_share, fan), 0) % att_share
        from_normed = places + net.d * att_share < qkv_cols
        for a in range(gx):
            span = slice(a * fan, (a + 1) * fan)
            grad = jnp.where(
                from_normed,
                weight_product(dall, nm_ref[:, span]),
                weight_product(dall, mx_ref[:, span]),
            ).astype(BF16)
            for b in range(gy):
                att_grad[a, b] = grad[b * att_share : (b + 1) * att_share]
        begin(att_sums, order)
        relay(mlp_sums, order[3:])
        finish(0, mlp_sums)
        relay(att_sums, order)
        finish(3, att_sums)
        for share in shares:
            share.relay()
        for share in shares:
            share.settle()
        wait_local(own)

    shapes = (
        jax.ShapeDtypeStruct(inputs.shape, BF16),
        jax.ShapeDtypeStruct(inputs.shape, BF16),
        jax.ShapeDtypeStruct((dp, 2) + pieces[0][0], BF16),
        jax.ShapeDtypeStruct((dp,) + pieces[2][0], BF16),
        jax.ShapeDtypeStruct((dp,) + pieces[3][0], BF16),
        jax.ShapeDtypeStruct((dp,) + pieces[4][0], F32),
    )
    scratch = [
        pltpu.VMEM((rows, q_pad), F32),
        pltpu.VMEM((rows, k_pad), F32),
        pltpu.VMEM(kv_all.shape, BF16),
        pltpu.VMEM((gy, rows, all_cols), BF16),
        pltpu.VMEM((dp, rows, gy * att_share), BF16),
        pltpu.VMEM((dp, rows, gy * att_share), BF16),
        pltpu.VMEM((rows, width), F32),
        pltpu.VMEM((gx, gy, att_share, fan), BF16),
        pltpu.VMEM((8, width), F32),
        pltpu.VMEM((rows, width), BF16),
        pltpu.VMEM((rows, width), F32),
    ]
    slab = pltpu.VMEM((dp // 2, rows, width), BF16)
    scratch += [pltpu.VMEM((2, rows, width), BF16), slab, slab, pltpu.SemaphoreType.DMA((2,))] * 2
    scratch += [pltpu.VMEM((gx, gy) + p, t) for p, t in pieces]
    scratch += [pltpu.VMEM((gy,) + p, t) for p, t in pieces] * 2
    scratch += [pltpu.VMEM(p, t) for p, t in pieces[:-1]]
    scratch += [pltpu.SemaphoreType.DMA((count - 1,))]
    sems = count * (gx * gy + gy) + (count - 1) * 2 * dp + 3 * dp
    return call(
        kernel, sizes, 5, "backward", shapes, [VMEM] * 2 + [ANY] * 4, [VMEM] * 5 + [ANY] * 2 + [VMEM] * 12, scratch, sems, sems,
    )(
        query, kv_all, bias, logsum, mixed, dnormed_part, mlp_part, hidden, cot, att, normed_all,
        mixed_all, inputs, gain, mlp_gain, cos, sin, gate_up, down,
    )


def rope_angles(positions):
    half_dim = HEAD_WIDTH // 2
    inverse = THETA ** (-(jnp.arange(half_dim, dtype=F32) * 2.0 / HEAD_WIDTH))
    angles = positions[:, None] * inverse[None, :]
    return (jnp.cos(angles)[:, None, :], jnp.sin(angles)[:, None, :])


def normalize(values, gain):
    rms_rows = lax.rsqrt(jnp.mean(values * values, axis=1, keepdims=True) + EPSILON)
    unit_rows = values * rms_rows
    return (rms_rows, unit_rows, (unit_rows * gain).astype(BF16))


def on_device(
    sizes,
    inputs,
    segments,
    attn_gain,
    query_weight,
    key_weight,
    value_weight,
    output_weight,
    mlp_gain,
    gate_weight,
    up_weight,
    down_weight,
    cotangent,
):
    dp, gx, gy = sizes
    count_of_rows, width = inputs.shape
    rank = lax.axis_index("dp")
    begin_row = (lax.axis_index("gx") * gy + lax.axis_index("gy")) * count_of_rows
    seq_begin = begin_row // SEQUENCE_LENGTH * SEQUENCE_LENGTH
    local_places = begin_row - seq_begin + jnp.arange(count_of_rows)
    cos_table, sin_table = rope_angles(local_places.astype(F32))
    query_segs = lax.dynamic_slice_in_dim(segments, begin_row, count_of_rows, 0)
    allowed = (jnp.arange(SEQUENCE_LENGTH)[:, None] <= local_places[None, :]) & (
        query_segs[None, :] == segments[:, None]
    )
    bias = jnp.where(allowed, 0.0, MASKED).astype(F32)
    residual = inputs.astype(F32)
    _, _, normed_one = normalize(residual, attn_gain)

    fan = query_weight.shape[0]
    q_cols, k_cols, v_cols = query_weight.shape[1], key_weight.shape[1], value_weight.shape[1]
    o_cols = output_weight.shape[1]
    qkv_cols = q_cols + k_cols + v_cols
    all_cols = qkv_cols + o_cols
    att_share = all_cols // dp
    packed = jnp.concatenate([query_weight, key_weight, value_weight, output_weight], axis=1).T
    att_part = lax.dynamic_slice_in_dim(packed, rank * att_share, att_share, 0)
    share = gate_weight.shape[1] // dp
    groups = gy // gx
    gate_up_part = jnp.stack(
        [
            lax.dynamic_slice_in_dim(gate_weight, rank * share, share, 1).T,
            lax.dynamic_slice_in_dim(up_weight, rank * share, share, 1).T,
        ]
    )
    down_cols = down_weight.shape[1]
    down_part = lax.dynamic_slice_in_dim(
        down_weight.reshape(groups, dp, share, down_cols), rank, 1, 1
    ).reshape(groups * share, down_cols).T

    att_all, gate_up_all = gather_weights(sizes, att_part, gate_up_part)
    att_all = att_all.reshape(gx, gy, all_cols, fan)
    cos_wide = jnp.tile(cos_table[:, 0], (1, 4))
    sin_wide = jnp.tile(jnp.concatenate([-sin_table[:, 0], sin_table[:, 0]], axis=1), (1, 2))
    (
        rotated_query, kv_all, attention_mixture, logsum, hidden,
        down_all, cot_all, normed_one_all, mixed_all, normed_all,
    ) = forward(
        sizes, (q_cols, k_cols, v_cols, o_cols), att_all, normed_one, inputs, mlp_gain.reshape(1, -1),
        cos_wide, sin_wide, bias, down_part, cotangent,
    )
    hidden_width = gy * share
    gate_up_all = gate_up_all.reshape(gx, 2 * hidden_width, fan)
    half_hidden = groups * share
    down_all = down_all.reshape(gx, gy * down_cols, half_hidden)
    cot_all, normed_one_all, mixed_all, normed_all = (
        rows.reshape(dp * count_of_rows, width) for rows in (cot_all, normed_one_all, mixed_all, normed_all)
    )
    dnormed_part, mlp_part, gate_up_grad, down_grad = mlp(normed_all, cot_all, gate_up_all, down_all)
    gate_up_grad = gate_up_grad.reshape(gx, 2, gy, share, fan)
    down_grad = down_grad.reshape(gx, gy, down_cols, half_hidden)

    layer_out, input_grad, gate_up_sum, down_sum, att_sum, gain_sum = backward(
        sizes, (q_cols, k_cols, v_cols, o_cols), rotated_query, kv_all, bias, logsum, attention_mixture,
        dnormed_part.reshape(dp, count_of_rows, width), mlp_part.reshape(dp, count_of_rows, width),
        hidden, cotangent, att_all, normed_one_all, mixed_all, inputs, attn_gain.reshape(1, -1),
        mlp_gain.reshape(1, -1), cos_wide, sin_wide, gate_up_grad, down_grad,
    )
    gate_grad = gate_up_sum[:, 0].reshape(dp * share, fan).T.astype(F32)
    up_grad = gate_up_sum[:, 1].reshape(dp * share, fan).T.astype(F32)
    down_grad = (
        down_sum.reshape(dp, down_cols, groups, share)
        .transpose(2, 0, 3, 1)
        .reshape(down_weight.shape)
        .astype(F32)
    )
    att_sum = att_sum.reshape(all_cols, fan).T.astype(F32)
    gains = jnp.sum(gain_sum, axis=0)
    return (
        layer_out,
        input_grad,
        att_sum[:, :q_cols],
        att_sum[:, q_cols : q_cols + k_cols],
        att_sum[:, q_cols + k_cols : qkv_cols],
        att_sum[:, qkv_cols:],
        gate_grad,
        up_grad,
        down_grad,
        gains[0],
        gains[1],
    )


def solution(mesh):
    sizes = (mesh.shape["dp"], mesh.shape["gx"], mesh.shape["gy"])
    tokens = P(("dp", "gx", "gy"), None)
    block = P("gx", "gy")
    return jax.shard_map(
        functools.partial(on_device, sizes),
        mesh=mesh,
        in_specs=(tokens, P("dp"), P(), block, block, block, block, P(), block, block, block, tokens),
        out_specs=(tokens, tokens) + (block,) * 7 + (P(), P()),
        check_vma=False,
    )
```

```python
import functools

import jax
import jax.numpy as jnp
from jax import lax
from jax.experimental import pallas as pl
from jax.experimental.pallas import tpu as pltpu
from jax.sharding import PartitionSpec as P

QUERY_HEADS = 15
KEY_VALUE_HEADS = 5
GROUPS = QUERY_HEADS // KEY_VALUE_HEADS
HEAD_WIDTH = 64
SEQUENCE_LENGTH = 1024

THETA = 100000.0
EPSILON = 1e-05
MASKED = -1e30

F32 = jnp.float32
BF16 = jnp.bfloat16
MESH = pl.DeviceIdType.MESH
ANY = pl.BlockSpec(memory_space=pl.ANY)
VMEM = pl.BlockSpec(memory_space=pltpu.VMEM)


def plain_product(left, right):
    return jnp.dot(left, right, preferred_element_type=F32)


def weight_product(left, right):
    return lax.dot_general(left, right, (((0,), (0,)), ((), ())), preferred_element_type=F32)


def back_product(left, right):
    return lax.dot_general(left, right, (((1,), (1,)), ((), ())), preferred_element_type=F32)


class Net:
    def __init__(self, sizes, send_sems, recv_sems):
        self.dp, self.gx, self.gy = sizes
        self.cores = 2 if self.dp % 2 == 0 else 1
        self.hops = self.dp // self.cores
        self.d = lax.axis_index("dp")
        self.x = lax.axis_index("gx")
        self.y = lax.axis_index("gy")
        self.core = lax.rem(self.d, self.cores)
        self.hop = self.d // self.cores
        self.send_sems, self.recv_sems = send_sems, recv_sems
        self.sent, self.slots, self.pending = 0, 0, []

    def at_gx(self, j):
        return lax.rem(self.x + j, self.gx)

    def at_gy(self, k):
        return lax.rem(self.y + k, self.gy)

    def at_hop(self, i):
        return lax.rem(self.hop + i, self.hops)

    def gx_peer(self, j):
        return {"gx": self.at_gx(j)}

    def gy_peer(self, k):
        return {"gy": self.at_gy(k)}

    def hop_peer(self, i):
        return {"dp": self.at_hop(i) * self.cores + self.core}

    def core_peer(self):
        return {"dp": self.hop * self.cores + 1 - self.core}

    def dp_peer(self, i):
        return {"dp": lax.rem(self.d + i, self.dp)}

    def plane_peers(self):
        return [self.gx_peer(j) for j in range(1, self.gx)] + [
            self.gy_peer(k) for k in range(1, self.gy)
        ]

    def share_peers(self):
        peers = [self.hop_peer(i) for i in range(1, self.hops)]
        return peers + ([self.core_peer()] if self.cores == 2 else [])

    def greet(self, peers):
        barrier = pltpu.get_barrier_semaphore()
        for peer in peers:
            pl.semaphore_signal(barrier, inc=1, device_id=peer, device_id_type=MESH)
        pl.semaphore_wait(barrier, len(peers))

    def block(self, count):
        first = self.slots
        self.slots += count
        return first

    def copy(self, src, dst, slot, peer):
        return pltpu.make_async_remote_copy(
            src_ref=src,
            dst_ref=dst,
            send_sem=self.send_sems.at[self.sent],
            recv_sem=self.recv_sems.at[slot],
            device_id=peer,
            device_id_type=MESH,
        )

    def send(self, src, dst, slot, peer):
        copy = self.copy(src, dst, slot, peer)
        copy.start()
        self.sent += 1
        self.pending.append(copy)

    def arrive(self, dst, slot):
        pltpu.make_async_remote_copy(
            src_ref=dst,
            dst_ref=dst,
            send_sem=self.send_sems.at[0],
            recv_sem=self.recv_sems.at[slot],
            device_id=self.gy_peer(1),
            device_id_type=MESH,
        ).wait_recv()

    def drain(self):
        for copy in self.pending:
            copy.wait_send()


def far_first(count):
    order = list(range(1, count))
    return sorted(order, key=lambda k: -min(k, count - k))


class PlaneGather:
    def __init__(self, net, src, out):
        self.net, self.src, self.out = net, src, out
        self.gy_slot = net.block(net.gy)
        self.gx_slot = net.block(net.gx * net.gy)

    def start(self):
        self.start_gy()
        self.start_gx()

    def start_gy(self):
        net = self.net
        own = self.out(net.x, net.y)
        for k in range(1, net.gy):
            net.send(self.src, own, self.gy_slot + net.y, net.gy_peer(k))

    def start_gx(self):
        net = self.net
        own = self.out(net.x, net.y)
        for j in range(1, net.gx):
            net.send(self.src, own, self.gx_slot + net.x * net.gy + net.y, net.gx_peer(j))

    def relay(self, k):
        net = self.net
        row = net.at_gy(k)
        piece = self.out(net.x, row)
        net.arrive(piece, self.gy_slot + row)
        for j in range(1, net.gx):
            net.send(piece, piece, self.gx_slot + net.x * net.gy + row, net.gx_peer(j))

    def settle(self, j, k):
        net = self.net
        side, row = net.at_gx(j), net.at_gy(k)
        net.arrive(self.out(side, row), self.gx_slot + side * net.gy + row)


class Share:
    def __init__(self, net, out):
        self.net, self.out = net, out
        self.hop_slot = net.block(net.hops)
        self.core_slot = net.block(net.dp)

    def start(self, src):
        net = self.net
        own = self.out(net.d)
        for i in range(1, net.hops):
            net.send(src, own, self.hop_slot + net.hop, net.hop_peer(i))
        if net.cores == 2:
            net.send(src, own, self.core_slot + net.d, net.core_peer())

    def relay(self):
        net = self.net
        for i in range(1, net.hops):
            hop = net.at_hop(i)
            rank = hop * net.cores + net.core
            piece = self.out(rank)
            net.arrive(piece, self.hop_slot + hop)
            if net.cores == 2:
                net.send(piece, piece, self.core_slot + rank, net.core_peer())

    def settle(self):
        net = self.net
        if net.cores == 2:
            for hop in range(net.hops):
                rank = hop * net.cores + 1 - net.core
                net.arrive(self.out(rank), self.core_slot + rank)


class PlaneSum:
    def __init__(self, net, src, landing_x, stage, landing_y):
        self.net, self.src = net, src
        self.landing_x, self.stage, self.landing_y = landing_x, stage, landing_y
        self.gx_slot = net.block(net.gx * net.gy)
        self.gy_slot = net.block(net.gy)

    def start(self, k):
        net = self.net
        row = net.at_gy(k)
        for j in range(1, net.gx):
            net.send(
                self.src(net.at_gx(j), row),
                self.landing_x.at[net.x, row],
                self.gx_slot + net.x * net.gy + row,
                net.gx_peer(j),
            )

    def relay(self, k):
        net = self.net
        row = net.at_gy(k)
        total = self.src(net.x, row)[...].astype(F32)
        for j in range(1, net.gx):
            side = net.at_gx(j)
            net.arrive(self.landing_x.at[side, row], self.gx_slot + side * net.gy + row)
            total = total + self.landing_x[side, row].astype(F32)
        if k == 0:
            self.landing_y[net.y] = total.astype(self.landing_y.dtype)
        else:
            self.stage[row] = total.astype(self.stage.dtype)
            net.send(
                self.stage.at[row], self.landing_y.at[net.y], self.gy_slot + net.y, net.gy_peer(k)
            )

    def total(self):
        net = self.net
        for k in range(1, net.gy):
            row = net.at_gy(k)
            net.arrive(self.landing_y.at[row], self.gy_slot + row)
        total = self.landing_y[0].astype(F32)
        for row in range(1, net.gy):
            total = total + self.landing_y[row].astype(F32)
        return total


class TokenSum:
    def __init__(self, net, src, mine, landing_core, landing_hop, sems):
        self.net, self.src, self.mine, self.sems = net, src, mine, sems
        self.landing_core, self.landing_hop = landing_core, landing_hop
        self.core_slot = net.block(net.hops)
        self.hop_slot = net.block(net.hops)
        self.order = list(range(1, net.hops)) + [0]

    def fetch(self, n):
        net = self.net
        rank = net.at_hop(self.order[n]) * net.cores + net.core
        return pltpu.make_async_copy(self.src.at[rank], self.mine.at[n % 2], self.sems.at[n % 2])

    def start(self):
        net = self.net
        for n in range(min(2, net.hops)):
            self.fetch(n).start()
        for i in self.order:
            hop = net.at_hop(i)
            net.send(
                self.src.at[hop * net.cores + 1 - net.core], self.landing_core.at[hop],
                self.core_slot + hop, net.core_peer(),
            )

    def relay(self):
        net = self.net
        for n, i in enumerate(self.order):
            hop = net.at_hop(i)
            self.fetch(n).wait()
            net.arrive(self.landing_core.at[hop], self.core_slot + hop)
            if i > 0:
                total = self.mine[n % 2].astype(F32) + self.landing_core[hop].astype(F32)
                self.landing_core[hop] = total.astype(BF16)
                net.send(
                    self.landing_core.at[hop], self.landing_hop.at[net.hop],
                    self.hop_slot + net.hop, net.hop_peer(i),
                )
            if n + 2 < net.hops:
                self.fetch(n + 2).start()

    def total(self):
        net = self.net
        own = self.mine[(net.hops - 1) % 2].astype(F32)
        total = own + self.landing_core[net.hop].astype(F32)
        for i in range(1, net.hops):
            hop = net.at_hop(i)
            net.arrive(self.landing_hop.at[hop], self.hop_slot + hop)
            total = total + self.landing_hop[hop].astype(F32)
        return total


def call(kernel, sizes, number, name, out_shapes, out_specs, in_specs, scratch, sends, slots):
    def body(*refs):
        net = Net(sizes, refs[-2], refs[-1])
        kernel(net, *refs[:-2])
        net.drain()
        assert net.sent <= sends and net.slots <= slots, (net.sent, net.slots)

    return pl.pallas_call(
        body,
        name=name,
        out_shape=out_shapes,
        in_specs=in_specs,
        out_specs=out_specs,
        scratch_shapes=list(scratch)
        + [pltpu.SemaphoreType.DMA((sends,)), pltpu.SemaphoreType.DMA((slots,))],
        compiler_params=pltpu.CompilerParams(collective_id=number, has_side_effects=True),
    )


def local(copies):
    for copy in copies:
        copy.start()


def wait_local(copies):
    for copy in copies:
        copy.wait()


def gather_weights(sizes, att, gate_up):
    dp, gx, gy = sizes
    hops = dp // 2

    def kernel(net, att_ref, gu_ref, att_out, gu_out, sems):
        net.greet(net.plane_peers() + net.share_peers())
        att_plane = PlaneGather(net, att_ref, lambda a, b: att_out.at[a, b, net.d])
        gu_plane = PlaneGather(net, gu_ref, lambda a, b: gu_out.at[a, :, b])
        first_hop = net.block(gx * gy * net.hops)
        first_core = net.block(gx * gy * net.dp)

        def shared(a, b):
            item = Share.__new__(Share)
            item.net = net
            item.out = lambda rank: att_out.at[a, b, rank]
            place = a * gy + b
            item.hop_slot = first_hop + place * net.hops
            item.core_slot = first_core + place * net.dp
            return item

        own = [
            pltpu.make_async_copy(att_ref, att_out.at[net.x, net.y, net.d], sems.at[0]),
            pltpu.make_async_copy(gu_ref, gu_out.at[net.x, :, net.y], sems.at[1]),
        ]
        att_plane.start()
        shared(net.x, net.y).start(att_ref)
        gu_plane.start_gy()
        local(own)
        for k in range(gy - 1, 0, -1):
            att_plane.relay(k)
            row = net.at_gy(k)
            shared(net.x, row).start(att_out.at[net.x, row, net.d])
        gu_plane.start_gx()
        for j in range(1, gx):
            for k in range(gy):
                att_plane.settle(j, k)
                side, row = net.at_gx(j), net.at_gy(k)
                shared(side, row).start(att_out.at[side, row, net.d])
        places = [(j, k) for j in range(gx) for k in range(gy)]
        for n, (j, k) in enumerate(places):
            shared(net.at_gx(j), net.at_gy(k)).relay()
            if n % 2 == 1 and n // 2 + 1 < gy:
                gu_plane.relay(gy - 1 - n // 2)
        for j, k in places:
            shared(net.at_gx(j), net.at_gy(k)).settle()
        for j in range(1, gx):
            for k in range(gy):
                gu_plane.settle(j, k)
        wait_local(own)

    shapes = (
        jax.ShapeDtypeStruct((gx, gy, dp) + att.shape, BF16),
        jax.ShapeDtypeStruct((gx, 2, gy) + gate_up.shape[1:], BF16),
    )
    count = gx * gy * (hops + dp) + 2 * (gx * gy + gy)
    return call(
        kernel, sizes, 1, "gather_weights", shapes, [ANY] * 2, [VMEM] * 2,
        [pltpu.SemaphoreType.DMA((2,))], count, count,
    )(att, gate_up)


def turned(values):
    return jnp.transpose(values)


def head_rows(ref, first, lead=()):
    return jnp.concatenate(
        [ref[:, h * HEAD_WIDTH : (h + 1) * HEAD_WIDTH] for h in range(first, first + GROUPS)], axis=0
    )


def key_columns(ref, place):
    columns = ref[:, :, :, place * HEAD_WIDTH : (place + 1) * HEAD_WIDTH]
    return columns.reshape(-1, HEAD_WIDTH)


def put_heads(ref, first, rows, values):
    for n in range(GROUPS):
        lanes = slice((first + n) * HEAD_WIDTH, (first + n + 1) * HEAD_WIDTH)
        ref[:, lanes] = values[n * rows : (n + 1) * rows].astype(ref.dtype)


def attend_heads(key_heads, q_ref, kv_ref, bias_ref, mixed_ref, logsum_ref):
    rows = q_ref.shape[0]
    bias = jnp.concatenate([bias_ref[...]] * GROUPS, axis=1)
    for k in key_heads:
        query = head_rows(q_ref, k * GROUPS)
        scores = back_product(key_columns(kv_ref, k), query) * HEAD_WIDTH ** (-0.5) + bias
        highest = jnp.max(scores, axis=0, keepdims=True)
        weights = jnp.exp(scores - highest)
        sums = jnp.sum(weights, axis=0, keepdims=True)
        logsum_ref[k : k + 1, :] = highest + jnp.log(sums)
        probs = (weights * (1.0 / sums)).astype(BF16)
        mixed = weight_product(key_columns(kv_ref, KEY_VALUE_HEADS + k), probs)
        put_heads(mixed_ref, k * GROUPS, rows, turned(mixed))


def attend_heads_back(q_ref, kv_ref, bias_ref, logsum_ref, mixed_ref, dmixed_ref, dq_ref, dkv_ref):
    rows = q_ref.shape[0]
    bias = jnp.concatenate([bias_ref[...]] * GROUPS, axis=1)
    blocks = kv_ref.shape[:3]
    for k in range(KEY_VALUE_HEADS):
        query = head_rows(q_ref, k * GROUPS)
        mixed = head_rows(mixed_ref, k * GROUPS)
        dmixed = head_rows(dmixed_ref, k * GROUPS)
        keys = key_columns(kv_ref, k)
        scores = back_product(keys, query) * HEAD_WIDTH ** (-0.5) + bias
        weights = jnp.exp(scores - logsum_ref[k : k + 1, :])
        delta = jnp.sum(turned(mixed.astype(F32) * dmixed.astype(F32)), axis=0, keepdims=True)
        dprobs = back_product(key_columns(kv_ref, KEY_VALUE_HEADS + k), dmixed)
        dscores = (weights * (dprobs - delta)).astype(BF16)
        dquery = weight_product(keys, dscores) * HEAD_WIDTH ** (-0.5)
        put_heads(dq_ref, k * GROUPS, rows, turned(dquery))
        dkeys = plain_product(dscores, query) * HEAD_WIDTH ** (-0.5)
        dvalues = plain_product(weights.astype(BF16), dmixed)
        lanes = slice(k * HEAD_WIDTH, (k + 1) * HEAD_WIDTH)
        dkv_ref[:, :, :, lanes] = dkeys.astype(BF16).reshape(blocks + (HEAD_WIDTH,))
        place = KEY_VALUE_HEADS + k
        lanes = slice(place * HEAD_WIDTH, (place + 1) * HEAD_WIDTH)
        dkv_ref[:, :, :, lanes] = dvalues.astype(BF16).reshape(blocks + (HEAD_WIDTH,))


def turn_pairs(values, cos, sin):
    lanes = cos.shape[1]
    half = HEAD_WIDTH // 2
    front = lax.broadcasted_iota(jnp.int32, cos.shape, 1) % HEAD_WIDTH < half
    pieces = []
    for first in range(0, values.shape[1], lanes):
        part = values[:, first : first + lanes]
        other = jnp.where(front, pltpu.roll(part, lanes - half, 1), pltpu.roll(part, half, 1))
        pieces.append(part * cos + other * sin)
    return jnp.concatenate(pieces, axis=1)


def forward(sizes, cols, att, normed, inputs, gain, cos, sin, bias, down, cot):
    dp, gx, gy = sizes
    q_cols, k_cols, v_cols, o_cols = cols
    qkv_cols = q_cols + k_cols + v_cols
    rows, width = inputs.shape
    fan = att.shape[3]
    lanes = cos.shape[1]
    q_width, k_width, v_width = gy * q_cols, gy * k_cols, gy * v_cols
    q_pad, k_pad = -(-q_width // lanes) * lanes, -(-k_width // lanes) * lanes

    def kernel(
        net, att_ref, nm_ref, in_ref, gain_ref, cos_ref, sin_ref, bias_ref, dn_ref, cot_ref,
        q_ref, kv_out, mixed_ref, logsum_ref, hidden_ref,
        dn_out, cot_out, nm_out, mixed_out, two_out,
        q_wide, k_wide, kv_ref, two_ref, sems,
    ):
        q_wide[...] = jnp.zeros_like(q_wide)
        k_wide[...] = jnp.zeros_like(k_wide)
        for b in range(gy):
            block = sum(
                back_product(nm_ref[:, a * fan : (a + 1) * fan], att_ref[a, b, :qkv_cols, :])
                for a in range(gx)
            ).astype(BF16)
            q_wide[:, b * q_cols : (b + 1) * q_cols] = block[:, :q_cols].astype(F32)
            k_wide[:, b * k_cols : (b + 1) * k_cols] = block[:, q_cols : q_cols + k_cols].astype(F32)
            first = k_width + b * v_cols
            kv_ref[:, first : first + v_cols] = block[:, q_cols + k_cols :]
        cos_rows, sin_rows = cos_ref[...], sin_ref[...]
        kv_ref[:, :k_width] = turn_pairs(k_wide[...], cos_rows, sin_rows)[:, :k_width].astype(BF16)

        net.greet(net.plane_peers() + net.share_peers())
        kv = PlaneGather(net, kv_ref, lambda a, b: kv_out.at[a, b])
        dn = PlaneGather(net, dn_ref, lambda a, b: dn_out.at[a, b])
        cot_share, nm_share, mixed_share, two_share = (
            Share(net, lambda r, out=out: out.at[r]) for out in (cot_out, nm_out, mixed_out, two_out)
        )
        own = [
            pltpu.make_async_copy(kv_ref, kv_out.at[net.x, net.y], sems.at[0]),
            pltpu.make_async_copy(dn_ref, dn_out.at[net.x, net.y], sems.at[2]),
            pltpu.make_async_copy(cot_ref, cot_out.at[net.d], sems.at[3]),
            pltpu.make_async_copy(nm_ref, nm_out.at[net.d], sems.at[4]),
        ]
        kv.start()
        dn.start_gy()
        local(own)
        cot_share.start(cot_ref)
        nm_share.start(nm_ref)
        q_ref[...] = turn_pairs(q_wide[...], cos_rows, sin_rows)[:, :q_width].astype(BF16)
        for k in range(gy - 1, 0, -1):
            kv.relay(k)
        dn.start_gx()
        for j in range(1, gx):
            for k in range(gy):
                kv.settle(j, k)
        wait_local(own)

        turns = list(range(gy - 1, 0, -1))
        heads = list(range(KEY_VALUE_HEADS))
        for n, k in enumerate(turns):
            mine = heads[n * len(heads) // len(turns) : (n + 1) * len(heads) // len(turns)]
            attend_heads(mine, q_ref, kv_out, bias_ref, mixed_ref, logsum_ref)
            if n + 1 < len(turns):
                dn.relay(k)
        last = pltpu.make_async_copy(mixed_ref, mixed_out.at[net.d], sems.at[5])
        last.start()
        mixed_share.start(mixed_ref)
        for b in range(gy):
            block = sum(
                back_product(mixed_ref[:, a * fan : (a + 1) * fan], att_ref[a, b, qkv_cols:, :])
                for a in range(gx)
            ).astype(BF16)
            span = slice(b * o_cols, (b + 1) * o_cols)
            hidden_ref[:, span] = in_ref[:, span].astype(F32) + block.astype(F32)
        hidden = hidden_ref[...]
        scale = lax.rsqrt(jnp.sum(hidden * hidden, axis=1, keepdims=True) / width + EPSILON)
        two_ref[...] = (hidden * scale * gain_ref[...]).astype(BF16)
        local_two = pltpu.make_async_copy(two_ref, two_out.at[net.d], sems.at[6])
        local_two.start()
        two_share.start(two_ref)
        dn.relay(turns[-1])
        shares = (cot_share, nm_share, mixed_share, two_share)
        for share in shares:
            share.relay()
        for share in shares:
            share.settle()
        for j in range(1, gx):
            for k in range(gy):
                dn.settle(j, k)
        wait_local([last, local_two])

    shared = jax.ShapeDtypeStruct((dp,) + inputs.shape, BF16)
    shapes = (
        jax.ShapeDtypeStruct((rows, q_width), BF16),
        jax.ShapeDtypeStruct((gx, gy, rows, k_width + v_width), BF16),
        jax.ShapeDtypeStruct((rows, q_width), BF16),
        jax.ShapeDtypeStruct((KEY_VALUE_HEADS, GROUPS * rows), F32),
        jax.ShapeDtypeStruct(inputs.shape, F32),
        jax.ShapeDtypeStruct((gx, gy) + down.shape, BF16),
        shared, shared, shared, shared,
    )
    scratch = [
        pltpu.VMEM((rows, q_pad), F32),
        pltpu.VMEM((rows, k_pad), F32),
        pltpu.VMEM((rows, k_width + v_width), BF16),
        pltpu.VMEM(inputs.shape, BF16),
        pltpu.SemaphoreType.DMA((7,)),
    ]
    count = 3 * (gx * gy + gy) + 4 * 2 * dp
    return call(
        kernel, sizes, 2, "forward", shapes, [VMEM] * 5 + [ANY] * 5, [VMEM] * 9, scratch, count, count,
    )(att, normed, inputs, gain, cos, sin, bias, down, cot)


def mlp(normed_all, cot_all, gate_up, down):
    gx, both, fan = gate_up.shape
    rows, width = normed_all.shape
    hidden = both // 2
    part = down.shape[2]
    step = rows // 2 if rows % 32 == 0 else rows

    def kernel(n_ref, c_ref, gu_ref, dt_ref, dn_ref, mo_ref, gg_ref, dg_ref, act_ref, delta_ref):
        def tokens(i, carry):
            span = pl.ds(pl.multiple_of(i * step, step), step)
            normed, cot = n_ref[span, :], c_ref[span, :]
            gate_up_rows = sum(
                back_product(normed[:, a * fan : (a + 1) * fan], gu_ref[a]) for a in range(gx)
            ).astype(BF16)
            gate = gate_up_rows[:, :hidden].astype(F32)
            up = gate_up_rows[:, hidden:].astype(F32)
            dact = jnp.concatenate([plain_product(cot, dt_ref[a]) for a in range(gx)], axis=1)
            sigmoid = jax.nn.sigmoid(gate)
            act = (gate * sigmoid * up).astype(BF16)
            gate_delta = (dact * up * sigmoid * (1.0 + gate * (1.0 - sigmoid))).astype(BF16)
            up_delta = (dact * gate * sigmoid).astype(BF16)
            deltas = jnp.concatenate([gate_delta, up_delta], axis=1)
            delta_ref[span, :] = deltas
            for a in range(gx):
                act_ref[a, span, :] = act[:, a * part : (a + 1) * part]
                dn_ref[span, a * fan : (a + 1) * fan] = plain_product(deltas, gu_ref[a]).astype(BF16)
            mo_ref[span, :] = sum(
                back_product(act[:, a * part : (a + 1) * part], dt_ref[a]) for a in range(gx)
            ).astype(BF16)
            return carry

        lax.fori_loop(0, rows // step, tokens, 0)
        for a in range(gx):
            gg_ref[a] = weight_product(delta_ref[...], n_ref[:, a * fan : (a + 1) * fan]).astype(BF16)
            dg_ref[a] = weight_product(c_ref[...], act_ref[a]).astype(BF16)

    return pl.pallas_call(
        kernel,
        name="mlp",
        out_shape=(
            jax.ShapeDtypeStruct(normed_all.shape, BF16),
            jax.ShapeDtypeStruct(normed_all.shape, BF16),
            jax.ShapeDtypeStruct(gate_up.shape, BF16),
            jax.ShapeDtypeStruct(down.shape, BF16),
        ),
        in_specs=[VMEM] * 4,
        out_specs=[VMEM] * 4,
        scratch_shapes=[pltpu.VMEM((gx, rows, part), BF16), pltpu.VMEM((rows, both), BF16)],
    )(normed_all, cot_all, gate_up, down)


def backward(
    sizes, cols, query, kv_all, bias, logsum, mixed, dnormed_part, mlp_part, hidden, cot, att, normed_all,
    mixed_all, inputs, gain, mlp_gain, cos, sin, gate_up, down,
):
    dp, gx, gy = sizes
    q_cols, k_cols, v_cols, o_cols = cols
    qkv_cols = q_cols + k_cols + v_cols
    all_cols = qkv_cols + o_cols
    att_share = all_cols // dp
    rows, width = inputs.shape
    fan = att.shape[3]
    lanes = cos.shape[1]
    q_width, k_width = gy * q_cols, gy * k_cols
    q_pad, k_pad = -(-q_width // lanes) * lanes, -(-k_width // lanes) * lanes
    kv_width = kv_all.shape[3]
    pieces = [
        (gate_up.shape[3:], BF16), (gate_up.shape[3:], BF16), (down.shape[2:], BF16),
        ((att_share, fan), BF16), ((8, width), F32), ((rows, kv_width), BF16),
    ]
    count = len(pieces)

    def kernel(net, *refs):
        (
            q_ref, kv_ref, bias_ref, logsum_ref, mixed_ref, two_ref, mo_ref, hidden_ref, cot_ref, att_ref,
            nm_ref, mx_ref, in_ref, gain_ref, two_gain_ref, cos_ref, sin_ref, gu_ref, dn_ref,
        ) = refs[:19]
        layer_out, input_grad, gu_out, dn_out, att_out, gain_out = refs[19:25]
        q_wide, k_wide, dkv_ref, p_ref, trade_src, trade_in, dn_one, att_grad, gains = refs[25:34]
        dmixed_ref, dhidden_ref = refs[34:36]
        two_scratch, mo_scratch = refs[36:40], refs[40:44]
        refs = refs[44:]
        landing_x, stage, landing_y = (refs[n * count : (n + 1) * count] for n in range(3))
        result, sems = refs[3 * count : 4 * count - 1], refs[4 * count - 1]

        net.greet(net.plane_peers() + [net.dp_peer(i) for i in range(1, dp)])
        sources = [
            lambda a, b: gu_ref.at[a, 0, b], lambda a, b: gu_ref.at[a, 1, b], lambda a, b: dn_ref.at[a, b],
            lambda a, b: att_grad.at[a, b], lambda a, b: gains, lambda a, b: dkv_ref.at[a, b],
        ]
        sums = [
            PlaneSum(net, sources[n], landing_x[n], stage[n], landing_y[n]) for n in range(count)
        ]
        outs = [
            lambda r: gu_out.at[r, 0], lambda r: gu_out.at[r, 1], lambda r: dn_out.at[r],
            lambda r: att_out.at[r], lambda r: gain_out.at[r],
        ]
        shares = [Share(net, out) for out in outs]
        mlp_sums, att_sums, dkv_sum = sums[:3], sums[3:5], sums[5]
        order = far_first(gy) + [0]

        def begin(items, turns):
            for k in turns:
                for item in items:
                    item.start(k)

        def relay(items, turns):
            for k in turns:
                for item in items:
                    item.relay(k)

        own = []

        def finish(first, items):
            for n, item in enumerate(items, first):
                result[n][...] = item.total().astype(result[n].dtype)
                shares[n].start(result[n])
                own.append(pltpu.make_async_copy(result[n], shares[n].out(net.d), sems.at[n]))
                own[-1].start()

        two_sum, mo_sum = TokenSum(net, two_ref, *two_scratch), TokenSum(net, mo_ref, *mo_scratch)
        two_sum.start()
        begin(mlp_sums, order[:2])
        two_sum.relay()
        mo_sum.start()
        hidden = hidden_ref[...]
        rms_two = lax.rsqrt(jnp.sum(hidden * hidden, axis=1, keepdims=True) / width + EPSILON)
        unit_two = hidden * rms_two
        dnormed_two = two_sum.total()
        scaled_two = dnormed_two * two_gain_ref[...]
        level_two = jnp.sum(scaled_two * unit_two, axis=1, keepdims=True) / width
        dhidden_ref[...] = cot_ref[...].astype(F32) + rms_two * (scaled_two - unit_two * level_two)
        gains[...] = jnp.zeros_like(gains)
        gains[1:2, :] = jnp.sum(dnormed_two * unit_two, axis=0, keepdims=True)
        mo_sum.relay()
        dhidden_bf = dhidden_ref[...].astype(BF16)
        for a in range(gx):
            dmixed_ref[:, a * fan : (a + 1) * fan] = sum(
                plain_product(dhidden_bf[:, b * o_cols : (b + 1) * o_cols], att_ref[a, b, qkv_cols:, :])
                for b in range(gy)
            ).astype(BF16)
        relay(mlp_sums, order[:1])
        q_wide[...] = jnp.zeros_like(q_wide)
        k_wide[...] = jnp.zeros_like(k_wide)
        attend_heads_back(
            q_ref, kv_ref, bias_ref, logsum_ref, mixed_ref, dmixed_ref, q_wide, dkv_ref
        )
        begin([dkv_sum], order)
        begin(mlp_sums, order[2:3])
        relay(mlp_sums, order[1:2])
        layer_out[...] = (hidden_ref[...] + mo_sum.total()).astype(BF16)
        relay([dkv_sum], order)
        begin(mlp_sums, order[3:])
        cos_rows, sin_rows = cos_ref[...], -sin_ref[...]
        dquery = turn_pairs(q_wide[...], cos_rows, sin_rows)[:, :q_width].astype(BF16)
        dhidden = dhidden_ref[...]
        for b in range(gy):
            p_ref[b, :, :q_cols] = dquery[:, b * q_cols : (b + 1) * q_cols]
            p_ref[b, :, qkv_cols:] = dhidden_bf[:, b * o_cols : (b + 1) * o_cols]
        dkv = dkv_sum.total()
        k_wide[:, :k_width] = dkv[:, :k_width]
        dkey = turn_pairs(k_wide[...], cos_rows, sin_rows)[:, :k_width].astype(BF16)
        dvalue = dkv[:, k_width:].astype(BF16)
        for b in range(gy):
            p_ref[b, :, q_cols : q_cols + k_cols] = dkey[:, b * k_cols : (b + 1) * k_cols]
            p_ref[b, :, q_cols + k_cols : qkv_cols] = dvalue[:, b * v_cols : (b + 1) * v_cols]
        for r in range(dp):
            for b in range(gy):
                trade_src[r, :, b * att_share : (b + 1) * att_share] = p_ref[
                    b, :, r * att_share : (r + 1) * att_share
                ]
        trade_slot = net.block(dp)
        for i in range(1, dp):
            rank = lax.rem(net.d + i, dp)
            net.send(trade_src.at[rank], trade_in.at[net.d], trade_slot + net.d, net.dp_peer(i))
        trade_in[net.d] = trade_src[net.d]
        relay(mlp_sums, order[2:3])

        for a in range(gx):
            dn_one[:, a * fan : (a + 1) * fan] = sum(
                plain_product(p_ref[b, :, :qkv_cols], att_ref[a, b, :qkv_cols, :]) for b in range(gy)
            )
        dnormed = dn_one[...]
        values = in_ref[...].astype(F32)
        rms = lax.rsqrt(jnp.sum(values * values, axis=1, keepdims=True) / width + EPSILON)
        unit = values * rms
        scaled = dnormed * gain_ref[...]
        level = jnp.sum(scaled * unit, axis=1, keepdims=True) / width
        input_grad[...] = (dhidden + rms * (scaled - unit * level)).astype(BF16)
        gains[0:1, :] = jnp.sum(dnormed * unit, axis=0, keepdims=True)

        for i in range(1, dp):
            rank = lax.rem(net.d + i, dp)
            net.arrive(trade_in.at[rank], trade_slot + rank)
        dall = trade_in[...].reshape(dp * rows, gy * att_share)
        places = lax.broadcasted_iota(jnp.int32, (gy * att_share, fan), 0) % att_share
        from_normed = places + net.d * att_share < qkv_cols
        for a in range(gx):
            span = slice(a * fan, (a + 1) * fan)
            grad = jnp.where(
                from_normed,
                weight_product(dall, nm_ref[:, span]),
                weight_product(dall, mx_ref[:, span]),
            ).astype(BF16)
            for b in range(gy):
                att_grad[a, b] = grad[b * att_share : (b + 1) * att_share]
        begin(att_sums, order)
        relay(mlp_sums, order[3:])
        finish(0, mlp_sums)
        relay(att_sums, order)
        finish(3, att_sums)
        for share in shares:
            share.relay()
        for share in shares:
            share.settle()
        wait_local(own)

    shapes = (
        jax.ShapeDtypeStruct(inputs.shape, BF16),
        jax.ShapeDtypeStruct(inputs.shape, BF16),
        jax.ShapeDtypeStruct((dp, 2) + pieces[0][0], BF16),
        jax.ShapeDtypeStruct((dp,) + pieces[2][0], BF16),
        jax.ShapeDtypeStruct((dp,) + pieces[3][0], BF16),
        jax.ShapeDtypeStruct((dp,) + pieces[4][0], F32),
    )
    scratch = [
        pltpu.VMEM((rows, q_pad), F32),
        pltpu.VMEM((rows, k_pad), F32),
        pltpu.VMEM(kv_all.shape, BF16),
        pltpu.VMEM((gy, rows, all_cols), BF16),
        pltpu.VMEM((dp, rows, gy * att_share), BF16),
        pltpu.VMEM((dp, rows, gy * att_share), BF16),
        pltpu.VMEM((rows, width), F32),
        pltpu.VMEM((gx, gy, att_share, fan), BF16),
        pltpu.VMEM((8, width), F32),
        pltpu.VMEM((rows, width), BF16),
        pltpu.VMEM((rows, width), F32),
    ]
    slab = pltpu.VMEM((dp // 2, rows, width), BF16)
    scratch += [pltpu.VMEM((2, rows, width), BF16), slab, slab, pltpu.SemaphoreType.DMA((2,))] * 2
    scratch += [pltpu.VMEM((gx, gy) + p, t) for p, t in pieces]
    scratch += [pltpu.VMEM((gy,) + p, t) for p, t in pieces] * 2
    scratch += [pltpu.VMEM(p, t) for p, t in pieces[:-1]]
    scratch += [pltpu.SemaphoreType.DMA((count - 1,))]
    sems = count * (gx * gy + gy) + (count - 1) * 2 * dp + 3 * dp
    return call(
        kernel, sizes, 5, "backward", shapes, [VMEM] * 2 + [ANY] * 4, [VMEM] * 5 + [ANY] * 2 + [VMEM] * 12, scratch, sems, sems,
    )(
        query, kv_all, bias, logsum, mixed, dnormed_part, mlp_part, hidden, cot, att, normed_all,
        mixed_all, inputs, gain, mlp_gain, cos, sin, gate_up, down,
    )


def rope_angles(positions):
    half_dim = HEAD_WIDTH // 2
    inverse = THETA ** (-(jnp.arange(half_dim, dtype=F32) * 2.0 / HEAD_WIDTH))
    angles = positions[:, None] * inverse[None, :]
    return (jnp.cos(angles)[:, None, :], jnp.sin(angles)[:, None, :])


def normalize(values, gain):
    rms_rows = lax.rsqrt(jnp.mean(values * values, axis=1, keepdims=True) + EPSILON)
    unit_rows = values * rms_rows
    return (rms_rows, unit_rows, (unit_rows * gain).astype(BF16))


def on_device(
    sizes,
    inputs,
    segments,
    attn_gain,
    query_weight,
    key_weight,
    value_weight,
    output_weight,
    mlp_gain,
    gate_weight,
    up_weight,
    down_weight,
    cotangent,
):
    dp, gx, gy = sizes
    count_of_rows, width = inputs.shape
    rank = lax.axis_index("dp")
    begin_row = (lax.axis_index("gx") * gy + lax.axis_index("gy")) * count_of_rows
    seq_begin = begin_row // SEQUENCE_LENGTH * SEQUENCE_LENGTH
    local_places = begin_row - seq_begin + jnp.arange(count_of_rows)
    cos_table, sin_table = rope_angles(local_places.astype(F32))
    query_segs = lax.dynamic_slice_in_dim(segments, begin_row, count_of_rows, 0)
    allowed = (jnp.arange(SEQUENCE_LENGTH)[:, None] <= local_places[None, :]) & (
        query_segs[None, :] == segments[:, None]
    )
    bias = jnp.where(allowed, 0.0, MASKED).astype(F32)
    residual = inputs.astype(F32)
    _, _, normed_one = normalize(residual, attn_gain)

    fan = query_weight.shape[0]
    q_cols, k_cols, v_cols = query_weight.shape[1], key_weight.shape[1], value_weight.shape[1]
    o_cols = output_weight.shape[1]
    qkv_cols = q_cols + k_cols + v_cols
    all_cols = qkv_cols + o_cols
    att_share = all_cols // dp
    packed = jnp.concatenate([query_weight, key_weight, value_weight, output_weight], axis=1).T
    att_part = lax.dynamic_slice_in_dim(packed, rank * att_share, att_share, 0)
    share = gate_weight.shape[1] // dp
    groups = gy // gx
    gate_up_part = jnp.stack(
        [
            lax.dynamic_slice_in_dim(gate_weight, rank * share, share, 1).T,
            lax.dynamic_slice_in_dim(up_weight, rank * share, share, 1).T,
        ]
    )
    down_cols = down_weight.shape[1]
    down_part = lax.dynamic_slice_in_dim(
        down_weight.reshape(groups, dp, share, down_cols), rank, 1, 1
    ).reshape(groups * share, down_cols).T

    att_all, gate_up_all = gather_weights(sizes, att_part, gate_up_part)
    att_all = att_all.reshape(gx, gy, all_cols, fan)
    cos_wide = jnp.tile(cos_table[:, 0], (1, 4))
    sin_wide = jnp.tile(jnp.concatenate([-sin_table[:, 0], sin_table[:, 0]], axis=1), (1, 2))
    (
        rotated_query, kv_all, attention_mixture, logsum, hidden,
        down_all, cot_all, normed_one_all, mixed_all, normed_all,
    ) = forward(
        sizes, (q_cols, k_cols, v_cols, o_cols), att_all, normed_one, inputs, mlp_gain.reshape(1, -1),
        cos_wide, sin_wide, bias, down_part, cotangent,
    )
    hidden_width = gy * share
    gate_up_all = gate_up_all.reshape(gx, 2 * hidden_width, fan)
    half_hidden = groups * share
    down_all = down_all.reshape(gx, gy * down_cols, half_hidden)
    cot_all, normed_one_all, mixed_all, normed_all = (
        rows.reshape(dp * count_of_rows, width) for rows in (cot_all, normed_one_all, mixed_all, normed_all)
    )
    dnormed_part, mlp_part, gate_up_grad, down_grad = mlp(normed_all, cot_all, gate_up_all, down_all)
    gate_up_grad = gate_up_grad.reshape(gx, 2, gy, share, fan)
    down_grad = down_grad.reshape(gx, gy, down_cols, half_hidden)

    layer_out, input_grad, gate_up_sum, down_sum, att_sum, gain_sum = backward(
        sizes, (q_cols, k_cols, v_cols, o_cols), rotated_query, kv_all, bias, logsum, attention_mixture,
        dnormed_part.reshape(dp, count_of_rows, width), mlp_part.reshape(dp, count_of_rows, width),
        hidden, cotangent, att_all, normed_one_all, mixed_all, inputs, attn_gain.reshape(1, -1),
        mlp_gain.reshape(1, -1), cos_wide, sin_wide, gate_up_grad, down_grad,
    )
    gate_grad = gate_up_sum[:, 0].reshape(dp * share, fan).T.astype(F32)
    up_grad = gate_up_sum[:, 1].reshape(dp * share, fan).T.astype(F32)
    down_grad = (
        down_sum.reshape(dp, down_cols, groups, share)
        .transpose(2, 0, 3, 1)
        .reshape(down_weight.shape)
        .astype(F32)
    )
    att_sum = att_sum.reshape(all_cols, fan).T.astype(F32)
    gains = jnp.sum(gain_sum, axis=0)
    return (
        layer_out,
        input_grad,
        att_sum[:, :q_cols],
        att_sum[:, q_cols : q_cols + k_cols],
        att_sum[:, q_cols + k_cols : qkv_cols],
        att_sum[:, qkv_cols:],
        gate_grad,
        up_grad,
        down_grad,
        gains[0],
        gains[1],
    )


def solution(mesh):
    sizes = (mesh.shape["dp"], mesh.shape["gx"], mesh.shape["gy"])
    tokens = P(("dp", "gx", "gy"), None)
    block = P("gx", "gy")
    return jax.shard_map(
        functools.partial(on_device, sizes),
        mesh=mesh,
        in_specs=(tokens, P("dp"), P(), block, block, block, block, P(), block, block, block, tokens),
        out_specs=(tokens, tokens) + (block,) * 7 + (P(), P()),
        check_vma=False,
    )
```
